32 devices in a mesh: batch: 4 (over z), seq: 8 (over y, x, core).
Axes of the slice: x: 2, y: 2, z: 4, core: 2. Of those that a mesh axis runs over, the one named last changes fastest.
Arguments:
- tokens: bfloat16 [16, 2048, 768], P('batch', 'seq'), may hold values from -6 to 6
- segment_ids: int32 [16, 2048], P('batch', 'seq'), may hold values from -1 to 5, as said below
- attn_gain: bfloat16 [768], replicated, may hold values from 0.5 to 1.5
- attn_shift: bfloat16 [768], replicated, may hold values from -1.75 to 1.75
- mlp_gain: bfloat16 [768], replicated, may hold values from 0.5 to 1.5
- mlp_shift: bfloat16 [768], replicated, may hold values from -1.75 to 1.75
- w_query: bfloat16 [768, 768], replicated, may hold values from -0.21875 to 0.21875
- b_query: bfloat16 [768], replicated, may hold values from -1.75 to 1.75
- w_keyvalue: bfloat16 [768, 128], replicated, may hold values from -0.21875 to 0.21875
- w_out: bfloat16 [768, 768], replicated, may hold values from -1.75 to 1.75
- b_out: bfloat16 [768], replicated, may hold values from -1.75 to 1.75
- w_up: bfloat16 [768, 3072], replicated, may hold values from -0.21875 to 0.21875
- b_up: bfloat16 [3072], replicated, may hold values from -1.75 to 1.75
- w_down: bfloat16 [3072, 768], replicated, may hold values from -0.109375 to 0.109375
- b_down: bfloat16 [768], replicated, may hold values from -1.75 to 1.75
- out_grad: bfloat16 [16, 2048, 768], P('batch', 'seq'), may hold values from -6 to 6
Outputs:
- output: bfloat16 [16, 2048, 768], P('batch', 'seq')
- keyvalue: bfloat16 [16, 2048, 128], P('batch', 'seq')
- tokens_grad: bfloat16 [16, 2048, 768], P('batch', 'seq')
- attn_gain_grad: float32 [768], P(('batch', 'seq'))
- attn_shift_grad: float32 [768], P(('batch', 'seq'))
- mlp_gain_grad: float32 [768], P(('batch', 'seq'))
- mlp_shift_grad: float32 [768], P(('batch', 'seq'))
- w_query_grad: float32 [768, 768], P(('batch', 'seq'))
- b_query_grad: float32 [768], P(('batch', 'seq'))
- w_keyvalue_grad: float32 [768, 128], P(('batch', 'seq'))
- w_out_grad: float32 [768, 768], P(None, ('batch', 'seq'))
- b_out_grad: float32 [768], P(('batch', 'seq'))
- w_up_grad: float32 [768, 3072], P(('batch', 'seq'))
- b_up_grad: float32 [3072], P(('batch', 'seq'))
- w_down_grad: float32 [3072, 768], P(None, ('batch', 'seq'))
- b_down_grad: float32 [768], P(('batch', 'seq'))
The draws below stay inside these ranges and needn't reach their ends.
Inputs may be any that keep to these rules, and one draw needn't show every extreme that they name: `segment_ids`: each row holds 6 documents with ids 0 to 5 in order, each a nonempty run of positions, followed by one or more padding positions with id -1 at the row's end.
All inputs are finite; a program needn't handle non-finite values.
Results may differ from the reference program's by a relative error of at most 0.011.
Values may be sent and summed in bfloat16 or wider, within the bound.
No kernel may reach another device: no remote copies, remote signals or barrier semaphores. Data moves between devices by JAX's collectives and lax.ppermute only.
A program may use at most 256 MiB of HBM per device.

```python
import math
import jax
import jax.numpy as jnp
from jax import lax

D = 768
HEADS = 12
HEAD_DIM = 64
FF = 3072
ROT_DIMS = 16
SEQ_LEN = 2048
DOCS = 6
ALL_ROWS = 16


def draw_segment_ids(key, part):
    cut_range = SEQ_LEN - SEQ_LEN // 8

    def one_row(row_key):
        cut_key, pad_key = jax.random.split(row_key)
        cut_points = jax.random.permutation(cut_key, cut_range - 1)[:DOCS - 1] + 1
        padding = jax.random.randint(pad_key, (), 1, SEQ_LEN // 8 + 1)
        position_ids = jnp.arange(SEQ_LEN)
        counted = jnp.sum((position_ids[:, None] >= cut_points[None, :]).astype(jnp.int32), axis=1)
        return jnp.where(position_ids < SEQ_LEN - padding, counted, -1).astype(jnp.int32)
    return jax.vmap(one_row)(jax.random.split(key, ALL_ROWS))


def with_spikes(result, key, source, target, blocks, factor):
    def block_of(dim):
        return (jnp.arange(result.shape[dim]) // (result.shape[dim] // blocks)).reshape((-1,) + (1,) * (result.ndim - 1 - dim))

    first = jax.random.permutation(key, blocks)[block_of(target)]
    far = (block_of(target) + blocks // 2) % blocks
    return jnp.where((block_of(source) == first) | (block_of(source) == far), factor * result, result)


def levels(key, shape, cuts, low, largest):
    level, own = 1.0, jax.random.fold_in(key, 6)
    for axis_at, shards_of in cuts:
        steps = jnp.exp(jax.random.uniform(jax.random.fold_in(own, axis_at), (shards_of,), jnp.float32, low / len(cuts), largest / len(cuts)))
        level = level * jnp.repeat(steps, shape[axis_at] // shards_of).reshape([-1 if axis == axis_at else 1 for axis in range(len(shape))])
    return level


def noise(rng, shape, width, bound, cuts=(), kind=jnp.bfloat16):
    entries = width * jax.random.normal(rng, shape, jnp.float32)
    if cuts:
        entries = entries * levels(rng, shape, cuts, -0.22, 0.18)
    return jnp.clip(entries, -bound, bound).astype(kind)


def heavy_noise(own_key, shape, scale, reach, pieces, heavy, dtype=jnp.bfloat16):
    entries = scale * jax.random.normal(own_key, shape, jnp.float32)
    if pieces:
        entries = entries * levels(own_key, shape, pieces, -0.22, 0.18)
    return jnp.clip(with_spikes(entries, jax.random.fold_in(own_key, 3), *heavy), -reach, reach).astype(dtype)


def setup_inputs(seed: int = 0) -> dict:
    keys = jax.random.split(jax.random.key(seed), 17)
    return {
        "tokens": noise(keys[0], (ALL_ROWS, SEQ_LEN, D), 1.0, 6.0, ((0, 4), (1, 8))),
        "segment_ids": draw_segment_ids(jax.random.fold_in(keys[16], 71), 0),
        "attn_gain": jnp.clip(1.0 + 0.1 * jax.random.normal(keys[2], (D,), jnp.float32), 0.5, 1.5).astype(jnp.bfloat16),
        "attn_shift": noise(keys[3], (D,), 0.3, 1.75),
        "mlp_gain": jnp.clip(1.0 + 0.1 * jax.random.normal(keys[4], (D,), jnp.float32), 0.5, 1.5).astype(jnp.bfloat16),
        "mlp_shift": noise(keys[5], (D,), 0.3, 1.75),
        "w_query": noise(keys[6], (D, D), D ** -0.5, 0.21875),
        "b_query": noise(keys[7], (D,), 0.3, 1.75),
        "w_keyvalue": noise(keys[8], (D, 2 * HEAD_DIM), D ** -0.5, 0.21875),
        "w_out": noise(keys[9], (D, D), (D // 64) ** -0.5, 1.75),
        "b_out": noise(keys[10], (D,), 0.3, 1.75),
        "w_up": noise(keys[11], (D, FF), D ** -0.5, 0.21875),
        "b_up": noise(keys[12], (FF,), 0.3, 1.75),
        "w_down": noise(keys[13], (FF, D), FF ** -0.5, 0.109375),
        "b_down": noise(keys[14], (D,), 0.3, 1.75),
        "out_grad": heavy_noise(keys[15], (ALL_ROWS, SEQ_LEN, D), 1.0, 6.0, ((0, 4), (1, 8)), (1, 2, 8, 2.0)),
    }


EPSILON = 1e-05
HIGHEST = lax.Precision.HIGHEST

@jax.custom_vjp
def low(v):
    return lax.optimization_barrier(v.astype(jnp.bfloat16)).astype(jnp.float32)

@jax.custom_vjp
def low_back(v):
    return v

def low_keep(v):
    return (low(v), None)

def low_pass(kept, grad):
    return (grad,)

def back_keep(v):
    return (v, None)

def back_low(kept, grad):
    return (low(grad),)
low.defvjp(low_keep, low_pass)
low_back.defvjp(back_keep, back_low)

def matmul(left, right):
    return jnp.dot(left, right, precision=HIGHEST)

def layer_norm(values, gain, shift):
    center = values - lax.optimization_barrier(jnp.mean(values, axis=-1, keepdims=True))
    spread = lax.optimization_barrier(jnp.mean(center * center, axis=-1, keepdims=True))
    return center * lax.rsqrt(spread + EPSILON) * gain + shift

def rotate(values, cosine, sine_table):
    halfway = ROT_DIMS // 2
    leading = values[..., :halfway]
    trailing = values[..., halfway:ROT_DIMS]
    return jnp.concatenate([leading * cosine - trailing * sine_table, trailing * cosine + leading * sine_table, values[..., ROT_DIMS:]], axis=-1)

def attention(queries, keyvalue, allowed):
    keys_all = keyvalue[:, :HEAD_DIM]
    values_all = keyvalue[:, HEAD_DIM:]

    def one_head(query_head):
        scores = low_back(matmul(query_head, keys_all.T))
        scores = jnp.where(allowed, scores, -1e+30)
        probabilities = low(jax.nn.softmax(scores, axis=-1))
        return matmul(probabilities, values_all)
    return lax.map(jax.checkpoint(one_head), jnp.transpose(queries, (1, 0, 2)))

def layer_forward(tokens_row, segments_row, weights):
    attn_gain, attn_shift, mlp_gain, mlp_shift, w_query, b_query, w_keyvalue, w_out, b_out, w_up, b_up, w_down, b_down = weights
    attn_in = low(layer_norm(tokens_row, attn_gain, attn_shift))
    mlp_in = low(layer_norm(tokens_row, mlp_gain, mlp_shift))
    halfway = ROT_DIMS // 2
    position_ids = jnp.arange(SEQ_LEN).astype(jnp.int32)
    inverse = 10000.0 ** (-(jnp.arange(halfway).astype(jnp.float32) * (2.0 / ROT_DIMS)))
    angles = position_ids.astype(jnp.float32)[:, None] * inverse[None, :]
    cosine = jnp.cos(angles)[:, None, :]
    sine_table = jnp.sin(angles)[:, None, :]
    query_pre = low_back(matmul(attn_in, w_query) + b_query)
    kv_pre = low_back(matmul(attn_in, w_keyvalue))
    queries = low(rotate(query_pre.reshape(SEQ_LEN, HEADS, HEAD_DIM), cosine, sine_table) * (1.0 / math.sqrt(HEAD_DIM)))
    keyvalue = low(rotate(kv_pre[:, None, :], cosine, sine_table)[:, 0, :])
    allowed = (position_ids[None, :] <= position_ids[:, None]) & (segments_row[:, None] == segments_row[None, :])
    head_mix = attention(queries, keyvalue, allowed)
    attn_mix = low_back(low(jnp.transpose(head_mix, (1, 0, 2)).reshape(SEQ_LEN, D)))
    attn_branch = matmul(attn_mix, w_out) + b_out
    hidden = low_back(matmul(mlp_in, w_up) + b_up)
    activated = low(jax.nn.gelu(hidden, approximate=False))
    mlp_branch = matmul(activated, w_down) + b_down
    branches = low_back(attn_branch + mlp_branch)
    valid_rows = (segments_row >= 0).astype(jnp.float32)
    return (tokens_row + valid_rows[:, None] * branches, keyvalue)

def reference(tokens, segment_ids, attn_gain, attn_shift, mlp_gain, mlp_shift, w_query, b_query, w_keyvalue, w_out, b_out, w_up, b_up, w_down, b_down, out_grad):
    weights = tuple((argument.astype(jnp.float32) for argument in (attn_gain, attn_shift, mlp_gain, mlp_shift, w_query, b_query, w_keyvalue, w_out, b_out, w_up, b_up, w_down, b_down)))

    def per_row(running, row_data):
        tokens_row, segments_row, grad_row = row_data

        def forward(tokens_value, *weight_values):
            return layer_forward(tokens_value, segments_row, weight_values)
        (output_row, keyvalue_row), pullback = jax.vjp(forward, tokens_row.astype(jnp.float32), *weights)
        gradients = pullback((grad_row.astype(jnp.float32), jnp.zeros_like(keyvalue_row)))
        updated = tuple((before + gradient for before, gradient in zip(running, gradients[1:])))
        return (updated, (output_row.astype(jnp.bfloat16), keyvalue_row.astype(jnp.bfloat16), gradients[0].astype(jnp.bfloat16)))
    starting = tuple((jnp.zeros_like(weight) for weight in weights))
    summed, (outputs, keyvalues, token_grads) = lax.scan(per_row, starting, (tokens, segment_ids, out_grad))
    return (outputs, keyvalues, token_grads, summed[0], summed[1], summed[2], summed[3], summed[4], summed[5], summed[6], summed[7], summed[8], summed[9], summed[10], summed[11], summed[12])
```

```python
import functools
import math

import jax
import jax.numpy as jnp
from jax import lax
from jax.experimental import pallas as pl
from jax.experimental.pallas import tpu as pltpu
from jax.sharding import PartitionSpec as P

ROT_DIMS = 16
HALF_ROT = ROT_DIMS // 2
DOCS = 6
EPSILON = 1e-05
KEY_BLOCK = 256
COUNT_ROWS = 16
LANES = 128
NEGATIVE = -1e30
BF = jnp.bfloat16
F32 = jnp.float32
NN = (((1,), (0,)), ((), ()))
NT = (((1,), (1,)), ((), ()))
TN = (((0,), (0,)), ((), ()))
VMEM_LIMIT = 60 * 1024 * 1024


def matmul(left, right, dims=NN):
    return lax.dot_general(left, right, dims, preferred_element_type=F32)


def params(count=1):
    return pltpu.CompilerParams(
        dimension_semantics=("arbitrary",) * count, vmem_limit_bytes=VMEM_LIMIT
    )


def whole(shape):
    return pl.BlockSpec(shape, lambda *_: (0,) * len(shape))


def permute_rows(values, order, rows):
    return jnp.concatenate([values[b * rows : (b + 1) * rows] for b in order], axis=0)


def valid_column(segment_row):
    length = segment_row.shape[-1]
    row = jnp.broadcast_to((segment_row >= 0).astype(F32), (LANES, length))
    return row.T[:, :1]


def norm_parts(values):
    center = values - jnp.mean(values, axis=-1, keepdims=True)
    spread = jnp.mean(center * center, axis=-1, keepdims=True)
    scale = lax.rsqrt(spread + EPSILON)
    return center * scale, scale


def turn(values, cosine, sine):
    leading = values[:HALF_ROT]
    trailing = values[HALF_ROT:ROT_DIMS]
    return jnp.concatenate(
        [leading * cosine - trailing * sine, trailing * cosine + leading * sine, values[ROT_DIMS:]],
        axis=0,
    )


def entry_kernel(
    head_size, order_a, order_b, rows, permuted,
    tok_ref, og_ref, seg_ref, gains_ref, wq_ref, bq_ref, wkv_ref, wo_ref, cos_ref, sin_ref,
    mlp_ref, bg_ref, mlp_t_ref, bg_t_ref, attn_t_ref, q_t_ref, g_t_ref, kv_ref, pay_ref,
):
    x = tok_ref[0].astype(F32)
    length, width = x.shape
    n, _ = norm_parts(x)
    attn_in = (n * gains_ref[0:1] + gains_ref[1:2]).astype(BF)
    mlp_in = (n * gains_ref[2:3] + gains_ref[3:4]).astype(BF)
    segments = seg_ref[0]
    bg = (og_ref[0].astype(F32) * valid_column(segments)).astype(BF)
    mlp_ref[...] = mlp_in
    bg_ref[...] = bg

    def turned(values, order):
        flipped = values.astype(F32).T
        if permuted:
            flipped = permute_rows(flipped, order, rows)
        return flipped.astype(BF)

    mlp_t_ref[...] = turned(mlp_in, order_a)
    attn_t_ref[...] = turned(attn_in, order_a)
    bg_t_ref[...] = turned(bg, order_b)

    cosine, sine = cos_ref[...], sin_ref[...]
    score_scale = 1.0 / math.sqrt(head_size)
    query_t = (matmul(attn_in, wq_ref[...]) + bq_ref[...]).T
    grad_t = matmul(wo_ref[...], bg, NT)
    for h in range(width // head_size):
        part = query_t[h * head_size : (h + 1) * head_size]
        q_t_ref[0, :, h * length : (h + 1) * length] = (
            turn(part, cosine, sine) * score_scale
        ).astype(BF)
        g_t_ref[0, :, h * length : (h + 1) * length] = grad_t[
            h * head_size : (h + 1) * head_size
        ].astype(BF)
    kv_t = matmul(attn_in, wkv_ref[...]).T
    kv = turn(kv_t, cosine, sine).T.astype(BF)
    kv_ref[0] = kv
    pay_ref[0, :length] = kv
    lane = lax.broadcasted_iota(jnp.int32, (1, LANES), 1)
    counts = jnp.zeros((1, LANES), F32)
    for c in range(DOCS):
        total = jnp.sum((segments == c).astype(F32), axis=1, keepdims=True)
        counts = counts + jnp.where(lane == c, total, 0.0)
    pay_ref[0, length:] = jnp.broadcast_to(counts, (COUNT_ROWS, LANES)).astype(BF)


def erf_parts(hidden):
    size = jnp.abs(hidden)
    t = 1.0 / (1.0 + (0.3275911 * math.sqrt(0.5)) * size)
    bell = jnp.exp(-0.5 * (hidden * hidden))
    poly = 0.5 * 1.061405429
    for c in (-1.453152027, 1.421413741, -0.284496736, 0.254829592):
        poly = poly * t + 0.5 * c
    tail = poly * t * bell
    cdf = jnp.where(hidden < 0, tail, 1.0 - tail)
    return hidden * cdf, cdf + hidden * bell * (1.0 / math.sqrt(2 * math.pi))


def mlp_kernel(
    chunk, side_ref, mlp_ref, bg_ref, mlp_t_ref, bg_t_ref, up_ref, bup_ref, down_ref,
    keep_a_ref, send_a_ref, keep_b_ref, send_b_ref, out_ref, din_ref, bupg_ref, act_s, hg_s,
):
    tokens, width = mlp_ref.shape
    first = pl.program_id(0) == 0

    @pl.when(first)
    def _():
        out_ref[...] = jnp.zeros_like(out_ref)
        din_ref[...] = jnp.zeros_like(din_ref)

    bupg_ref[...] = jnp.zeros_like(bupg_ref)
    bias = bup_ref[...].astype(F32)

    def step(i, carry):
        at = pl.ds(pl.multiple_of(i * chunk, chunk), chunk)
        hidden = matmul(mlp_ref[at, :], up_ref[...]) + bias
        back = matmul(bg_ref[at, :], down_ref[...], NT)
        act, slope = erf_parts(hidden)
        act = act.astype(BF)
        hg = (back * slope).astype(BF)
        act_s[at, :] = act
        hg_s[at, :] = hg
        bupg_ref[...] += jnp.sum(hg.astype(F32), axis=0, keepdims=True)
        out_ref[at, :] += matmul(act, down_ref[...])
        din_ref[at, :] += matmul(hg, up_ref[...], NT)
        return carry

    lax.fori_loop(0, tokens // chunk, step, 0)
    half = width // 2
    side = side_ref[0]
    mine = pl.ds(pl.multiple_of(side * half, half), half)
    other = pl.ds(pl.multiple_of((1 - side) * half, half), half)
    keep_a_ref[...] = matmul(mlp_t_ref[mine, :], hg_s[...]).astype(BF)
    send_a_ref[...] = matmul(mlp_t_ref[other, :], hg_s[...]).astype(BF)
    keep_b_ref[...] = matmul(bg_t_ref[mine, :], act_s[...]).astype(BF)
    send_b_ref[...] = matmul(bg_t_ref[other, :], act_s[...]).astype(BF)


def attention_kernel(
    heads, head_size, seq_devices, place_ref, seg_ref, q_t_ref, g_t_ref, even_ref, odd_ref,
    cos_ref, sin_ref, mix_t_ref, qpg_t_ref, dkeep_ref, dsend_ref,
    kv_s, kv_t_s, bias_s, p_s, ds_s, o_s, dq_s, dkv_s, m_s, l_s, d_s, mk_s,
):
    length = seg_ref.shape[-1]
    me = place_ref[0]
    start = me * length
    total = kv_s.shape[0]
    blocks = total // KEY_BLOCK

    counts = jnp.zeros((1, LANES), F32)
    for m in range(seq_devices):
        ref = (even_ref, odd_ref)[m % 2]
        at = pl.multiple_of((me ^ m) * length, length)
        kv_s[pl.ds(at, length), :] = ref[m // 2, 0, :length]
        counts = counts + ref[m // 2, 0, length : length + COUNT_ROWS].astype(F32)[:1]

    segments = seg_ref[0]
    low = jnp.zeros((1, length), F32)
    for c in range(DOCS):
        later = (segments > c) | (segments < 0)
        low = low + jnp.where(later, counts[:, c : c + 1], 0.0)
    low = low.astype(jnp.int32)
    first_block = jnp.min(low) // KEY_BLOCK
    end_block = (start + length - 1) // KEY_BLOCK + 1
    place = start + lax.broadcasted_iota(jnp.int32, (1, length), 1)

    m_s[...] = jnp.full_like(m_s, NEGATIVE)
    l_s[...] = jnp.zeros_like(l_s)
    o_s[...] = jnp.zeros_like(o_s)
    dq_s[...] = jnp.zeros_like(dq_s)
    dkv_s[...] = jnp.zeros_like(dkv_s)

    def forward(b, carry):
        at = pl.multiple_of(b * KEY_BLOCK, KEY_BLOCK)
        kv = kv_s[pl.ds(at, KEY_BLOCK), :]
        keys = kv[:, :head_size]
        kv_t = kv.astype(F32).T.astype(BF)
        kv_t_s[b] = kv_t
        values_t = kv_t[head_size:]
        key_place = at + lax.broadcasted_iota(jnp.int32, (KEY_BLOCK, length), 0)
        allowed = (key_place <= place) & (key_place >= low)
        bias_s[...] = jnp.where(allowed, 0.0, NEGATIVE)
        for h in range(heads):
            cols = slice(h * length, (h + 1) * length)
            row = slice(h, h + 1)
            s = matmul(keys, q_t_ref[0, :, cols]) + bias_s[...]
            before = m_s[row, :]
            now = jnp.maximum(before, jnp.max(s, axis=0, keepdims=True))
            p = jnp.exp(s - now)
            shrink = jnp.exp(before - now)
            l_s[row, :] = l_s[row, :] * shrink + jnp.sum(p, axis=0, keepdims=True)
            low_p = p.astype(BF)
            p_s[b, :, cols] = low_p
            o_s[:, cols] = o_s[:, cols] * shrink + matmul(values_t, low_p)
            m_s[row, :] = now
            mk_s[b, row, :] = now
        return carry

    lax.fori_loop(first_block, end_block, forward, 0)

    for h in range(heads):
        cols = slice(h * length, (h + 1) * length)
        row = slice(h, h + 1)
        inverse = 1.0 / l_s[row, :]
        mixed = o_s[:, cols] * inverse
        mix_t_ref[h * head_size : (h + 1) * head_size, :] = mixed.astype(BF)
        d_s[row, :] = jnp.sum(mixed * g_t_ref[0, :, cols].astype(F32), axis=0, keepdims=True)
        l_s[row, :] = inverse

    def backward(b, carry):
        at = pl.multiple_of(b * KEY_BLOCK, KEY_BLOCK)
        values = kv_s[pl.ds(at, KEY_BLOCK), :][:, head_size:]
        keys_t = kv_t_s[b][:head_size]
        for h in range(heads):
            cols = slice(h * length, (h + 1) * length)
            row = slice(h, h + 1)
            factor = jnp.exp(mk_s[b, row, :] - m_s[row, :]) * l_s[row, :]
            p = p_s[b, :, cols].astype(F32) * factor
            dp = matmul(values, g_t_ref[0, :, cols])
            ds = (p * (dp - d_s[row, :])).astype(BF)
            p_s[b, :, cols] = p.astype(BF)
            ds_s[:, cols] = ds
            dq_s[:, cols] += matmul(keys_t, ds)
        dk = matmul(ds_s[...], q_t_ref[0], NT)
        dv = matmul(p_s[b], g_t_ref[0], NT)
        dkv_s[pl.ds(at, KEY_BLOCK), :] = jnp.concatenate([dk, dv], axis=1).astype(BF)
        return carry

    lax.fori_loop(first_block, end_block, backward, 0)

    cosine, sine = cos_ref[...], sin_ref[...]
    score_scale = 1.0 / math.sqrt(head_size)
    for h in range(heads):
        cols = slice(h * length, (h + 1) * length)
        qpg_t_ref[h * head_size : (h + 1) * head_size, :] = turn(
            dq_s[:, cols] * score_scale, cosine, -sine
        ).astype(BF)
    for m in range(seq_devices):
        ref = (dkeep_ref, dsend_ref)[m % 2]
        at = pl.multiple_of((me ^ m) * length, length)
        ref[m // 2, 0] = dkv_s[pl.ds(at, length), :]


def mix_kernel(
    side_ref, tok_ref, seg_ref, mix_t_ref, qpg_t_ref, attn_t_ref, bg_t_ref, mlp_ref, wo_ref,
    bias_ref, out_ref, keep_q_ref, send_q_ref, keep_o_ref, send_o_ref, acc_q, acc_o,
):
    step, steps = pl.program_id(0), pl.num_programs(0)

    @pl.when(step == 0)
    def _():
        acc_q[...] = jnp.zeros_like(acc_q)
        acc_o[...] = jnp.zeros_like(acc_o)

    mix_t = mix_t_ref[...]
    branch = matmul(mix_t, wo_ref[...], TN) + bias_ref[...] + mlp_ref[...]
    out_ref[0] = (tok_ref[0].astype(F32) + valid_column(seg_ref[0]) * branch).astype(BF)
    acc_q[...] += matmul(attn_t_ref[...], qpg_t_ref[...], NT)
    acc_o[...] += matmul(bg_t_ref[...], mix_t, NT)

    @pl.when(step == steps - 1)
    def _():
        half = acc_q.shape[0] // 2
        side = side_ref[0]
        mine = pl.ds(pl.multiple_of(side * half, half), half)
        other = pl.ds(pl.multiple_of((1 - side) * half, half), half)
        keep_q_ref[...] = acc_q[mine, :].astype(BF)
        send_q_ref[...] = acc_q[other, :].astype(BF)
        keep_o_ref[...] = acc_o[mine, :].astype(BF)
        send_o_ref[...] = acc_o[other, :].astype(BF)


def exit_kernel(
    order_a, rows, permuted,
    side_ref, tok_ref, og_ref, seg_ref, qpg_t_ref, attn_t_ref, din_ref, wq_ref, wkv_ref,
    gains_ref, cos_ref, sin_ref, bupg_ref, shuffle_ref, dkv_refs,
    tg_ref, keep_ref, send_ref, acc, vec,
):
    step, steps = pl.program_id(0), pl.num_programs(0)

    @pl.when(step == 0)
    def _():
        acc[...] = jnp.zeros_like(acc)
        vec[...] = jnp.zeros_like(vec)

    dkv = sum((ref[0].astype(F32) for ref in dkv_refs[1:]), dkv_refs[0][0].astype(F32))
    kvpg_t = turn(dkv.T, cos_ref[...], -sin_ref[...]).astype(BF)
    acc[...] += matmul(attn_t_ref[...], kvpg_t, NT)
    qpg_t = qpg_t_ref[...]
    d_attn = (matmul(wq_ref[...], qpg_t) + matmul(wkv_ref[...], kvpg_t)).T
    d_mlp = din_ref[...]
    n, scale = norm_parts(tok_ref[0].astype(F32))
    og = og_ref[0].astype(F32)
    e = d_attn * gains_ref[0:1] + d_mlp * gains_ref[2:3]
    inner = jnp.mean(e * n, axis=-1, keepdims=True)
    tg_ref[0] = (og + scale * (e - jnp.mean(e, axis=-1, keepdims=True) - n * inner)).astype(BF)
    ones = jnp.ones((8, qpg_t.shape[1]), BF)
    bg = (og * valid_column(seg_ref[0])).astype(BF)
    sums = [d_attn * n, d_attn, d_mlp * n, d_mlp, None, bg.astype(F32)]
    for j, value in enumerate(sums):
        if value is None:
            part = matmul(ones, qpg_t, NT)[:1]
        else:
            part = jnp.sum(value, axis=0, keepdims=True)
        vec[j : j + 1, :] += part

    @pl.when(step == steps - 1)
    def _():
        vec[8:12, :] = bupg_ref[...]
        if permuted:
            columns = permute_rows(vec[...].T, order_a, rows)
        else:
            columns = lax.dot_general(
                shuffle_ref[...], vec[...], NT, precision=lax.Precision.HIGHEST,
                preferred_element_type=F32,
            )
        half = columns.shape[0] // 2
        acc_columns = slice(0, LANES)
        vec_columns = slice(LANES, 2 * LANES)
        for side in range(2):

            @pl.when(side_ref[0] == side)
            def _():
                mine = slice(side * half, (side + 1) * half)
                other = slice((1 - side) * half, (2 - side) * half)
                keep_ref[:, acc_columns] = acc[mine, :].astype(BF)
                send_ref[:, acc_columns] = acc[other, :].astype(BF)
                keep_ref[:, vec_columns] = columns[mine].astype(BF)
                send_ref[:, vec_columns] = columns[other].astype(BF)


def group_of(count, most):
    size = min(count, most)
    while count % size:
        size -= 1
    return size


def combine_level(bits, pairs):
    pairs = list(pairs)
    count = pairs[0][0].shape[0]
    half = count // 2
    widest = max(keep.shape[2] for keep, _ in pairs)
    group = group_of(half, max(1, (4 * 3072) // widest))
    groups = half // group

    def body(bits_ref, *refs):
        inputs, outputs = refs[: 4 * len(pairs)], refs[4 * len(pairs) :]
        for j in range(len(pairs)):
            for k in range(2):
                left, right = inputs[4 * j + 2 * k], inputs[4 * j + 2 * k + 1]
                outputs[2 * j + k][...] = (
                    left[...].astype(F32) + right[...].astype(F32)
                ).astype(BF)

    in_specs, operands, out_specs, out_shapes = [], [], [], []
    for j, (keep, recv) in enumerate(pairs):
        block = (group,) + keep.shape[1:]

        def mine(i, bits_ref, j=j):
            return (bits_ref[j] * groups + i, 0, 0)

        def other(i, bits_ref, j=j):
            return ((1 - bits_ref[j]) * groups + i, 0, 0)

        for index in (mine, other):
            for operand in (keep, recv):
                in_specs.append(pl.BlockSpec(block, index))
                operands.append(operand)
            out_specs.append(pl.BlockSpec(block, lambda i, bits_ref: (i, 0, 0)))
            out_shapes.append(jax.ShapeDtypeStruct((half,) + keep.shape[1:], BF))
    results = pl.pallas_call(
        body,
        grid_spec=pltpu.PrefetchScalarGridSpec(
            num_scalar_prefetch=1, grid=(groups,), in_specs=in_specs, out_specs=out_specs
        ),
        out_shape=out_shapes,
        compiler_params=params(),
        name="combine",
    )(bits, *operands)
    return [(results[2 * j], results[2 * j + 1]) for j in range(len(pairs))]


def partners(size, mask):
    return [(i, i ^ mask) for i in range(size)]


def reduce_blocks(a_pair, b_pair, batch_devices, seq_devices, batch_index, seq_index):
    bits = list(range(1, seq_devices.bit_length() - 1))
    order_a, order_b = bits, bits[::-1]
    a_keep, a_send = a_pair
    b_keep, b_send = b_pair
    masks = (1, 1)
    for level in range(len(bits) + 1):
        a_recv = lax.ppermute(a_send, "seq", partners(seq_devices, masks[0]))
        b_recv = lax.ppermute(b_send, "seq", partners(seq_devices, masks[1]))
        if level == len(bits):
            break
        bit_a, bit_b = order_a[level], order_b[level]
        sides = jnp.stack([(seq_index >> bit_a) & 1, (seq_index >> bit_b) & 1])
        (a_keep, a_send), (b_keep, b_send) = combine_level(
            sides, [(a_keep, a_recv), (b_keep, b_recv)]
        )
        masks = (1 << bit_a, 1 << bit_b)
    totals = []
    for keep, recv in ((a_keep, a_recv), (b_keep, b_recv)):
        both = keep.astype(F32) + recv.astype(F32)
        own = lax.dynamic_index_in_dim(both, batch_index, 0, keepdims=False)
        for mask in range(1, batch_devices):
            away = lax.dynamic_index_in_dim(both, batch_index ^ mask, 0, keepdims=False)
            got = lax.ppermute(away.astype(BF), "batch", partners(batch_devices, mask))
            own = own + got.astype(F32)
        totals.append(own)
    return totals


def on_device(
    tokens, segment_ids, attn_gain, attn_shift, mlp_gain, mlp_shift, w_query, b_query,
    w_keyvalue, w_out, b_out, w_up, b_up, w_down, b_down, out_grad,
):
    row_count, length, width = tokens.shape
    head_size = w_keyvalue.shape[1] // 2
    heads = width // head_size
    hidden = w_up.shape[1]
    token_count = row_count * length
    seq_devices = lax.axis_size("seq")
    batch_devices = lax.axis_size("batch")
    devices = seq_devices * batch_devices
    seq_index = lax.axis_index("seq").astype(jnp.int32)
    batch_index = lax.axis_index("batch").astype(jnp.int32)
    side = (seq_index & 1).reshape(1)
    place = seq_index.reshape(1)
    total = length * seq_devices
    rows = width // devices
    permuted = rows % 8 == 0
    seq_bits = list(range(seq_devices.bit_length() - 1))

    def device_order(bits):
        order = []
        for k in range(seq_devices):
            at = 0
            for j, bit in enumerate(bits):
                at |= ((k >> (len(bits) - 1 - j)) & 1) << bit
            order += [z * seq_devices + at for z in range(batch_devices)]
        return order

    order_a = device_order(seq_bits)
    order_b = device_order(seq_bits[:1] + seq_bits[:0:-1])

    def ordered(values, order):
        if permuted:
            return values
        shaped = values.reshape(values.shape[:-2] + (devices, rows, values.shape[-1]))
        return jnp.take(shaped, jnp.array(order), axis=-3).reshape(values.shape)

    gains = jnp.stack([attn_gain, attn_shift, mlp_gain, mlp_shift]).astype(F32)
    positions = (seq_index * length + jnp.arange(length)).astype(F32)
    inverse = 10000.0 ** (-(jnp.arange(HALF_ROT).astype(F32) * (2.0 / ROT_DIMS)))
    angles = inverse[:, None] * positions[None, :]
    cosine, sine = jnp.cos(angles), jnp.sin(angles)
    segments = segment_ids.reshape(row_count, 1, length)

    def row_block(shape):
        return pl.BlockSpec((1,) + shape, lambda r, *_: (r, 0, 0))

    token_block = pl.BlockSpec((length, width), lambda r, *_: (r, 0))
    if length % LANES == 0:
        column_block = pl.BlockSpec((width, length), lambda r, *_: (0, r))
        columns = jax.ShapeDtypeStruct((width, token_count), BF)
    else:
        column_block = pl.BlockSpec((None, width, length), lambda r, *_: (r, 0, 0))
        columns = jax.ShapeDtypeStruct((row_count, width, length), BF)

    def joined(values):
        if values.ndim == 2:
            return values
        return jnp.transpose(values, (1, 0, 2)).reshape(width, token_count)

    mlp_in, bg, mlp_t, bg_t, attn_t, q_t, g_t, keyvalue, payload = pl.pallas_call(
        functools.partial(entry_kernel, head_size, order_a, order_b, rows, permuted),
        grid=(row_count,),
        in_specs=[
            row_block((length, width)), row_block((length, width)), row_block((1, length)),
            whole((4, width)), whole((width, width)), whole((1, width)),
            whole((width, 2 * head_size)), whole((width, width)),
            whole((HALF_ROT, length)), whole((HALF_ROT, length)),
        ],
        out_specs=[
            token_block, token_block, column_block, column_block, column_block,
            row_block((head_size, heads * length)), row_block((head_size, heads * length)),
            row_block((length, 2 * head_size)), row_block((length + COUNT_ROWS, 2 * head_size)),
        ],
        out_shape=[
            jax.ShapeDtypeStruct((token_count, width), BF),
            jax.ShapeDtypeStruct((token_count, width), BF),
            columns,
            columns,
            columns,
            jax.ShapeDtypeStruct((row_count, head_size, heads * length), BF),
            jax.ShapeDtypeStruct((row_count, head_size, heads * length), BF),
            jax.ShapeDtypeStruct((row_count, length, 2 * head_size), BF),
            jax.ShapeDtypeStruct((row_count, length + COUNT_ROWS, 2 * head_size), BF),
        ],
        compiler_params=params(),
        name="entry",
    )(
        tokens, out_grad, segments, gains, w_query, b_query.astype(F32).reshape(1, width),
        w_keyvalue, w_out, cosine, sine,
    )
    mlp_t, attn_t = ordered(mlp_t, order_a), ordered(attn_t, order_a)
    bg_t = ordered(bg_t, order_b)

    gathered = [payload]
    for mask in range(2, seq_devices, 2):
        gathered.append(lax.ppermute(payload, "seq", partners(seq_devices, mask)))
    even = jnp.stack(gathered)
    odd = lax.ppermute(even, "seq", partners(seq_devices, 1))

    tile = min(512, hidden)
    half = width // 2
    tile_cols = pl.BlockSpec((half, tile), lambda f, *_: (0, f))
    half_shape = jax.ShapeDtypeStruct((half, hidden), BF)
    keep_a, send_a, keep_b, send_b, mlp_out, mlp_din, b_up_part = pl.pallas_call(
        functools.partial(mlp_kernel, math.gcd(256, token_count)),
        grid_spec=pltpu.PrefetchScalarGridSpec(
            num_scalar_prefetch=1,
            grid=(hidden // tile,),
            in_specs=[
                whole((token_count, width)), whole((token_count, width)),
                whole((width, token_count)), whole((width, token_count)),
                pl.BlockSpec((width, tile), lambda f, *_: (0, f)),
                pl.BlockSpec((1, tile), lambda f, *_: (0, f)),
                pl.BlockSpec((tile, width), lambda f, *_: (f, 0)),
            ],
            out_specs=[
                tile_cols, tile_cols, tile_cols, tile_cols,
                whole((token_count, width)), whole((token_count, width)),
                pl.BlockSpec((1, tile), lambda f, *_: (0, f)),
            ],
            scratch_shapes=[
                pltpu.VMEM((token_count, tile), BF), pltpu.VMEM((token_count, tile), BF),
            ],
        ),
        out_shape=[
            half_shape, half_shape, half_shape, half_shape,
            jax.ShapeDtypeStruct((token_count, width), F32),
            jax.ShapeDtypeStruct((token_count, width), F32),
            jax.ShapeDtypeStruct((1, hidden), F32),
        ],
        compiler_params=params(),
        name="mlp",
    )(side, mlp_in, bg, joined(mlp_t), joined(bg_t), w_up, b_up.reshape(1, hidden), w_down)

    def blocks_of(values):
        return values.reshape(devices // 2, rows, values.shape[1])

    def reduced(a_pair, b_pair):
        return reduce_blocks(
            tuple(blocks_of(v) for v in a_pair), tuple(blocks_of(v) for v in b_pair),
            batch_devices, seq_devices, batch_index, seq_index,
        )

    w_up_grad, w_down_grad_t = reduced((keep_a, send_a), (keep_b, send_b))

    half_seq = seq_devices // 2
    lanes = heads * length
    blocks = total // KEY_BLOCK
    kv_rows = pl.BlockSpec(
        (half_seq, 1, length + COUNT_ROWS, 2 * head_size), lambda r, *_: (0, r, 0, 0)
    )
    dkv_rows = pl.BlockSpec((half_seq, 1, length, 2 * head_size), lambda r, *_: (0, r, 0, 0))
    stat_rows = -(-heads // 8) * 8
    mix_t, qpg_t, dkv_keep, dkv_send = pl.pallas_call(
        functools.partial(attention_kernel, heads, head_size, seq_devices),
        grid_spec=pltpu.PrefetchScalarGridSpec(
            num_scalar_prefetch=1,
            grid=(row_count,),
            in_specs=[
                row_block((1, length)),
                row_block((head_size, lanes)), row_block((head_size, lanes)),
                kv_rows, kv_rows, whole((HALF_ROT, length)), whole((HALF_ROT, length)),
            ],
            out_specs=[column_block, column_block, dkv_rows, dkv_rows],
            scratch_shapes=[
                pltpu.VMEM((total, 2 * head_size), BF),
                pltpu.VMEM((blocks, 2 * head_size, KEY_BLOCK), BF),
                pltpu.VMEM((KEY_BLOCK, length), F32),
                pltpu.VMEM((blocks, KEY_BLOCK, lanes), BF),
                pltpu.VMEM((KEY_BLOCK, lanes), BF),
                pltpu.VMEM((head_size, lanes), F32),
                pltpu.VMEM((head_size, lanes), F32),
                pltpu.VMEM((total, 2 * head_size), BF),
                pltpu.VMEM((stat_rows, length), F32),
                pltpu.VMEM((stat_rows, length), F32),
                pltpu.VMEM((stat_rows, length), F32),
                pltpu.VMEM((blocks, stat_rows, length), F32),
            ],
        ),
        out_shape=[
            columns,
            columns,
            jax.ShapeDtypeStruct((half_seq, row_count, length, 2 * head_size), BF),
            jax.ShapeDtypeStruct((half_seq, row_count, length, 2 * head_size), BF),
        ],
        compiler_params=params(),
        name="attention",
    )(place, segments, q_t, g_t, even, odd, cosine, sine)

    dkv_recv = lax.ppermute(dkv_send, "seq", partners(seq_devices, 1))
    dkv_sum = dkv_keep.astype(F32) + dkv_recv.astype(F32)
    dkv_parts = [dkv_sum[0].astype(BF)]
    for j in range(1, half_seq):
        dkv_parts.append(
            lax.ppermute(dkv_sum[j].astype(BF), "seq", partners(seq_devices, 2 * j))
        )

    half_spec = whole((half, width))
    half_width = jax.ShapeDtypeStruct((half, width), BF)
    output, keep_q, send_q, keep_o, send_o = pl.pallas_call(
        mix_kernel,
        grid_spec=pltpu.PrefetchScalarGridSpec(
            num_scalar_prefetch=1,
            grid=(row_count,),
            in_specs=[
                row_block((length, width)), row_block((1, length)), column_block, column_block,
                column_block, column_block, token_block, whole((width, width)),
                whole((1, width)),
            ],
            out_specs=[row_block((length, width)), half_spec, half_spec, half_spec, half_spec],
            scratch_shapes=[pltpu.VMEM((width, width), F32), pltpu.VMEM((width, width), F32)],
        ),
        out_shape=[
            jax.ShapeDtypeStruct((row_count, length, width), BF),
            half_width, half_width, half_width, half_width,
        ],
        compiler_params=params(),
        name="mix",
    )(
        side, tokens, segments, mix_t, qpg_t, attn_t, bg_t, mlp_out, w_out,
        (b_out.astype(F32) + b_down.astype(F32)).reshape(1, width),
    )

    dkv_count = len(dkv_parts)

    def exit_body(*refs):
        fixed, rest = refs[:14], refs[14:]
        exit_kernel(order_a, rows, permuted, *fixed, rest[:dkv_count], *rest[dkv_count:])

    places = (
        jnp.array(order_a)[:, None] * rows + jnp.arange(rows)[None, :]
    ).reshape(width, 1)
    shuffle = (places == jnp.arange(width)[None, :]).astype(F32)
    if permuted:
        shuffle = shuffle[:8, :LANES]

    extra_spec = whole((half, 2 * LANES))
    extra_shape = jax.ShapeDtypeStruct((half, 2 * LANES), BF)
    tokens_grad, keep_x, send_x = pl.pallas_call(
        exit_body,
        grid_spec=pltpu.PrefetchScalarGridSpec(
            num_scalar_prefetch=1,
            grid=(row_count,),
            in_specs=[
                row_block((length, width)), row_block((length, width)), row_block((1, length)),
                column_block, column_block, token_block, whole((width, width)),
                whole((width, 2 * head_size)), whole((4, width)),
                whole((HALF_ROT, length)), whole((HALF_ROT, length)),
                whole((4, width)), whole(shuffle.shape),
            ]
            + [row_block((length, 2 * head_size))] * dkv_count,
            out_specs=[row_block((length, width)), extra_spec, extra_spec],
            scratch_shapes=[
                pltpu.VMEM((width, 2 * head_size), F32), pltpu.VMEM((LANES, width), F32),
            ],
        ),
        out_shape=[
            jax.ShapeDtypeStruct((row_count, length, width), BF), extra_shape, extra_shape,
        ],
        compiler_params=params(),
        name="exit",
    )(
        side, tokens, out_grad, segments, qpg_t, attn_t, mlp_din, w_query, w_keyvalue, gains,
        cosine, sine, b_up_part.reshape(width, hidden // width).T, shuffle, *dkv_parts,
    )

    own_a, own_b = reduced(
        (jnp.concatenate([keep_q, keep_x], axis=1), jnp.concatenate([send_q, send_x], axis=1)),
        (keep_o, send_o),
    )
    vectors = own_a[:, width + LANES :]
    return (
        output,
        keyvalue,
        tokens_grad,
        vectors[:, 0],
        vectors[:, 1],
        vectors[:, 2],
        vectors[:, 3],
        own_a[:, :width],
        vectors[:, 4],
        own_a[:, width : width + LANES],
        own_b.T,
        vectors[:, 5],
        w_up_grad,
        vectors[:, 8 : 8 + hidden // width].reshape(-1),
        w_down_grad_t.T,
        vectors[:, 5],
    )


def solution(mesh):
    row_spec = P("batch", "seq", None)
    split = P(("batch", "seq"))
    first = P(("batch", "seq"), None)
    last = P(None, ("batch", "seq"))
    return jax.shard_map(
        on_device,
        mesh=mesh,
        in_specs=(row_spec, P("batch", "seq")) + (P(),) * 13 + (row_spec,),
        out_specs=(
            row_spec, row_spec, row_spec, split, split, split, split, first, split, first, last,
            split, first, split, last, split,
        ),
        check_vma=False,
    )
```

```python
import functools
import math

import jax
import jax.numpy as jnp
from jax import lax
from jax.experimental import pallas as pl
from jax.experimental.pallas import tpu as pltpu
from jax.sharding import PartitionSpec as P

ROT_DIMS = 16
HALF_ROT = ROT_DIMS // 2
DOCS = 6
EPSILON = 1e-05
KEY_BLOCK = 256
COUNT_ROWS = 16
LANES = 128
NEGATIVE = -1e30
BF = jnp.bfloat16
F32 = jnp.float32
NN = (((1,), (0,)), ((), ()))
NT = (((1,), (1,)), ((), ()))
TN = (((0,), (0,)), ((), ()))


def matmul(left, right, dims=NN):
    return lax.dot_general(left, right, dims, preferred_element_type=F32)


def params(limit):
    return pltpu.CompilerParams(
        dimension_semantics=("arbitrary",), vmem_limit_bytes=limit * 1024 * 1024
    )


def cost(flops, size):
    return pl.CostEstimate(flops=int(flops), transcendentals=0, bytes_accessed=int(size))


def whole(shape):
    return pl.BlockSpec(shape, lambda *_: (0,) * len(shape))


def permute_rows(values, order, rows):
    return jnp.concatenate([values[b * rows : (b + 1) * rows] for b in order], axis=0)


def row_of(ref):
    return ref[...].astype(F32).reshape(1, ref.shape[0])


def valid_column(segment_row):
    length = segment_row.shape[-1]
    row = jnp.broadcast_to((segment_row >= 0).astype(F32), (LANES, length))
    return row.T[:, :1]


def norm_parts(values):
    center = values - jnp.mean(values, axis=-1, keepdims=True)
    spread = jnp.mean(center * center, axis=-1, keepdims=True)
    scale = lax.rsqrt(spread + EPSILON)
    return center * scale, scale


def turn(values, cosine, sine):
    leading = values[:HALF_ROT]
    trailing = values[HALF_ROT:ROT_DIMS]
    return jnp.concatenate(
        [leading * cosine - trailing * sine, trailing * cosine + leading * sine, values[ROT_DIMS:]],
        axis=0,
    )


def entry_kernel(
    head_size, order_a, order_b, rows, permuted,
    tok_ref, og_ref, seg_ref, ag_ref, as_ref, mg_ref, ms_ref, bq_ref, wq_ref, wkv_ref, wo_ref,
    cos_ref, sin_ref, mlp_ref, bg_ref, mlp_t_ref, bg_t_ref, attn_t_ref, q_t_ref, g_t_ref, kv_ref, pay_ref,
):
    x = tok_ref[0].astype(F32)
    length, width = x.shape
    n, _ = norm_parts(x)
    attn_in = (n * row_of(ag_ref) + row_of(as_ref)).astype(BF)
    mlp_in = (n * row_of(mg_ref) + row_of(ms_ref)).astype(BF)
    segments = seg_ref[pl.ds(pl.program_id(0), 1), :]
    bg = (og_ref[0].astype(F32) * valid_column(segments)).astype(BF)
    mlp_ref[...] = mlp_in
    bg_ref[...] = bg

    def turned(values, order):
        flipped = values.astype(F32).T
        if permuted:
            flipped = permute_rows(flipped, order, rows)
        return flipped.astype(BF)

    mlp_t_ref[...] = turned(mlp_in, order_a)
    attn_t_ref[...] = turned(attn_in, order_a)
    bg_t_ref[...] = turned(bg, order_b)

    cosine, sine = cos_ref[...], sin_ref[...]
    score_scale = 1.0 / math.sqrt(head_size)
    query_t = (matmul(attn_in, wq_ref[...]) + row_of(bq_ref)).T
    grad_t = matmul(wo_ref[...], bg, NT)
    for h in range(width // head_size):
        part = query_t[h * head_size : (h + 1) * head_size]
        q_t_ref[0, :, h * length : (h + 1) * length] = (
            turn(part, cosine, sine) * score_scale
        ).astype(BF)
        g_t_ref[0, :, h * length : (h + 1) * length] = grad_t[
            h * head_size : (h + 1) * head_size
        ].astype(BF)
    kv_t = matmul(attn_in, wkv_ref[...]).T
    kv = turn(kv_t, cosine, sine).T.astype(BF)
    kv_ref[0] = kv
    pay_ref[0, :length] = kv
    lane = lax.broadcasted_iota(jnp.int32, (1, LANES), 1)
    counts = jnp.zeros((1, LANES), F32)
    for c in range(DOCS):
        total = jnp.sum((segments == c).astype(F32), axis=1, keepdims=True)
        counts = counts + jnp.where(lane == c, total, 0.0)
    pay_ref[0, length:] = jnp.broadcast_to(counts, (COUNT_ROWS, LANES)).astype(BF)


def gelu_parts(hidden):
    cdf = 0.5 * (1.0 + lax.erf(hidden * math.sqrt(0.5)))
    bell = jnp.exp(-0.5 * (hidden * hidden)) * (1.0 / math.sqrt(2 * math.pi))
    return hidden * cdf, cdf + hidden * bell


def mlp_kernel(
    chunk, side_ref, mlp_ref, bg_ref, mlp_t_ref, bg_t_ref, up_ref, bup_ref, down_ref,
    keep_ref, send_ref, out_ref, din_ref, bupg_ref, act_s, hg_s,
):
    tokens, width = mlp_ref.shape

    @pl.when(pl.program_id(0) == 0)
    def _():
        out_ref[...] = jnp.zeros_like(out_ref)
        din_ref[...] = jnp.zeros_like(din_ref)

    bupg_ref[...] = jnp.zeros_like(bupg_ref)
    bias = bup_ref[...].astype(F32)

    def step(i, carry):
        at = pl.ds(pl.multiple_of(i * chunk, chunk), chunk)
        hidden = matmul(mlp_ref[at, :], up_ref[...]) + bias
        back = matmul(bg_ref[at, :], down_ref[...], NT)
        act, slope = gelu_parts(hidden)
        act = act.astype(BF)
        hg = (back * slope).astype(BF)
        act_s[at, :] = act
        hg_s[at, :] = hg
        bupg_ref[...] += jnp.sum(hg.astype(F32), axis=0, keepdims=True)
        out_ref[at, :] += matmul(act, down_ref[...])
        din_ref[at, :] += matmul(hg, up_ref[...], NT)
        return carry

    lax.fori_loop(0, tokens // chunk, step, 0)
    half = width // 2
    side = side_ref[0]
    mine = pl.ds(pl.multiple_of(side * half, half), half)
    other = pl.ds(pl.multiple_of((1 - side) * half, half), half)
    send_ref[0] = matmul(mlp_t_ref[other, :], hg_s[...]).astype(BF)
    send_ref[1] = matmul(bg_t_ref[other, :], act_s[...]).astype(BF)
    keep_ref[0] = matmul(mlp_t_ref[mine, :], hg_s[...]).astype(BF)
    keep_ref[1] = matmul(bg_t_ref[mine, :], act_s[...]).astype(BF)


def attention_kernel(
    heads, head_size, seq_devices, first_row, where_ref, seg_ref, q_t_ref, g_t_ref, even_ref,
    odd_ref, cos_ref, sin_ref, *refs,
):
    (mix_t_ref, qpg_t_ref, dkeep_ref, dsend_ref, kv_s, kv_t_s, bias_s, p_s, ds_s, gk_s, o_s, dq_s,
     dkv_s, m_s, l_s, d_s, mk_s) = refs[-17:]
    length = seg_ref.shape[-1]
    me = where_ref[0]
    start = me * length
    group = math.gcd(heads, 3)

    def columns(h, count=1):
        return slice(h * length, (h + count) * length)

    def head(h):
        return slice(h * head_size, (h + 1) * head_size)

    counts = jnp.zeros((1, LANES), F32)
    for m in range(seq_devices):
        ref = (even_ref, odd_ref)[m % 2]
        at = pl.multiple_of((me ^ m) * length, length)
        kv_s[pl.ds(at, length), :] = ref[m // 2, 0, :length]
        counts = counts + ref[m // 2, 0, length : length + COUNT_ROWS].astype(F32)[:1]

    segments = seg_ref[pl.ds(first_row + pl.program_id(0), 1), :]
    low = jnp.zeros((1, length), F32)
    for c in range(DOCS):
        later = (segments > c) | (segments < 0)
        low = low + jnp.where(later, counts[:, c : c + 1], 0.0)
    low = low.astype(jnp.int32)
    first_block = jnp.min(low) // KEY_BLOCK
    end_block = (start + length - 1) // KEY_BLOCK + 1
    place = start + lax.broadcasted_iota(jnp.int32, (1, length), 1)

    m_s[...] = jnp.full_like(m_s, NEGATIVE)
    l_s[...] = jnp.zeros_like(l_s)
    o_s[...] = jnp.zeros_like(o_s)
    dq_s[...] = jnp.zeros_like(dq_s)
    dkv_s[...] = jnp.zeros_like(dkv_s)

    def forward(b, carry):
        at = pl.multiple_of(b * KEY_BLOCK, KEY_BLOCK)
        kv = kv_s[pl.ds(at, KEY_BLOCK), :]
        keys = kv[:, :head_size]
        kv_t = kv.astype(F32).T.astype(BF)
        kv_t_s[b] = kv_t
        summed = jnp.concatenate([kv_t[head_size:], jnp.ones((16, KEY_BLOCK), BF)], axis=0)
        key_place = at + lax.broadcasted_iota(jnp.int32, (KEY_BLOCK, length), 0)
        allowed = (key_place <= place) & (key_place >= low)
        bias_s[...] = jnp.where(allowed, 0.0, NEGATIVE)
        bias = bias_s[...]
        shrinks = {}

        def scores(h):
            return matmul(keys, q_t_ref[0, :, columns(h, group)])

        def mix(h):
            o = matmul(summed, p_s[b, :, columns(h, group)])
            for j in range(group):
                row = slice(h + j, h + j + 1)
                part = o[:, columns(j)]
                shrink = shrinks.pop(h + j)
                o_s[:, columns(h + j)] = o_s[:, columns(h + j)] * shrink + part[:head_size]
                l_s[row, :] = l_s[row, :] * shrink + part[head_size : head_size + 1]

        ready = scores(0)
        for h in range(0, heads, group):
            now_scores = ready
            if h + group < heads:
                ready = scores(h + group)
            for j in range(group):
                row = slice(h + j, h + j + 1)
                s = now_scores[:, columns(j)] + bias
                before = m_s[row, :]
                now = jnp.maximum(before, jnp.max(s, axis=0, keepdims=True))
                p_s[b, :, columns(h + j)] = jnp.exp(s - now).astype(BF)
                shrinks[h + j] = jnp.exp(before - now)
                m_s[row, :] = now
                mk_s[b, row, :] = now
            if h > 0:
                mix(h - group)
        mix(heads - group)
        return carry

    lax.fori_loop(first_block, end_block, forward, 0)

    for h in range(heads):
        row = slice(h, h + 1)
        inverse = 1.0 / l_s[row, :]
        mixed = o_s[:, columns(h)] * inverse
        mix_t_ref[head(h), :] = mixed.astype(BF)
        d_s[row, :] = jnp.sum(
            mixed * g_t_ref[0, :, columns(h)].astype(F32), axis=0, keepdims=True
        )
        l_s[row, :] = inverse

    def backward(b, carry):
        at = pl.multiple_of(b * KEY_BLOCK, KEY_BLOCK)
        values = kv_s[pl.ds(at, KEY_BLOCK), :][:, head_size:]
        keys_t = kv_t_s[b][:head_size]
        inners = {}

        def prob_grads(h):
            for j in range(group):
                row = slice(h + j, h + j + 1)
                factor = jnp.exp(mk_s[b, row, :] - m_s[row, :]) * l_s[row, :]
                scaled = g_t_ref[0, :, columns(h + j)].astype(F32) * factor
                gk_s[:, columns(h + j)] = scaled.astype(BF)
                inners[h + j] = d_s[row, :] * factor
            return matmul(values, gk_s[:, columns(h, group)])

        ready = prob_grads(0)
        for h in range(0, heads, group):
            now_grads = ready
            if h + group < heads:
                ready = prob_grads(h + group)
            for j in range(group):
                p = p_s[b, :, columns(h + j)].astype(F32)
                ds_s[:, columns(h + j)] = (
                    p * (now_grads[:, columns(j)] - inners.pop(h + j))
                ).astype(BF)
        dq_s[...] += matmul(keys_t, ds_s[...])
        dk = matmul(ds_s[...], q_t_ref[0], NT)
        dv = matmul(p_s[b], gk_s[...], NT)
        dkv_s[pl.ds(at, KEY_BLOCK), :] = jnp.concatenate([dk, dv], axis=1).astype(BF)
        return carry

    lax.fori_loop(first_block, end_block, backward, 0)

    cosine, sine = cos_ref[...], sin_ref[...]
    score_scale = 1.0 / math.sqrt(head_size)
    for h in range(heads):
        qpg_t_ref[head(h), :] = turn(
            dq_s[:, columns(h)] * score_scale, cosine, -sine
        ).astype(BF)
    for m in range(seq_devices):
        ref = (dkeep_ref, dsend_ref)[m % 2]
        at = pl.multiple_of((me ^ m) * length, length)
        ref[m // 2, 0] = dkv_s[pl.ds(at, length), :]


def mix_kernel(
    side_ref, tok_ref, seg_ref, mix_t_ref, qpg_t_ref, attn_t_ref, bg_t_ref, mlp_ref, wo_ref,
    bo_ref, bd_ref, out_ref, keep_ref, send_ref, acc_q, acc_o,
):
    step, steps = pl.program_id(0), pl.num_programs(0)

    @pl.when(step == 0)
    def _():
        acc_q[...] = jnp.zeros_like(acc_q)
        acc_o[...] = jnp.zeros_like(acc_o)

    mix_t = mix_t_ref[...]
    branch = matmul(mix_t, wo_ref[...], TN) + (row_of(bo_ref) + row_of(bd_ref)) + mlp_ref[...]
    out_ref[0] = (tok_ref[0].astype(F32) + valid_column(seg_ref[pl.ds(step, 1), :]) * branch).astype(BF)
    acc_q[...] += matmul(attn_t_ref[...], qpg_t_ref[...], NT)
    acc_o[...] += matmul(bg_t_ref[...], mix_t, NT)

    @pl.when(step == steps - 1)
    def _():
        half = acc_q.shape[0] // 2
        side = side_ref[0]
        mine = pl.ds(pl.multiple_of(side * half, half), half)
        other = pl.ds(pl.multiple_of((1 - side) * half, half), half)
        for j, acc in enumerate((acc_q, acc_o)):
            keep_ref[j] = acc[mine, :].astype(BF)
            send_ref[j] = acc[other, :].astype(BF)


def exit_kernel(
    order_a, rows, permuted,
    side_ref, tok_ref, og_ref, seg_ref, qpg_t_ref, attn_t_ref, din_ref, wq_ref, wkv_ref,
    ag_ref, mg_ref, cos_ref, sin_ref, bupg_ref, shuffle_ref, dkv_refs,
    tg_ref, keep_ref, send_ref, acc, vec,
):
    step, steps = pl.program_id(0), pl.num_programs(0)

    @pl.when(step == 0)
    def _():
        acc[...] = jnp.zeros_like(acc)
        vec[...] = jnp.zeros_like(vec)

    dkv = sum((ref[0].astype(F32) for ref in dkv_refs[1:]), dkv_refs[0][0].astype(F32))
    kvpg_t = turn(dkv.T, cos_ref[...], -sin_ref[...]).astype(BF)
    acc[...] += matmul(attn_t_ref[...], kvpg_t, NT)
    qpg_t = qpg_t_ref[...]
    d_attn = (matmul(wq_ref[...], qpg_t) + matmul(wkv_ref[...], kvpg_t)).T
    d_mlp = din_ref[...]
    n, scale = norm_parts(tok_ref[0].astype(F32))
    og = og_ref[0].astype(F32)
    e = d_attn * row_of(ag_ref) + d_mlp * row_of(mg_ref)
    inner = jnp.mean(e * n, axis=-1, keepdims=True)
    tg_ref[0] = (og + scale * (e - jnp.mean(e, axis=-1, keepdims=True) - n * inner)).astype(BF)
    ones = jnp.ones((8, qpg_t.shape[1]), BF)
    bg = (og * valid_column(seg_ref[pl.ds(step, 1), :])).astype(BF)
    sums = [d_attn * n, d_attn, d_mlp * n, d_mlp, None, bg.astype(F32)]
    for j, value in enumerate(sums):
        if value is None:
            part = matmul(ones, qpg_t, NT)[:1]
        else:
            part = jnp.sum(value, axis=0, keepdims=True)
        vec[j : j + 1, :] += part

    @pl.when(step == steps - 1)
    def _():
        vec[8:12, :] = bupg_ref[...]
        if permuted:
            columns = permute_rows(vec[...].T, order_a, rows)
        else:
            columns = lax.dot_general(
                shuffle_ref[...], vec[...], NT, precision=lax.Precision.HIGHEST,
                preferred_element_type=F32,
            )
        half = columns.shape[0] // 2
        acc_columns = slice(0, LANES)
        vec_columns = slice(LANES, 2 * LANES)
        for side in range(2):

            @pl.when(side_ref[0] == side)
            def _():
                mine = slice(side * half, (side + 1) * half)
                other = slice((1 - side) * half, (2 - side) * half)
                keep_ref[:, acc_columns] = acc[mine, :].astype(BF)
                send_ref[:, acc_columns] = acc[other, :].astype(BF)
                keep_ref[:, vec_columns] = columns[mine].astype(BF)
                send_ref[:, vec_columns] = columns[other].astype(BF)


def partners(size, mask):
    return [(i, i ^ mask) for i in range(size)]


class Stream:
    def __init__(self, arrays, count):
        self.terms = [(array, False, at, ()) for array, at in arrays]
        self.count = count

    def halve(self, bit):
        count = self.count = self.count // 2
        other = [(a, r, at + count, adds + ((bit, -count),)) for a, r, at, adds in self.terms]
        self.terms = [(a, r, at, adds + ((bit, count),)) for a, r, at, adds in self.terms]
        return other


def first_block(term, where_ref):
    at = term[2]
    for bit, weight in term[3]:
        at = at + ((where_ref[0] >> bit) & 1) * weight
    return at


def term_spec(term, group, move):
    if term[1]:
        return pl.BlockSpec(memory_space=pltpu.VMEM)
    shape = term[0].shape[1:]
    return pl.BlockSpec(
        (group,) + shape,
        lambda i, where_ref: (first_block(term, where_ref) // group + move(i, where_ref), 0, 0),
    )


def read_terms(terms, refs, group, move, where_ref):
    total = None
    for term, ref in zip(terms, refs):
        if term[1]:
            at = first_block(term, where_ref) + move * group
            value = ref[pl.ds(at, group)]
        else:
            value = ref[...]
        value = value.astype(F32)
        total = value if total is None else total + value
    return total


def call_on_terms(body, name, where, after, steps, in_specs, operands, out_specs, out_shape, size):
    return pl.pallas_call(
        body,
        grid_spec=pltpu.PrefetchScalarGridSpec(
            num_scalar_prefetch=1, grid=(steps,), in_specs=in_specs, out_specs=out_specs
        ),
        out_shape=out_shape,
        compiler_params=params(limit=24),
        cost_estimate=cost(0, size),
        name=name,
    )(ordered_after(where, *after), *operands)


def sums_to_send(picks, count, where, after, in_vmem):
    widest = max(terms[0][0].shape[2] for terms in picks)
    group = count
    while group > 1 and group * widest > 4 * 3072:
        group //= 2
    if in_vmem:
        group = count
    terms = [term for pick in picks for term in pick]
    shapes = [pick[0][0].shape[1:] for pick in picks]

    def body(where_ref, *refs):
        at = 0
        for j, pick in enumerate(picks):
            total = read_terms(
                pick, refs[at : at + len(pick)], group, pl.program_id(0), where_ref
            )
            refs[len(terms) + j][...] = total.astype(BF)
            at += len(pick)

    if in_vmem:
        out_specs = [pl.BlockSpec(memory_space=pltpu.VMEM) for _ in shapes]
    else:
        out_specs = [pl.BlockSpec((group,) + shape, lambda i, _: (i, 0, 0)) for shape in shapes]
    return call_on_terms(
        body, "combine", where, after, count // group,
        [term_spec(term, group, lambda i, _: i) for term in terms],
        [term[0] for term in terms],
        out_specs,
        [jax.ShapeDtypeStruct((count,) + shape, BF) for shape in shapes],
        2 * count * sum(math.prod(term[0].shape[1:]) for term in terms),
    )


def sums_along_batch(streams, batch_devices, where, after):
    masks = batch_devices - 1
    terms = [term for stream in streams for term in stream.terms]
    widths = [stream.terms[0][0].shape[2] for stream in streams]
    shape = (terms[0][0].shape[1], sum(widths))

    def body(where_ref, *refs):
        at = column = 0
        place = where_ref[1]
        for stream, width in zip(streams, widths):
            size = len(stream.terms)
            for m in range(masks):
                total = None
                for term, ref in zip(stream.terms, refs[at : at + size]):
                    first = first_block(term, where_ref) if term[1] else 0
                    value = ref[first + (place ^ (m + 1))].astype(F32)
                    total = value if total is None else total + value
                refs[len(terms) + m][:, column : column + width] = total.astype(BF)
            at, column = at + size, column + width

    return call_on_terms(
        body, "spread", where, after, 1,
        [term_spec(term, batch_devices, lambda i, _: 0) for term in terms],
        [term[0] for term in terms],
        [pl.BlockSpec(memory_space=pltpu.VMEM)] * masks,
        [jax.ShapeDtypeStruct(shape, BF)] * masks,
        2 * batch_devices * sum(math.prod(term[0].shape[1:]) for term in terms),
    )


def own_sums(streams, received, where, after=()):
    terms = [term for stream in streams for term in stream.terms]
    widths = [stream.terms[0][0].shape[2] for stream in streams]
    rows = terms[0][0].shape[1]

    def body(where_ref, *refs):
        gots, outputs = refs[len(terms) : -len(streams)], refs[-len(streams) :]
        at = column = 0
        for stream, width, output in zip(streams, widths, outputs):
            total = read_terms(
                stream.terms, refs[at : at + len(stream.terms)], 1, where_ref[1], where_ref
            )[0]
            for got in gots:
                total = total + got[:, column : column + width].astype(F32)
            output[...] = total
            at, column = at + len(stream.terms), column + width

    return call_on_terms(
        body, "own", where, after, 1,
        [term_spec(term, 1, lambda i, where_ref: where_ref[1]) for term in terms]
        + [pl.BlockSpec(memory_space=pltpu.VMEM)] * len(received),
        [term[0] for term in terms] + list(received),
        [whole((rows, width)) for width in widths],
        [jax.ShapeDtypeStruct((rows, width), F32) for width in widths],
        2 * rows * sum(term[0].shape[2] for term in terms),
    )


def ordered_after(value, *others):
    if not others:
        return value
    return lax.optimization_barrier((value, others))[0]


def reduce_level(streams, bits, seq_devices, where, after=(), in_vmem=False, recv_in_vmem=False):
    picks = [stream.halve(bit) for stream, bit in zip(streams, bits)]
    sends = sums_to_send(picks, streams[0].count, where, after, in_vmem)
    for stream, bit, send in zip(streams, bits, sends):
        recv = lax.ppermute(send, "seq", partners(seq_devices, 1 << bit))
        stream.terms.append((recv, recv_in_vmem, 0, ()))
    return sends


def reduce_along_batch(streams, batch_devices, where, after=()):
    sends = sums_along_batch(streams, batch_devices, where, after)
    return sends, [
        lax.ppermute(send, "batch", partners(batch_devices, m + 1)) for m, send in enumerate(sends)
    ]


def on_device(
    tokens, segment_ids, attn_gain, attn_shift, mlp_gain, mlp_shift, w_query, b_query,
    w_keyvalue, w_out, b_out, w_up, b_up, w_down, b_down, out_grad,
):
    row_count, length, width = tokens.shape
    head_size = w_keyvalue.shape[1] // 2
    heads = width // head_size
    hidden = w_up.shape[1]
    token_count = row_count * length
    seq_devices = lax.axis_size("seq")
    batch_devices = lax.axis_size("batch")
    devices = seq_devices * batch_devices
    seq_index = lax.axis_index("seq").astype(jnp.int32)
    batch_index = lax.axis_index("batch").astype(jnp.int32)
    side = (seq_index & 1).reshape(1)
    where = jnp.stack([seq_index, batch_index])
    rows = width // devices
    permuted = rows % 8 == 0
    seq_bits = list(range(seq_devices.bit_length() - 1))

    def device_order(bits):
        order = []
        for k in range(seq_devices):
            at = 0
            for j, bit in enumerate(bits):
                at |= ((k >> (len(bits) - 1 - j)) & 1) << bit
            order += [z * seq_devices + at for z in range(batch_devices)]
        return order

    order_a = device_order(seq_bits)
    order_b = device_order(seq_bits[:1] + seq_bits[:0:-1])

    def ordered(values, order):
        if permuted:
            return values
        shaped = values.reshape(values.shape[:-2] + (devices, rows, values.shape[-1]))
        return jnp.take(shaped, jnp.array(order), axis=-3).reshape(values.shape)

    positions = (seq_index * length + jnp.arange(length)).astype(F32)
    inverse = 10000.0 ** (-(jnp.arange(HALF_ROT).astype(F32) * (2.0 / ROT_DIMS)))
    angles = inverse[:, None] * positions[None, :]
    cosine, sine = jnp.cos(angles), jnp.sin(angles)
    segments_spec = whole((row_count, length))
    turn_spec = whole((HALF_ROT, length))
    width_spec = whole((width,))

    def row_block(shape, first=0):
        return pl.BlockSpec((1,) + shape, lambda r, *_: (first + r, 0, 0))

    token_block = pl.BlockSpec((length, width), lambda r, *_: (r, 0))
    whole_lanes = length % LANES == 0

    def column_block(first=0):
        if whole_lanes:
            return pl.BlockSpec((width, length), lambda r, *_: (0, first + r))
        return pl.BlockSpec((None, width, length), lambda r, *_: (first + r, 0, 0))

    columns = jax.ShapeDtypeStruct(
        (width, token_count) if whole_lanes else (row_count, width, length), BF
    )

    def joined(values):
        if whole_lanes:
            return values
        return jnp.transpose(values, (1, 0, 2)).reshape(width, token_count)

    lanes = heads * length
    mlp_in, bg, mlp_t, bg_t, attn_t, q_t, g_t, keyvalue, payload = pl.pallas_call(
        functools.partial(entry_kernel, head_size, order_a, order_b, rows, permuted),
        grid=(row_count,),
        in_specs=[
            row_block((length, width)), row_block((length, width)), segments_spec,
            width_spec, width_spec, width_spec, width_spec, width_spec,
            whole((width, width)), whole((width, 2 * head_size)), whole((width, width)),
            turn_spec, turn_spec,
        ],
        out_specs=[
            token_block, token_block, column_block(), column_block(), column_block(),
            row_block((head_size, lanes)), row_block((head_size, lanes)),
            row_block((length, 2 * head_size)), row_block((length + COUNT_ROWS, 2 * head_size)),
        ],
        out_shape=[
            jax.ShapeDtypeStruct((token_count, width), BF),
            jax.ShapeDtypeStruct((token_count, width), BF),
            columns,
            columns,
            columns,
            jax.ShapeDtypeStruct((row_count, head_size, lanes), BF),
            jax.ShapeDtypeStruct((row_count, head_size, lanes), BF),
            jax.ShapeDtypeStruct((row_count, length, 2 * head_size), BF),
            jax.ShapeDtypeStruct((row_count, length + COUNT_ROWS, 2 * head_size), BF),
        ],
        compiler_params=params(60),
        cost_estimate=cost(2 * token_count * width * (2 * width + 2 * head_size), 20 * token_count * width),
        name="entry",
    )(
        tokens, out_grad, segment_ids, attn_gain, attn_shift, mlp_gain, mlp_shift, b_query,
        w_query, w_keyvalue, w_out, cosine, sine,
    )
    mlp_t, attn_t = ordered(mlp_t, order_a), ordered(attn_t, order_a)
    bg_t = ordered(bg_t, order_b)

    gathered = [payload]
    for mask in range(2, seq_devices, 2):
        gathered.append(lax.ppermute(payload, "seq", partners(seq_devices, mask)))

    tile = math.gcd(512, hidden)
    half = width // 2
    pair_cols = pl.BlockSpec((2, half, tile), lambda f, *_: (0, 0, f))
    pair_shape = jax.ShapeDtypeStruct((2, half, hidden), BF)
    keep, send, mlp_out, mlp_din, b_up_part = pl.pallas_call(
        functools.partial(mlp_kernel, token_count),
        grid_spec=pltpu.PrefetchScalarGridSpec(
            num_scalar_prefetch=1,
            grid=(hidden // tile,),
            in_specs=[
                whole((token_count, width)), whole((token_count, width)),
                whole((width, token_count)), whole((width, token_count)),
                pl.BlockSpec((width, tile), lambda f, *_: (0, f)),
                pl.BlockSpec((1, tile), lambda f, *_: (0, f)),
                pl.BlockSpec((tile, width), lambda f, *_: (f, 0)),
            ],
            out_specs=[
                pair_cols, pair_cols, whole((token_count, width)), whole((token_count, width)),
                pl.BlockSpec((1, tile), lambda f, *_: (0, f)),
            ],
            scratch_shapes=[
                pltpu.VMEM((token_count, tile), BF), pltpu.VMEM((token_count, tile), BF),
            ],
        ),
        out_shape=[
            pair_shape, pair_shape,
            jax.ShapeDtypeStruct((token_count, width), F32),
            jax.ShapeDtypeStruct((token_count, width), F32),
            jax.ShapeDtypeStruct((1, hidden), F32),
        ],
        compiler_params=params(60),
        cost_estimate=cost(12 * token_count * width * hidden, 40 * token_count * width),
        name="mlp",
    )(side, mlp_in, bg, joined(mlp_t), joined(bg_t), w_up, b_up.reshape(1, hidden), w_down)

    even = jnp.stack(ordered_after(tuple(gathered), b_up_part))
    odd = lax.ppermute(even, "seq", partners(seq_devices, 1))

    bits = list(range(1, seq_devices.bit_length() - 1))
    blocks = devices // 2

    def pair_streams(keep, send):
        shape = (2 * blocks, rows, keep.shape[2])
        keep = keep.reshape(shape)
        recv = lax.ppermute(send.reshape(shape), "seq", partners(seq_devices, 1))
        return [Stream([(keep, at), (recv, at)], blocks) for at in (0, blocks)]

    mlp_streams = pair_streams(keep, send)

    half_seq = seq_devices // 2
    key_blocks = length * seq_devices // KEY_BLOCK
    stat_rows = -(-heads // 8) * 8

    def attention(first, count, after, before):
        kv_rows = pl.BlockSpec(
            (half_seq, 1, length + COUNT_ROWS, 2 * head_size), lambda r, *_: (0, first + r, 0, 0)
        )
        dkv_rows = pl.BlockSpec(
            (half_seq, 1, length, 2 * head_size), lambda r, *_: (0, first + r, 0, 0)
        )
        dkv_shape = jax.ShapeDtypeStruct((half_seq, row_count, length, 2 * head_size), BF)
        return pl.pallas_call(
            functools.partial(attention_kernel, heads, head_size, seq_devices, first),
            grid_spec=pltpu.PrefetchScalarGridSpec(
                num_scalar_prefetch=1,
                grid=(count,),
                in_specs=[
                    segments_spec, row_block((head_size, lanes), first),
                    row_block((head_size, lanes), first), kv_rows, kv_rows, turn_spec, turn_spec,
                ]
                + [pl.BlockSpec(memory_space=pl.ANY)] * len(before),
                out_specs=[column_block(first), column_block(first), dkv_rows, dkv_rows],
                scratch_shapes=[
                    pltpu.VMEM((key_blocks * KEY_BLOCK, 2 * head_size), BF),
                    pltpu.VMEM((key_blocks, 2 * head_size, KEY_BLOCK), BF),
                    pltpu.VMEM((KEY_BLOCK, length), F32),
                    pltpu.VMEM((key_blocks, KEY_BLOCK, lanes), BF),
                    pltpu.VMEM((KEY_BLOCK, lanes), BF),
                    pltpu.VMEM((head_size, lanes), BF),
                    pltpu.VMEM((head_size, lanes), F32),
                    pltpu.VMEM((head_size, lanes), F32),
                    pltpu.VMEM((key_blocks * KEY_BLOCK, 2 * head_size), BF),
                    pltpu.VMEM((stat_rows, length), F32),
                    pltpu.VMEM((stat_rows, length), F32),
                    pltpu.VMEM((stat_rows, length), F32),
                    pltpu.VMEM((key_blocks, stat_rows, length), F32),
                ],
            ),
            out_shape=[columns, columns, dkv_shape, dkv_shape],
            input_output_aliases={8 + j: j for j in range(len(before))},
            compiler_params=params(60),
            cost_estimate=cost(400 * count * length * length * width * 3, 8 * count * length * width),
        name="attention",
        )(
            ordered_after(where, *after), segment_ids, q_t, g_t, even, odd, cosine, sine, *before
        )

    first_rows = (row_count + 1) // 2
    results = attention(0, first_rows, [b_up_part], [])
    sends = reduce_level(
        mlp_streams, (bits[0], bits[-1]), seq_devices, where, [results[0]]
    )
    results = attention(first_rows, row_count - first_rows, [sends[0]], results)
    mix_t, qpg_t, dkv_keep, dkv_send = results
    dkv_recv = lax.ppermute(dkv_send, "seq", partners(seq_devices, 1))
    for level in range(1, len(bits)):
        sends = reduce_level(
            mlp_streams, (bits[level], bits[-1 - level]), seq_devices, where, [mix_t]
        )

    pair_spec = whole((2, half, width))
    pair_width = jax.ShapeDtypeStruct((2, half, width), BF)
    output, keep, send = pl.pallas_call(
        mix_kernel,
        grid_spec=pltpu.PrefetchScalarGridSpec(
            num_scalar_prefetch=1,
            grid=(row_count,),
            in_specs=[
                row_block((length, width)), segments_spec, column_block(), column_block(),
                column_block(), column_block(), token_block, whole((width, width)),
                width_spec, width_spec,
            ],
            out_specs=[row_block((length, width)), pair_spec, pair_spec],
            scratch_shapes=[pltpu.VMEM((width, width), F32), pltpu.VMEM((width, width), F32)],
        ),
        out_shape=[
            jax.ShapeDtypeStruct((row_count, length, width), BF), pair_width, pair_width,
        ],
        compiler_params=params(60),
        cost_estimate=cost(6 * token_count * width * width, 18 * token_count * width),
        name="mix",
    )(
        ordered_after(side, sends[0]), tokens, segment_ids, mix_t, qpg_t, attn_t, bg_t, mlp_out,
        w_out, b_out, b_down,
    )

    mix_streams = pair_streams(keep, send)
    dkv_recv, _ = lax.optimization_barrier((dkv_recv, keep))
    dkv_sum = dkv_keep.astype(F32) + dkv_recv.astype(F32)
    dkv_parts = [dkv_sum[0].astype(BF)]
    for j in range(1, half_seq):
        dkv_parts.append(
            lax.ppermute(dkv_sum[j].astype(BF), "seq", partners(seq_devices, 2 * j))
        )
    mlp_sends, mlp_received = reduce_along_batch(mlp_streams, batch_devices, where, [keep])

    dkv_count = len(dkv_parts)

    def exit_body(*refs):
        fixed, rest = refs[:15], refs[15:]
        exit_kernel(order_a, rows, permuted, *fixed, rest[:dkv_count], *rest[dkv_count:])

    if permuted:
        shuffle = jnp.zeros((8, LANES), F32)
    else:
        places = (jnp.array(order_a)[:, None] * rows + jnp.arange(rows)[None, :]).reshape(width, 1)
        shuffle = (places == jnp.arange(width)[None, :]).astype(F32)
    extra_spec = whole((half, 2 * LANES))
    extra_shape = jax.ShapeDtypeStruct((half, 2 * LANES), BF)
    tokens_grad, keep, send = pl.pallas_call(
        exit_body,
        grid_spec=pltpu.PrefetchScalarGridSpec(
            num_scalar_prefetch=1,
            grid=(row_count,),
            in_specs=[
                row_block((length, width)), row_block((length, width)), segments_spec,
                column_block(), column_block(), token_block, whole((width, width)),
                whole((width, 2 * head_size)), width_spec, width_spec, turn_spec, turn_spec,
                whole((hidden // width, width)), whole(shuffle.shape),
            ]
            + [row_block((length, 2 * head_size))] * dkv_count,
            out_specs=[row_block((length, width)), extra_spec, extra_spec],
            scratch_shapes=[
                pltpu.VMEM((width, 2 * head_size), F32), pltpu.VMEM((LANES, width), F32),
            ],
        ),
        out_shape=[
            jax.ShapeDtypeStruct((row_count, length, width), BF), extra_shape, extra_shape,
        ],
        compiler_params=params(60),
        cost_estimate=cost(2 * token_count * width * (width + 4 * head_size), 18 * token_count * width),
        name="exit",
    )(
        ordered_after(side, mlp_sends[0]), tokens, out_grad, segment_ids, qpg_t, attn_t, mlp_din, w_query, w_keyvalue,
        attn_gain, mlp_gain, cosine, sine, b_up_part.reshape(width, hidden // width).T, shuffle,
        *dkv_parts,
    )

    shape = (blocks, rows, 2 * LANES)
    keep = keep.reshape(shape)
    recv = lax.ppermute(send.reshape(shape), "seq", partners(seq_devices, 1))
    extra_streams = [Stream([(keep, 0), (recv, 0)], blocks)]
    for level in range(len(bits)):
        reduce_level(
            mix_streams, (bits[level], bits[-1 - level]), seq_devices, where,
            in_vmem=True, recv_in_vmem=True,
        )
        reduce_level(
            extra_streams, (bits[level],), seq_devices, where, in_vmem=True, recv_in_vmem=True
        )
    _, mix_received = reduce_along_batch(mix_streams, batch_devices, where)
    _, extra_received = reduce_along_batch(extra_streams, batch_devices, where)
    sums = own_sums(mlp_streams, mlp_received, where)
    sums += own_sums(mix_streams, mix_received, where)
    sums += own_sums(extra_streams, extra_received, where)
    w_up_grad, w_down_grad_t, w_query_grad, w_out_grad_t, extra = sums
    vectors = extra[:, LANES:]
    return (
        output,
        keyvalue,
        tokens_grad,
        vectors[:, 0],
        vectors[:, 1],
        vectors[:, 2],
        vectors[:, 3],
        w_query_grad,
        vectors[:, 4],
        extra[:, :LANES],
        w_out_grad_t.T,
        vectors[:, 5],
        w_up_grad,
        vectors[:, 8 : 8 + hidden // width].reshape(-1),
        w_down_grad_t.T,
        vectors[:, 5],
    )


def solution(mesh):
    row_spec = P("batch", "seq", None)
    split = P(("batch", "seq"))
    first = P(("batch", "seq"), None)
    last = P(None, ("batch", "seq"))
    return jax.shard_map(
        on_device,
        mesh=mesh,
        in_specs=(row_spec, P("batch", "seq")) + (P(),) * 13 + (row_spec,),
        out_specs=(
            row_spec, row_spec, row_spec, split, split, split, split, first, split, first, last,
            split, first, split, last, split,
        ),
        check_vma=False,
    )
```

```python
import functools
import math

import jax
import jax.numpy as jnp
from jax import lax
from jax.experimental import pallas as pl
from jax.experimental.pallas import tpu as pltpu
from jax.sharding import PartitionSpec as P

ROT_DIMS = 16
HALF_ROT = ROT_DIMS // 2
DOCS = 6
EPSILON = 1e-05
KEY_BLOCK = 256
COUNT_ROWS = 16
LANES = 128
NEGATIVE = -1e30
BF = jnp.bfloat16
F32 = jnp.float32
NN = (((1,), (0,)), ((), ()))
NT = (((1,), (1,)), ((), ()))
TN = (((0,), (0,)), ((), ()))


def matmul(left, right, dims=NN):
    return lax.dot_general(left, right, dims, preferred_element_type=F32)


def params(limit):
    return pltpu.CompilerParams(
        dimension_semantics=("arbitrary",), vmem_limit_bytes=limit * 1024 * 1024
    )


def cost(flops, size):
    return pl.CostEstimate(flops=int(flops), transcendentals=0, bytes_accessed=int(size))


def whole(shape):
    return pl.BlockSpec(shape, lambda *_: (0,) * len(shape))


def permute_rows(values, order, rows):
    return jnp.concatenate([values[b * rows : (b + 1) * rows] for b in order], axis=0)


def row_of(ref):
    return ref[...].astype(F32).reshape(1, ref.shape[0])


def valid_column(segment_row):
    length = segment_row.shape[-1]
    row = jnp.broadcast_to((segment_row >= 0).astype(F32), (LANES, length))
    return row.T[:, :1]


def norm_parts(values):
    center = values - jnp.mean(values, axis=-1, keepdims=True)
    spread = jnp.mean(center * center, axis=-1, keepdims=True)
    scale = lax.rsqrt(spread + EPSILON)
    return center * scale, scale


def turn(values, cosine, sine):
    leading = values[:HALF_ROT]
    trailing = values[HALF_ROT:ROT_DIMS]
    return jnp.concatenate(
        [leading * cosine - trailing * sine, trailing * cosine + leading * sine, values[ROT_DIMS:]],
        axis=0,
    )


def entry_kernel(
    head_size, order_a, order_b, rows, permuted,
    tok_ref, og_ref, seg_ref, ag_ref, as_ref, mg_ref, ms_ref, bq_ref, wq_ref, wkv_ref, wo_ref,
    cos_ref, sin_ref, mlp_ref, bg_ref, mlp_t_ref, bg_t_ref, attn_t_ref, q_t_ref, g_t_ref, kv_ref, pay_ref,
):
    x = tok_ref[0].astype(F32)
    length, width = x.shape
    n, _ = norm_parts(x)
    attn_in = (n * row_of(ag_ref) + row_of(as_ref)).astype(BF)
    mlp_in = (n * row_of(mg_ref) + row_of(ms_ref)).astype(BF)
    segments = seg_ref[pl.ds(pl.program_id(0), 1), :]
    bg = (og_ref[0].astype(F32) * valid_column(segments)).astype(BF)
    mlp_ref[...] = mlp_in
    bg_ref[...] = bg

    def turned(values, order):
        flipped = values.astype(F32).T
        if permuted:
            flipped = permute_rows(flipped, order, rows)
        return flipped.astype(BF)

    mlp_t_ref[...] = turned(mlp_in, order_a)
    attn_t_ref[...] = turned(attn_in, order_a)
    bg_t_ref[...] = turned(bg, order_b)

    cosine, sine = cos_ref[...], sin_ref[...]
    score_scale = 1.0 / math.sqrt(head_size)
    query_t = (matmul(attn_in, wq_ref[...]) + row_of(bq_ref)).T
    grad_t = matmul(wo_ref[...], bg, NT)
    for h in range(width // head_size):
        part = query_t[h * head_size : (h + 1) * head_size]
        q_t_ref[0, :, h * length : (h + 1) * length] = (
            turn(part, cosine, sine) * score_scale
        ).astype(BF)
        g_t_ref[0, :, h * length : (h + 1) * length] = grad_t[
            h * head_size : (h + 1) * head_size
        ].astype(BF)
    kv_t = matmul(attn_in, wkv_ref[...]).T
    kv = turn(kv_t, cosine, sine).T.astype(BF)
    kv_ref[0] = kv
    pay_ref[0, :length] = kv
    lane = lax.broadcasted_iota(jnp.int32, (1, LANES), 1)
    counts = jnp.zeros((1, LANES), F32)
    for c in range(DOCS):
        total = jnp.sum((segments == c).astype(F32), axis=1, keepdims=True)
        counts = counts + jnp.where(lane == c, total, 0.0)
    pay_ref[0, length:] = jnp.broadcast_to(counts, (COUNT_ROWS, LANES)).astype(BF)


def gelu_parts(hidden):
    cdf = 0.5 * (1.0 + lax.erf(hidden * math.sqrt(0.5)))
    bell = jnp.exp(-0.5 * (hidden * hidden)) * (1.0 / math.sqrt(2 * math.pi))
    return hidden * cdf, cdf + hidden * bell


def mlp_kernel(
    chunk, side_ref, mlp_ref, bg_ref, mlp_t_ref, bg_t_ref, up_ref, bup_ref, down_ref,
    keep_ref, send_ref, out_ref, din_ref, bupg_ref, act_s, hg_s,
):
    tokens, width = mlp_ref.shape

    @pl.when(pl.program_id(0) == 0)
    def _():
        out_ref[...] = jnp.zeros_like(out_ref)
        din_ref[...] = jnp.zeros_like(din_ref)

    bupg_ref[...] = jnp.zeros_like(bupg_ref)
    bias = bup_ref[...].astype(F32)

    def step(i, carry):
        at = pl.ds(pl.multiple_of(i * chunk, chunk), chunk)
        hidden = matmul(mlp_ref[at, :], up_ref[...]) + bias
        back = matmul(bg_ref[at, :], down_ref[...], NT)
        act, slope = gelu_parts(hidden)
        act = act.astype(BF)
        hg = (back * slope).astype(BF)
        act_s[at, :] = act
        hg_s[at, :] = hg
        bupg_ref[...] += jnp.sum(hg.astype(F32), axis=0, keepdims=True)
        out_ref[at, :] += matmul(act, down_ref[...])
        din_ref[at, :] += matmul(hg, up_ref[...], NT)
        return carry

    lax.fori_loop(0, tokens // chunk, step, 0)
    half = width // 2
    side = side_ref[0]
    mine = pl.ds(pl.multiple_of(side * half, half), half)
    other = pl.ds(pl.multiple_of((1 - side) * half, half), half)
    send_ref[0] = matmul(mlp_t_ref[other, :], hg_s[...]).astype(BF)
    send_ref[1] = matmul(bg_t_ref[other, :], act_s[...]).astype(BF)
    keep_ref[0] = matmul(mlp_t_ref[mine, :], hg_s[...]).astype(BF)
    keep_ref[1] = matmul(bg_t_ref[mine, :], act_s[...]).astype(BF)


def attention_kernel(
    heads, head_size, seq_devices, first_row, where_ref, seg_ref, q_t_ref, g_t_ref, even_ref,
    odd_ref, cos_ref, sin_ref, *refs,
):
    (mix_t_ref, qpg_t_ref, dkeep_ref, dsend_ref, kv_s, kv_t_s, bias_s, p_s, ds_s, gk_s, o_s, dq_s,
     dkv_s, m_s, l_s, d_s, mk_s) = refs[-17:]
    length = seg_ref.shape[-1]
    me = where_ref[0]
    start = me * length
    group = math.gcd(heads, 3)

    def columns(h, count=1):
        return slice(h * length, (h + count) * length)

    def head(h):
        return slice(h * head_size, (h + 1) * head_size)

    counts = jnp.zeros((1, LANES), F32)
    for m in range(seq_devices):
        ref = (even_ref, odd_ref)[m % 2]
        at = pl.multiple_of((me ^ m) * length, length)
        kv_s[pl.ds(at, length), :] = ref[m // 2, 0, :length]
        counts = counts + ref[m // 2, 0, length : length + COUNT_ROWS].astype(F32)[:1]

    segments = seg_ref[pl.ds(first_row + pl.program_id(0), 1), :]
    low = jnp.zeros((1, length), F32)
    for c in range(DOCS):
        later = (segments > c) | (segments < 0)
        low = low + jnp.where(later, counts[:, c : c + 1], 0.0)
    low = low.astype(jnp.int32)
    first_block = jnp.min(low) // KEY_BLOCK
    end_block = (start + length - 1) // KEY_BLOCK + 1
    place = start + lax.broadcasted_iota(jnp.int32, (1, length), 1)

    m_s[...] = jnp.full_like(m_s, NEGATIVE)
    l_s[...] = jnp.zeros_like(l_s)
    o_s[...] = jnp.zeros_like(o_s)
    dq_s[...] = jnp.zeros_like(dq_s)
    dkv_s[...] = jnp.zeros_like(dkv_s)

    def forward(b, carry):
        at = pl.multiple_of(b * KEY_BLOCK, KEY_BLOCK)
        kv = kv_s[pl.ds(at, KEY_BLOCK), :]
        keys = kv[:, :head_size]
        kv_t = kv.astype(F32).T.astype(BF)
        kv_t_s[b] = kv_t
        summed = jnp.concatenate([kv_t[head_size:], jnp.ones((16, KEY_BLOCK), BF)], axis=0)
        key_place = at + lax.broadcasted_iota(jnp.int32, (KEY_BLOCK, length), 0)
        allowed = (key_place <= place) & (key_place >= low)
        bias_s[...] = jnp.where(allowed, 0.0, NEGATIVE)
        bias = bias_s[...]
        shrinks = {}

        def scores(h):
            return matmul(keys, q_t_ref[0, :, columns(h, group)])

        def mix(h):
            o = matmul(summed, p_s[b, :, columns(h, group)])
            for j in range(group):
                row = slice(h + j, h + j + 1)
                part = o[:, columns(j)]
                shrink = shrinks.pop(h + j)
                o_s[:, columns(h + j)] = o_s[:, columns(h + j)] * shrink + part[:head_size]
                l_s[row, :] = l_s[row, :] * shrink + part[head_size : head_size + 1]

        ready = scores(0)
        for h in range(0, heads, group):
            now_scores = ready
            if h + group < heads:
                ready = scores(h + group)
            for j in range(group):
                row = slice(h + j, h + j + 1)
                s = now_scores[:, columns(j)] + bias
                before = m_s[row, :]
                now = jnp.maximum(before, jnp.max(s, axis=0, keepdims=True))
                p_s[b, :, columns(h + j)] = jnp.exp(s - now).astype(BF)
                shrinks[h + j] = jnp.exp(before - now)
                m_s[row, :] = now
                mk_s[b, row, :] = now
            if h > 0:
                mix(h - group)
        mix(heads - group)
        return carry

    lax.fori_loop(first_block, end_block, forward, 0)

    for h in range(heads):
        row = slice(h, h + 1)
        inverse = 1.0 / l_s[row, :]
        mixed = o_s[:, columns(h)] * inverse
        mix_t_ref[head(h), :] = mixed.astype(BF)
        d_s[row, :] = jnp.sum(
            mixed * g_t_ref[0, :, columns(h)].astype(F32), axis=0, keepdims=True
        )
        l_s[row, :] = inverse

    def backward(b, carry):
        at = pl.multiple_of(b * KEY_BLOCK, KEY_BLOCK)
        values = kv_s[pl.ds(at, KEY_BLOCK), :][:, head_size:]
        keys_t = kv_t_s[b][:head_size]
        inners = {}

        def prob_grads(h):
            for j in range(group):
                row = slice(h + j, h + j + 1)
                factor = jnp.exp(mk_s[b, row, :] - m_s[row, :]) * l_s[row, :]
                scaled = g_t_ref[0, :, columns(h + j)].astype(F32) * factor
                gk_s[:, columns(h + j)] = scaled.astype(BF)
                inners[h + j] = d_s[row, :] * factor
            return matmul(values, gk_s[:, columns(h, group)])

        ready = prob_grads(0)
        for h in range(0, heads, group):
            now_grads = ready
            if h + group < heads:
                ready = prob_grads(h + group)
            for j in range(group):
                p = p_s[b, :, columns(h + j)].astype(F32)
                ds_s[:, columns(h + j)] = (
                    p * (now_grads[:, columns(j)] - inners.pop(h + j))
                ).astype(BF)
        dq_s[...] += matmul(keys_t, ds_s[...])
        dk = matmul(ds_s[...], q_t_ref[0], NT)
        dv = matmul(p_s[b], gk_s[...], NT)
        dkv_s[pl.ds(at, KEY_BLOCK), :] = jnp.concatenate([dk, dv], axis=1).astype(BF)
        return carry

    lax.fori_loop(first_block, end_block, backward, 0)

    cosine, sine = cos_ref[...], sin_ref[...]
    score_scale = 1.0 / math.sqrt(head_size)
    for h in range(heads):
        qpg_t_ref[head(h), :] = turn(
            dq_s[:, columns(h)] * score_scale, cosine, -sine
        ).astype(BF)
    for m in range(seq_devices):
        ref = (dkeep_ref, dsend_ref)[m % 2]
        at = pl.multiple_of((me ^ m) * length, length)
        ref[m // 2, 0] = dkv_s[pl.ds(at, length), :]


def weights_kernel(
    side_ref, mix_t_ref, qpg_t_ref, attn_t_ref, bg_t_ref, keep_ref, send_ref, acc_q, acc_o,
):
    step, steps = pl.program_id(0), pl.num_programs(0)

    @pl.when(step == 0)
    def _():
        acc_q[...] = jnp.zeros_like(acc_q)
        acc_o[...] = jnp.zeros_like(acc_o)

    acc_q[...] += matmul(attn_t_ref[...], qpg_t_ref[...], NT)
    acc_o[...] += matmul(bg_t_ref[...], mix_t_ref[...], NT)

    @pl.when(step == steps - 1)
    def _():
        half = acc_q.shape[0] // 2
        side = side_ref[0]
        mine = pl.ds(pl.multiple_of(side * half, half), half)
        other = pl.ds(pl.multiple_of((1 - side) * half, half), half)
        for j, acc in enumerate((acc_q, acc_o)):
            keep_ref[j] = acc[mine, :].astype(BF)
            send_ref[j] = acc[other, :].astype(BF)


def output_kernel(
    where_ref, tok_ref, seg_ref, mix_t_ref, mlp_ref, wo_ref, bo_ref, bd_ref, out_ref
):
    branch = matmul(mix_t_ref[...], wo_ref[...], TN) + (row_of(bo_ref) + row_of(bd_ref))
    valid = valid_column(seg_ref[pl.ds(pl.program_id(0), 1), :])
    out_ref[0] = (tok_ref[0].astype(F32) + valid * (branch + mlp_ref[...])).astype(BF)


def exit_kernel(
    order_a, rows, permuted,
    side_ref, tok_ref, og_ref, seg_ref, qpg_t_ref, attn_t_ref, din_ref, wq_ref, wkv_ref,
    ag_ref, mg_ref, cos_ref, sin_ref, bupg_ref, shuffle_ref, dkv_refs,
    tg_ref, keep_ref, send_ref, acc, vec,
):
    step, steps = pl.program_id(0), pl.num_programs(0)

    @pl.when(step == 0)
    def _():
        acc[...] = jnp.zeros_like(acc)
        vec[...] = jnp.zeros_like(vec)

    dkv = sum((ref[0].astype(F32) for ref in dkv_refs[1:]), dkv_refs[0][0].astype(F32))
    kvpg_t = turn(dkv.T, cos_ref[...], -sin_ref[...]).astype(BF)
    acc[...] += matmul(attn_t_ref[...], kvpg_t, NT)
    qpg_t = qpg_t_ref[...]
    d_attn = (matmul(wq_ref[...], qpg_t) + matmul(wkv_ref[...], kvpg_t)).T
    d_mlp = din_ref[...]
    n, scale = norm_parts(tok_ref[0].astype(F32))
    og = og_ref[0].astype(F32)
    e = d_attn * row_of(ag_ref) + d_mlp * row_of(mg_ref)
    inner = jnp.mean(e * n, axis=-1, keepdims=True)
    tg_ref[0] = (og + scale * (e - jnp.mean(e, axis=-1, keepdims=True) - n * inner)).astype(BF)
    ones = jnp.ones((8, qpg_t.shape[1]), BF)
    bg = (og * valid_column(seg_ref[pl.ds(step, 1), :])).astype(BF)
    sums = [d_attn * n, d_attn, d_mlp * n, d_mlp, None, bg.astype(F32)]
    for j, value in enumerate(sums):
        if value is None:
            part = matmul(ones, qpg_t, NT)[:1]
        else:
            part = jnp.sum(value, axis=0, keepdims=True)
        vec[j : j + 1, :] += part

    @pl.when(step == steps - 1)
    def _():
        vec[8:12, :] = bupg_ref[...]
        if permuted:
            columns = permute_rows(vec[...].T, order_a, rows)
        else:
            columns = lax.dot_general(
                shuffle_ref[...], vec[...], NT, precision=lax.Precision.HIGHEST,
                preferred_element_type=F32,
            )
        half = columns.shape[0] // 2
        acc_columns = slice(0, LANES)
        vec_columns = slice(LANES, 2 * LANES)
        for side in range(2):

            @pl.when(side_ref[0] == side)
            def _():
                mine = slice(side * half, (side + 1) * half)
                other = slice((1 - side) * half, (2 - side) * half)
                keep_ref[:, acc_columns] = acc[mine, :].astype(BF)
                send_ref[:, acc_columns] = acc[other, :].astype(BF)
                keep_ref[:, vec_columns] = columns[mine].astype(BF)
                send_ref[:, vec_columns] = columns[other].astype(BF)


def partners(size, mask):
    return [(i, i ^ mask) for i in range(size)]


class Stream:
    def __init__(self, arrays, count, resident, width):
        self.terms = [(array, resident, 0, at, ()) for array, at in arrays]
        self.count, self.resident, self.width = count, resident, width
        self.rows = arrays[0][0].shape[1]

    def halve(self, bit):
        count = self.count = self.count // 2
        mine, other = [], []
        for array, resident, column, at, adds in self.terms:
            mine.append((array, resident, column, at, adds + ((bit, count),)))
            other.append((array, resident, column, at + count, adds + ((bit, -count),)))
        self.terms = mine
        return other


def first_block(term, where_ref):
    at = term[3]
    for (axis, bit), weight in term[4]:
        at = at + ((where_ref[axis] >> bit) & 1) * weight
    return at


def term_spec(term, width, group):
    if term[1]:
        return pl.BlockSpec(memory_space=pltpu.VMEM)
    return pl.BlockSpec(
        (group, term[0].shape[1], width),
        lambda i, where_ref: (first_block(term, where_ref) // group + i, 0, term[2]),
    )


def in_hbm(value):
    return pltpu.with_memory_space_constraint(value, pltpu.HBM)


def operands_of(terms):
    return [term[0] if term[1] else in_hbm(term[0]) for term in terms]


def read_terms(terms, refs, width, group, where_ref):
    total = None
    for term, ref in zip(terms, refs):
        if term[1]:
            at = first_block(term, where_ref) + pl.program_id(0) * group
            value = ref[pl.ds(at, group), :, term[2] * width : (term[2] + 1) * width]
        else:
            value = ref[...]
        value = value.astype(F32)
        total = value if total is None else total + value
    return total


def call_on_terms(body, name, where, after, steps, in_specs, operands, out_specs, out_shape, size):
    return pl.pallas_call(
        body,
        grid_spec=pltpu.PrefetchScalarGridSpec(
            num_scalar_prefetch=1, grid=(steps,), in_specs=in_specs, out_specs=out_specs
        ),
        out_shape=out_shape,
        compiler_params=params(limit=24),
        cost_estimate=cost(0, size),
        name=name,
    )(ordered_after(where, *after), *operands)


def sums_to_send(picks, streams, joined, where, after):
    count, width, rows = streams[0].count, streams[0].width, streams[0].rows
    resident = streams[0].resident
    group = count
    while group > 1 and group * width > 4 * 3072 and not resident:
        group //= 2
    terms = [term for pick in picks for term in pick]
    outputs = 1 if joined else len(picks)
    shape = (rows, width * len(picks) // outputs)

    def body(where_ref, *refs):
        at = 0
        for j, pick in enumerate(picks):
            total = read_terms(pick, refs[at : at + len(pick)], width, group, where_ref).astype(BF)
            if joined:
                refs[-1][:, :, j * width : (j + 1) * width] = total
            else:
                refs[len(terms) + j][...] = total
            at += len(pick)

    if resident:
        out_spec = pl.BlockSpec(memory_space=pltpu.VMEM)
    else:
        out_spec = pl.BlockSpec((group,) + shape, lambda i, _: (i, 0, 0))
    return call_on_terms(
        body, "combine", where, after, count // group,
        [term_spec(term, width, group) for term in terms],
        operands_of(terms),
        [out_spec] * outputs,
        [jax.ShapeDtypeStruct((count,) + shape, BF)] * outputs,
        2 * count * rows * width * len(terms),
    )


def own_sums(streams, where, after=()):
    terms = [term for stream in streams for term in stream.terms]

    def body(where_ref, *refs):
        at = 0
        for stream, output in zip(streams, refs[len(terms) :]):
            size = len(stream.terms)
            output[...] = read_terms(
                stream.terms, refs[at : at + size], stream.width, 1, where_ref
            )[0]
            at += size

    return call_on_terms(
        body, "own", where, after, 1,
        [term_spec(term, stream.width, 1) for stream in streams for term in stream.terms],
        operands_of(terms),
        [whole((stream.rows, stream.width)) for stream in streams],
        [jax.ShapeDtypeStruct((stream.rows, stream.width), F32) for stream in streams],
        2 * len(terms) * streams[0].rows * streams[0].width,
    )


def ordered_after(value, *others):
    if not others:
        return value
    return lax.optimization_barrier((value, others))[0]


AXES = ("seq", "batch")


def reduce_level(streams, bits, where, after=()):
    picks = [stream.halve(bit) for stream, bit in zip(streams, bits)]
    joined = len(set(bits)) == 1
    sends = sums_to_send(picks, streams, joined, where, after)
    recvs = []
    for (axis, bit), send in zip(bits, sends):
        recvs.append(
            lax.ppermute(send, AXES[axis], partners(lax.axis_size(AXES[axis]), 1 << bit))
        )
    for j, stream in enumerate(streams):
        column = j if joined else 0
        stream.terms.append((recvs[0 if joined else j], stream.resident, column, 0, ()))
    return sends, recvs


def on_device(
    tokens, segment_ids, attn_gain, attn_shift, mlp_gain, mlp_shift, w_query, b_query,
    w_keyvalue, w_out, b_out, w_up, b_up, w_down, b_down, out_grad,
):
    row_count, length, width = tokens.shape
    head_size = w_keyvalue.shape[1] // 2
    heads = width // head_size
    hidden = w_up.shape[1]
    token_count = row_count * length
    seq_devices = lax.axis_size("seq")
    batch_devices = lax.axis_size("batch")
    devices = seq_devices * batch_devices
    seq_index = lax.axis_index("seq").astype(jnp.int32)
    batch_index = lax.axis_index("batch").astype(jnp.int32)
    side = (seq_index & 1).reshape(1)
    where = jnp.stack([seq_index, batch_index])
    rows = width // devices
    permuted = rows % 8 == 0
    seq_bits = list(range(seq_devices.bit_length() - 1))

    def reversed_bits(value, count):
        return sum(((value >> j) & 1) << (count - 1 - j) for j in range(count))

    batch_order = [
        reversed_bits(z, batch_devices.bit_length() - 1) for z in range(batch_devices)
    ]

    def device_order(bits):
        order = []
        for k in range(seq_devices):
            at = 0
            for j, bit in enumerate(bits):
                at |= ((k >> (len(bits) - 1 - j)) & 1) << bit
            order += [z * seq_devices + at for z in batch_order]
        return order

    order_a = device_order(seq_bits)
    order_b = device_order(seq_bits[:1] + seq_bits[:0:-1])

    def ordered(values, order):
        if permuted:
            return values
        shaped = values.reshape(values.shape[:-2] + (devices, rows, values.shape[-1]))
        return jnp.take(shaped, jnp.array(order), axis=-3).reshape(values.shape)

    positions = (seq_index * length + jnp.arange(length)).astype(F32)
    inverse = 10000.0 ** (-(jnp.arange(HALF_ROT).astype(F32) * (2.0 / ROT_DIMS)))
    angles = inverse[:, None] * positions[None, :]
    cosine, sine = jnp.cos(angles), jnp.sin(angles)
    segments_spec = whole((row_count, length))
    turn_spec = whole((HALF_ROT, length))
    width_spec = whole((width,))

    def row_block(shape, first=0):
        return pl.BlockSpec((1,) + shape, lambda r, *_: (first + r, 0, 0))

    token_block = pl.BlockSpec((length, width), lambda r, *_: (r, 0))
    whole_lanes = length % LANES == 0

    def column_block(first=0):
        if whole_lanes:
            return pl.BlockSpec((width, length), lambda r, *_: (0, first + r))
        return pl.BlockSpec((None, width, length), lambda r, *_: (first + r, 0, 0))

    columns = jax.ShapeDtypeStruct(
        (width, token_count) if whole_lanes else (row_count, width, length), BF
    )

    def joined(values):
        if whole_lanes:
            return values
        return jnp.transpose(values, (1, 0, 2)).reshape(width, token_count)

    lanes = heads * length
    mlp_in, bg, mlp_t, bg_t, attn_t, q_t, g_t, keyvalue, payload = pl.pallas_call(
        functools.partial(entry_kernel, head_size, order_a, order_b, rows, permuted),
        grid=(row_count,),
        in_specs=[
            row_block((length, width)), row_block((length, width)), segments_spec,
            width_spec, width_spec, width_spec, width_spec, width_spec,
            whole((width, width)), whole((width, 2 * head_size)), whole((width, width)),
            turn_spec, turn_spec,
        ],
        out_specs=[
            token_block, token_block, column_block(), column_block(), column_block(),
            row_block((head_size, lanes)), row_block((head_size, lanes)),
            row_block((length, 2 * head_size)), row_block((length + COUNT_ROWS, 2 * head_size)),
        ],
        out_shape=[
            jax.ShapeDtypeStruct((token_count, width), BF),
            jax.ShapeDtypeStruct((token_count, width), BF),
            columns,
            columns,
            columns,
            jax.ShapeDtypeStruct((row_count, head_size, lanes), BF),
            jax.ShapeDtypeStruct((row_count, head_size, lanes), BF),
            jax.ShapeDtypeStruct((row_count, length, 2 * head_size), BF),
            jax.ShapeDtypeStruct((row_count, length + COUNT_ROWS, 2 * head_size), BF),
        ],
        compiler_params=params(60),
        cost_estimate=cost(2 * token_count * width * (2 * width + 2 * head_size), 20 * token_count * width),
        name="entry",
    )(
        tokens, out_grad, segment_ids, attn_gain, attn_shift, mlp_gain, mlp_shift, b_query,
        w_query, w_keyvalue, w_out, cosine, sine,
    )
    mlp_t, attn_t = ordered(mlp_t, order_a), ordered(attn_t, order_a)
    bg_t = ordered(bg_t, order_b)

    gathered = [payload]
    for mask in range(2, seq_devices, 2):
        gathered.append(lax.ppermute(payload, "seq", partners(seq_devices, mask)))

    tile = math.gcd(512, hidden)
    half = width // 2
    pair_cols = pl.BlockSpec((2, half, tile), lambda f, *_: (0, 0, f))
    pair_shape = jax.ShapeDtypeStruct((2, half, hidden), BF)
    keep, send, mlp_out, mlp_din, b_up_part = pl.pallas_call(
        functools.partial(mlp_kernel, token_count),
        grid_spec=pltpu.PrefetchScalarGridSpec(
            num_scalar_prefetch=1,
            grid=(hidden // tile,),
            in_specs=[
                whole((token_count, width)), whole((token_count, width)),
                whole((width, token_count)), whole((width, token_count)),
                pl.BlockSpec((width, tile), lambda f, *_: (0, f)),
                pl.BlockSpec((1, tile), lambda f, *_: (0, f)),
                pl.BlockSpec((tile, width), lambda f, *_: (f, 0)),
            ],
            out_specs=[
                pair_cols, pair_cols, whole((token_count, width)), whole((token_count, width)),
                pl.BlockSpec((1, tile), lambda f, *_: (0, f)),
            ],
            scratch_shapes=[
                pltpu.VMEM((token_count, tile), BF), pltpu.VMEM((token_count, tile), BF),
            ],
        ),
        out_shape=[
            pair_shape, pair_shape,
            jax.ShapeDtypeStruct((token_count, width), F32),
            jax.ShapeDtypeStruct((token_count, width), F32),
            jax.ShapeDtypeStruct((1, hidden), F32),
        ],
        compiler_params=params(60),
        cost_estimate=cost(12 * token_count * width * hidden, 40 * token_count * width),
        name="mlp",
    )(side, mlp_in, bg, joined(mlp_t), joined(bg_t), w_up, b_up.reshape(1, hidden), w_down)

    even = jnp.stack(ordered_after(tuple(gathered), b_up_part))
    odd = lax.ppermute(even, "seq", partners(seq_devices, 1))

    bits = [(0, bit) for bit in range(1, seq_devices.bit_length() - 1)]
    batch_bits = [(1, bit) for bit in range(batch_devices.bit_length() - 1)]
    blocks = devices // 2

    def pair_streams(keep, send, resident):
        shape = (2 * blocks, rows, keep.shape[2])
        keep = keep.reshape(shape)
        recv = lax.ppermute(send.reshape(shape), "seq", partners(seq_devices, 1))
        return [
            Stream([(keep, at), (recv, at)], blocks, resident, keep.shape[2])
            for at in (0, blocks)
        ]

    mlp_streams = pair_streams(keep, send, False)

    half_seq = seq_devices // 2
    key_blocks = length * seq_devices // KEY_BLOCK
    stat_rows = -(-heads // 8) * 8

    def attention(first, count, after, before):
        kv_rows = pl.BlockSpec(
            (half_seq, 1, length + COUNT_ROWS, 2 * head_size), lambda r, *_: (0, first + r, 0, 0)
        )
        dkv_rows = pl.BlockSpec(
            (half_seq, 1, length, 2 * head_size), lambda r, *_: (0, first + r, 0, 0)
        )
        dkv_shape = jax.ShapeDtypeStruct((half_seq, row_count, length, 2 * head_size), BF)
        return pl.pallas_call(
            functools.partial(attention_kernel, heads, head_size, seq_devices, first),
            grid_spec=pltpu.PrefetchScalarGridSpec(
                num_scalar_prefetch=1,
                grid=(count,),
                in_specs=[
                    segments_spec, row_block((head_size, lanes), first),
                    row_block((head_size, lanes), first), kv_rows, kv_rows, turn_spec, turn_spec,
                ]
                + [pl.BlockSpec(memory_space=pl.ANY)] * len(before),
                out_specs=[column_block(first), column_block(first), dkv_rows, dkv_rows],
                scratch_shapes=[
                    pltpu.VMEM((key_blocks * KEY_BLOCK, 2 * head_size), BF),
                    pltpu.VMEM((key_blocks, 2 * head_size, KEY_BLOCK), BF),
                    pltpu.VMEM((KEY_BLOCK, length), F32),
                    pltpu.VMEM((key_blocks, KEY_BLOCK, lanes), BF),
                    pltpu.VMEM((KEY_BLOCK, lanes), BF),
                    pltpu.VMEM((head_size, lanes), BF),
                    pltpu.VMEM((head_size, lanes), F32),
                    pltpu.VMEM((head_size, lanes), F32),
                    pltpu.VMEM((key_blocks * KEY_BLOCK, 2 * head_size), BF),
                    pltpu.VMEM((stat_rows, length), F32),
                    pltpu.VMEM((stat_rows, length), F32),
                    pltpu.VMEM((stat_rows, length), F32),
                    pltpu.VMEM((key_blocks, stat_rows, length), F32),
                ],
            ),
            out_shape=[columns, columns, dkv_shape, dkv_shape],
            input_output_aliases={8 + j: j for j in range(len(before))},
            compiler_params=params(60),
            cost_estimate=cost(400 * count * length * length * width * 3, 8 * count * length * width),
        name="attention",
        )(
            ordered_after(where, *after), segment_ids, q_t, g_t, in_hbm(even), in_hbm(odd), cosine,
            sine, *before,
        )

    pair_levels = [(bits[i], bits[-1 - i]) for i in range(len(bits))]
    batch_levels = [(bit, bit) for bit in batch_bits]
    mlp_levels = iter(pair_levels + batch_levels)
    calls = min(len(bits) + 1, row_count)
    shares = [row_count // calls + (calls // 2 == i) * (row_count % calls) for i in range(calls)]
    results, after, first_row = [], [b_up_part], 0
    for i, share in enumerate(shares):
        results = attention(first_row, share, after, results)
        first_row += share
        after, mlp_recv = reduce_level(mlp_streams, next(mlp_levels), where, [results[0]])
    mix_t, qpg_t, dkv_keep, dkv_send = results
    dkv_recv = lax.ppermute(dkv_send, "seq", partners(seq_devices, 1))

    pair_spec = whole((2, half, width))
    pair_width = jax.ShapeDtypeStruct((2, half, width), BF)
    keep, send = pl.pallas_call(
        weights_kernel,
        grid_spec=pltpu.PrefetchScalarGridSpec(
            num_scalar_prefetch=1,
            grid=(row_count,),
            in_specs=[column_block()] * 4,
            out_specs=[pair_spec, pair_spec],
            scratch_shapes=[pltpu.VMEM((width, width), F32), pltpu.VMEM((width, width), F32)],
        ),
        out_shape=[pair_width, pair_width],
        compiler_params=params(60),
        cost_estimate=cost(4 * token_count * width * width, 8 * token_count * width),
        name="weights",
    )(ordered_after(side, *after), mix_t, qpg_t, attn_t, bg_t)
    mix_streams = pair_streams(keep, send, True)

    dkv_recv = ordered_after(dkv_recv, keep)
    dkv_sum = dkv_keep.astype(F32) + dkv_recv.astype(F32)
    dkv_low = dkv_sum.astype(BF)
    dkv_parts = [dkv_low[0]]
    for j in range(1, half_seq):
        dkv_parts.append(lax.ppermute(dkv_low[j], "seq", partners(seq_devices, 2 * j)))
    mix_levels = iter(pair_levels + batch_levels)
    after, _ = reduce_level(mix_streams, next(mix_levels), where, [dkv_parts[0], *mlp_recv])

    output = pl.pallas_call(
        output_kernel,
        grid_spec=pltpu.PrefetchScalarGridSpec(
            num_scalar_prefetch=1,
            grid=(row_count,),
            in_specs=[
                row_block((length, width)), segments_spec, column_block(), token_block,
                whole((width, width)), width_spec, width_spec,
            ],
            out_specs=row_block((length, width)),
        ),
        out_shape=jax.ShapeDtypeStruct((row_count, length, width), BF),
        compiler_params=params(60),
        cost_estimate=cost(2 * token_count * width * width, 10 * token_count * width),
        name="output",
    )(ordered_after(where, *after), tokens, segment_ids, mix_t, mlp_out, w_out, b_out, b_down)

    after = []
    for level in mlp_levels:
        after, mlp_recv = reduce_level(mlp_streams, level, where, [output])

    dkv_count = len(dkv_parts)

    def exit_body(*refs):
        fixed, rest = refs[:15], refs[15:]
        exit_kernel(order_a, rows, permuted, *fixed, rest[:dkv_count], *rest[dkv_count:])

    if permuted:
        shuffle = jnp.zeros((8, LANES), F32)
    else:
        places = (jnp.array(order_a)[:, None] * rows + jnp.arange(rows)[None, :]).reshape(width, 1)
        shuffle = (places == jnp.arange(width)[None, :]).astype(F32)
    extra_spec = whole((half, 2 * LANES))
    extra_shape = jax.ShapeDtypeStruct((half, 2 * LANES), BF)
    tokens_grad, keep, send = pl.pallas_call(
        exit_body,
        grid_spec=pltpu.PrefetchScalarGridSpec(
            num_scalar_prefetch=1,
            grid=(row_count,),
            in_specs=[
                row_block((length, width)), row_block((length, width)), segments_spec,
                column_block(), column_block(), token_block, whole((width, width)),
                whole((width, 2 * head_size)), width_spec, width_spec, turn_spec, turn_spec,
                whole((hidden // width, width)), whole(shuffle.shape),
            ]
            + [row_block((length, 2 * head_size))] * dkv_count,
            out_specs=[row_block((length, width)), extra_spec, extra_spec],
            scratch_shapes=[
                pltpu.VMEM((width, 2 * head_size), F32), pltpu.VMEM((LANES, width), F32),
            ],
        ),
        out_shape=[
            jax.ShapeDtypeStruct((row_count, length, width), BF), extra_shape, extra_shape,
        ],
        compiler_params=params(60),
        cost_estimate=cost(2 * token_count * width * (width + 4 * head_size), 18 * token_count * width),
        name="exit",
    )(
        ordered_after(side, output, *after), tokens, out_grad, segment_ids, qpg_t, attn_t, mlp_din, w_query, w_keyvalue,
        attn_gain, mlp_gain, cosine, sine, b_up_part.reshape(width, hidden // width).T, shuffle,
        *dkv_parts,
    )

    shape = (blocks, rows, 2 * LANES)
    keep = keep.reshape(shape)
    recv = lax.ppermute(send.reshape(shape), "seq", partners(seq_devices, 1))
    extra_streams = [Stream([(keep, 0), (recv, 0)], blocks, True, 2 * LANES)]
    extra_levels = [(bit,) for bit in bits + batch_bits]
    mlp_sums = own_sums(mlp_streams, where, [keep])
    after = mlp_sums[:1]
    for level in extra_levels:
        reduce_level(extra_streams, level, where, after)
        after = []
        level = next(mix_levels, None)
        if level:
            reduce_level(mix_streams, level, where)
    sums = mlp_sums + own_sums(mix_streams, where) + own_sums(extra_streams, where)
    w_up_grad, w_down_grad_t, w_query_grad, w_out_grad_t, extra = sums
    vectors = extra[:, LANES:]
    return (
        output,
        keyvalue,
        tokens_grad,
        vectors[:, 0],
        vectors[:, 1],
        vectors[:, 2],
        vectors[:, 3],
        w_query_grad,
        vectors[:, 4],
        extra[:, :LANES],
        w_out_grad_t.T,
        vectors[:, 5],
        w_up_grad,
        vectors[:, 8 : 8 + hidden // width].reshape(-1),
        w_down_grad_t.T,
        vectors[:, 5],
    )


def solution(mesh):
    row_spec = P("batch", "seq", None)
    split = P(("batch", "seq"))
    first = P(("batch", "seq"), None)
    last = P(None, ("batch", "seq"))
    return jax.shard_map(
        on_device,
        mesh=mesh,
        in_specs=(row_spec, P("batch", "seq")) + (P(),) * 13 + (row_spec,),
        out_specs=(
            row_spec, row_spec, row_spec, split, split, split, split, first, split, first, last,
            split, first, split, last, split,
        ),
        check_vma=False,
    )
```

```python
import functools
import math

import jax
import jax.numpy as jnp
from jax import lax
from jax.experimental import pallas as pl
from jax.experimental.pallas import tpu as pltpu
from jax.sharding import PartitionSpec as P

ROT_DIMS = 16
HALF_ROT = ROT_DIMS // 2
DOCS = 6
EPSILON = 1e-05
KEY_BLOCK = 256
COUNT_ROWS = 16
LANES = 128
NEGATIVE = -1e30
BF = jnp.bfloat16
F32 = jnp.float32
NN = (((1,), (0,)), ((), ()))
NT = (((1,), (1,)), ((), ()))
TN = (((0,), (0,)), ((), ()))


def matmul(left, right, dims=NN):
    return lax.dot_general(left, right, dims, preferred_element_type=F32)


def params(limit):
    return pltpu.CompilerParams(
        dimension_semantics=("arbitrary",), vmem_limit_bytes=limit * 1024 * 1024
    )


LONG = pl.CostEstimate(flops=4 * 10**10, transcendentals=0, bytes_accessed=10**7)


def short(size):
    return pl.CostEstimate(flops=0, transcendentals=0, bytes_accessed=size)


def whole(shape):
    return pl.BlockSpec(shape, lambda *_: (0,) * len(shape))


def permute_rows(values, order, rows):
    return jnp.concatenate([values[b * rows : (b + 1) * rows] for b in order], axis=0)


def row_of(ref):
    return ref[...].astype(F32).reshape(1, ref.shape[0])


def valid_column(segment_row):
    length = segment_row.shape[-1]
    row = jnp.broadcast_to((segment_row >= 0).astype(F32), (LANES, length))
    return row.T[:, :1]


def norm_parts(values):
    center = values - jnp.mean(values, axis=-1, keepdims=True)
    spread = jnp.mean(center * center, axis=-1, keepdims=True)
    scale = lax.rsqrt(spread + EPSILON)
    return center * scale, scale


def turn(values, cosine, sine):
    leading = values[:HALF_ROT]
    trailing = values[HALF_ROT:ROT_DIMS]
    return jnp.concatenate(
        [leading * cosine - trailing * sine, trailing * cosine + leading * sine, values[ROT_DIMS:]],
        axis=0,
    )


def entry_kernel(
    head_size, order_a, order_b, rows, permuted,
    tok_ref, og_ref, seg_ref, ag_ref, as_ref, mg_ref, ms_ref, bq_ref, wq_ref, wkv_ref, wo_ref,
    cos_ref, sin_ref, mlp_ref, bg_ref, mlp_t_ref, bg_t_ref, attn_t_ref, q_t_ref, g_t_ref, kv_ref, pay_ref,
):
    x = tok_ref[0].astype(F32)
    length, width = x.shape
    n, _ = norm_parts(x)
    attn_in = (n * row_of(ag_ref) + row_of(as_ref)).astype(BF)
    mlp_in = (n * row_of(mg_ref) + row_of(ms_ref)).astype(BF)
    segments = seg_ref[pl.ds(pl.program_id(0), 1), :]
    bg = (og_ref[0].astype(F32) * valid_column(segments)).astype(BF)
    mlp_ref[...] = mlp_in
    bg_ref[...] = bg

    def turned(values, order):
        flipped = values.astype(F32).T
        if permuted:
            flipped = permute_rows(flipped, order, rows)
        return flipped.astype(BF)

    mlp_t_ref[...] = turned(mlp_in, order_a)
    attn_t_ref[...] = turned(attn_in, order_a)
    bg_t_ref[...] = turned(bg, order_b)

    cosine, sine = cos_ref[...], sin_ref[...]
    score_scale = 1.0 / math.sqrt(head_size)
    query_t = (matmul(attn_in, wq_ref[...]) + row_of(bq_ref)).T
    grad_t = matmul(wo_ref[...], bg, NT)
    for h in range(width // head_size):
        part = query_t[h * head_size : (h + 1) * head_size]
        q_t_ref[0, :, h * length : (h + 1) * length] = (
            turn(part, cosine, sine) * score_scale
        ).astype(BF)
        g_t_ref[0, :, h * length : (h + 1) * length] = grad_t[
            h * head_size : (h + 1) * head_size
        ].astype(BF)
    kv_t = matmul(attn_in, wkv_ref[...]).T
    kv = turn(kv_t, cosine, sine).T.astype(BF)
    kv_ref[0] = kv
    pay_ref[0, :length] = kv
    lane = lax.broadcasted_iota(jnp.int32, (1, LANES), 1)
    counts = jnp.zeros((1, LANES), F32)
    for c in range(DOCS):
        total = jnp.sum((segments == c).astype(F32), axis=1, keepdims=True)
        counts = counts + jnp.where(lane == c, total, 0.0)
    pay_ref[0, length:] = jnp.broadcast_to(counts, (COUNT_ROWS, LANES)).astype(BF)


def gelu_parts(hidden):
    cdf = 0.5 * (1.0 + lax.erf(hidden * math.sqrt(0.5)))
    bell = jnp.exp(-0.5 * (hidden * hidden)) * (1.0 / math.sqrt(2 * math.pi))
    return hidden * cdf, cdf + hidden * bell


def mlp_kernel(
    chunk, side_ref, mlp_ref, bg_ref, mlp_t_ref, bg_t_ref, up_ref, bup_ref, down_ref,
    keep_ref, send_ref, out_ref, din_ref, bupg_ref, act_s, hg_s,
):
    tokens, width = mlp_ref.shape

    @pl.when(pl.program_id(0) == 0)
    def _():
        out_ref[...] = jnp.zeros_like(out_ref)
        din_ref[...] = jnp.zeros_like(din_ref)

    bupg_ref[...] = jnp.zeros_like(bupg_ref)
    bias = bup_ref[...].astype(F32)

    def step(i, carry):
        at = pl.ds(pl.multiple_of(i * chunk, chunk), chunk)
        hidden = matmul(mlp_ref[at, :], up_ref[...]) + bias
        back = matmul(bg_ref[at, :], down_ref[...], NT)
        act, slope = gelu_parts(hidden)
        act = act.astype(BF)
        hg = (back * slope).astype(BF)
        act_s[at, :] = act
        hg_s[at, :] = hg
        bupg_ref[...] += jnp.sum(hg.astype(F32), axis=0, keepdims=True)
        out_ref[at, :] += matmul(act, down_ref[...])
        din_ref[at, :] += matmul(hg, up_ref[...], NT)
        return carry

    lax.fori_loop(0, tokens // chunk, step, 0)
    half = width // 2
    side = side_ref[0]
    mine = pl.ds(pl.multiple_of(side * half, half), half)
    other = pl.ds(pl.multiple_of((1 - side) * half, half), half)
    send_ref[0] = matmul(mlp_t_ref[other, :], hg_s[...]).astype(BF)
    send_ref[1] = matmul(bg_t_ref[other, :], act_s[...]).astype(BF)
    keep_ref[0] = matmul(mlp_t_ref[mine, :], hg_s[...]).astype(BF)
    keep_ref[1] = matmul(bg_t_ref[mine, :], act_s[...]).astype(BF)


def attention_kernel(
    heads, head_size, seq_devices, first_row, where_ref, seg_ref, q_t_ref, g_t_ref, even_ref,
    odd_ref, cos_ref, sin_ref, *refs,
):
    (mix_t_ref, qpg_t_ref, dkeep_ref, dsend_ref, kv_s, kv_t_s, bias_s, p_s, ds_s, gk_s, o_s, dq_s,
     dkv_s, m_s, l_s, d_s, mk_s) = refs[-17:]
    length = seg_ref.shape[-1]
    me = where_ref[0]
    start = me * length
    group = math.gcd(heads, 3)

    def columns(h, count=1):
        return slice(h * length, (h + count) * length)

    def head(h):
        return slice(h * head_size, (h + 1) * head_size)

    counts = jnp.zeros((1, LANES), F32)
    for m in range(seq_devices):
        ref = (even_ref, odd_ref)[m % 2]
        at = pl.multiple_of((me ^ m) * length, length)
        kv_s[pl.ds(at, length), :] = ref[m // 2, 0, :length]
        counts = counts + ref[m // 2, 0, length : length + COUNT_ROWS].astype(F32)[:1]

    segments = seg_ref[pl.ds(first_row + pl.program_id(0), 1), :]
    low = jnp.zeros((1, length), F32)
    for c in range(DOCS):
        later = (segments > c) | (segments < 0)
        low = low + jnp.where(later, counts[:, c : c + 1], 0.0)
    low = low.astype(jnp.int32)
    first_block = jnp.min(low) // KEY_BLOCK
    end_block = (start + length - 1) // KEY_BLOCK + 1
    place = start + lax.broadcasted_iota(jnp.int32, (1, length), 1)

    m_s[...] = jnp.full_like(m_s, NEGATIVE)
    l_s[...] = jnp.zeros_like(l_s)
    o_s[...] = jnp.zeros_like(o_s)
    dq_s[...] = jnp.zeros_like(dq_s)
    dkv_s[...] = jnp.zeros_like(dkv_s)

    def forward(b, carry):
        at = pl.multiple_of(b * KEY_BLOCK, KEY_BLOCK)
        kv = kv_s[pl.ds(at, KEY_BLOCK), :]
        keys = kv[:, :head_size]
        kv_t = kv.astype(F32).T.astype(BF)
        kv_t_s[b] = kv_t
        summed = jnp.concatenate([kv_t[head_size:], jnp.ones((16, KEY_BLOCK), BF)], axis=0)
        key_place = at + lax.broadcasted_iota(jnp.int32, (KEY_BLOCK, length), 0)
        allowed = (key_place <= place) & (key_place >= low)
        bias_s[...] = jnp.where(allowed, 0.0, NEGATIVE)
        bias = bias_s[...]
        shrinks = {}

        def scores(h):
            return matmul(keys, q_t_ref[0, :, columns(h, group)])

        def mix(h):
            o = matmul(summed, p_s[b, :, columns(h, group)])
            for j in range(group):
                row = slice(h + j, h + j + 1)
                part = o[:, columns(j)]
                shrink = shrinks.pop(h + j)
                o_s[:, columns(h + j)] = o_s[:, columns(h + j)] * shrink + part[:head_size]
                l_s[row, :] = l_s[row, :] * shrink + part[head_size : head_size + 1]

        ready = scores(0)
        for h in range(0, heads, group):
            now_scores = ready
            if h + group < heads:
                ready = scores(h + group)
            for j in range(group):
                row = slice(h + j, h + j + 1)
                s = now_scores[:, columns(j)] + bias
                before = m_s[row, :]
                now = jnp.maximum(before, jnp.max(s, axis=0, keepdims=True))
                p_s[b, :, columns(h + j)] = jnp.exp(s - now).astype(BF)
                shrinks[h + j] = jnp.exp(before - now)
                m_s[row, :] = now
                mk_s[b, row, :] = now
            if h > 0:
                mix(h - group)
        mix(heads - group)
        return carry

    lax.fori_loop(first_block, end_block, forward, 0)

    for h in range(heads):
        row = slice(h, h + 1)
        inverse = 1.0 / l_s[row, :]
        mixed = o_s[:, columns(h)] * inverse
        mix_t_ref[head(h), :] = mixed.astype(BF)
        d_s[row, :] = jnp.sum(
            mixed * g_t_ref[0, :, columns(h)].astype(F32), axis=0, keepdims=True
        )
        l_s[row, :] = inverse

    def backward(b, carry):
        at = pl.multiple_of(b * KEY_BLOCK, KEY_BLOCK)
        values = kv_s[pl.ds(at, KEY_BLOCK), :][:, head_size:]
        keys_t = kv_t_s[b][:head_size]
        inners = {}

        def prob_grads(h):
            for j in range(group):
                row = slice(h + j, h + j + 1)
                factor = jnp.exp(mk_s[b, row, :] - m_s[row, :]) * l_s[row, :]
                scaled = g_t_ref[0, :, columns(h + j)].astype(F32) * factor
                gk_s[:, columns(h + j)] = scaled.astype(BF)
                inners[h + j] = d_s[row, :] * factor
            return matmul(values, gk_s[:, columns(h, group)])

        ready = prob_grads(0)
        for h in range(0, heads, group):
            now_grads = ready
            if h + group < heads:
                ready = prob_grads(h + group)
            for j in range(group):
                p = p_s[b, :, columns(h + j)].astype(F32)
                ds_s[:, columns(h + j)] = (
                    p * (now_grads[:, columns(j)] - inners.pop(h + j))
                ).astype(BF)
        dq_s[...] += matmul(keys_t, ds_s[...])
        dk = matmul(ds_s[...], q_t_ref[0], NT)
        dv = matmul(p_s[b], gk_s[...], NT)
        dkv_s[pl.ds(at, KEY_BLOCK), :] = jnp.concatenate([dk, dv], axis=1).astype(BF)
        return carry

    lax.fori_loop(first_block, end_block, backward, 0)

    cosine, sine = cos_ref[...], sin_ref[...]
    score_scale = 1.0 / math.sqrt(head_size)
    for h in range(heads):
        qpg_t_ref[head(h), :] = turn(
            dq_s[:, columns(h)] * score_scale, cosine, -sine
        ).astype(BF)
    for m in range(seq_devices):
        ref = (dkeep_ref, dsend_ref)[m % 2]
        at = pl.multiple_of((me ^ m) * length, length)
        ref[m // 2, 0] = dkv_s[pl.ds(at, length), :]


def mix_kernel(
    side_ref, tok_ref, seg_ref, mix_t_ref, qpg_t_ref, attn_t_ref, bg_t_ref, mlp_ref, wo_ref,
    bo_ref, bd_ref, out_ref, keep_ref, send_ref, acc_q, acc_o,
):
    step, steps = pl.program_id(0), pl.num_programs(0)

    @pl.when(step == 0)
    def _():
        acc_q[...] = jnp.zeros_like(acc_q)
        acc_o[...] = jnp.zeros_like(acc_o)

    mix_t = mix_t_ref[...]
    branch = matmul(mix_t, wo_ref[...], TN) + (row_of(bo_ref) + row_of(bd_ref)) + mlp_ref[...]
    valid = valid_column(seg_ref[pl.ds(step, 1), :])
    out_ref[0] = (tok_ref[0].astype(F32) + valid * branch).astype(BF)
    acc_q[...] += matmul(attn_t_ref[...], qpg_t_ref[...], NT)
    acc_o[...] += matmul(bg_t_ref[...], mix_t, NT)

    @pl.when(step == steps - 1)
    def _():
        half = acc_q.shape[0] // 2
        side = side_ref[0]
        mine = pl.ds(pl.multiple_of(side * half, half), half)
        other = pl.ds(pl.multiple_of((1 - side) * half, half), half)
        for j, acc in enumerate((acc_q, acc_o)):
            keep_ref[j] = acc[mine, :].astype(BF)
            send_ref[j] = acc[other, :].astype(BF)


def exit_kernel(
    order_a, rows, permuted,
    side_ref, tok_ref, og_ref, seg_ref, qpg_t_ref, attn_t_ref, din_ref, wq_ref, wkv_ref,
    ag_ref, mg_ref, cos_ref, sin_ref, bupg_ref, shuffle_ref, dkv_refs,
    tg_ref, keep_ref, send_ref, acc, vec,
):
    step, steps = pl.program_id(0), pl.num_programs(0)

    @pl.when(step == 0)
    def _():
        acc[...] = jnp.zeros_like(acc)
        vec[...] = jnp.zeros_like(vec)

    dkv = sum((ref[0].astype(F32) for ref in dkv_refs[1:]), dkv_refs[0][0].astype(F32))
    kvpg_t = turn(dkv.T, cos_ref[...], -sin_ref[...]).astype(BF)
    acc[...] += matmul(attn_t_ref[...], kvpg_t, NT)
    qpg_t = qpg_t_ref[...]
    d_attn = (matmul(wq_ref[...], qpg_t) + matmul(wkv_ref[...], kvpg_t)).T
    d_mlp = din_ref[...]
    n, scale = norm_parts(tok_ref[0].astype(F32))
    og = og_ref[0].astype(F32)
    e = d_attn * row_of(ag_ref) + d_mlp * row_of(mg_ref)
    inner = jnp.mean(e * n, axis=-1, keepdims=True)
    tg_ref[0] = (og + scale * (e - jnp.mean(e, axis=-1, keepdims=True) - n * inner)).astype(BF)
    ones = jnp.ones((8, qpg_t.shape[1]), BF)
    bg = (og * valid_column(seg_ref[pl.ds(step, 1), :])).astype(BF)
    sums = [d_attn * n, d_attn, d_mlp * n, d_mlp, None, bg.astype(F32)]
    for j, value in enumerate(sums):
        if value is None:
            part = matmul(ones, qpg_t, NT)[:1]
        else:
            part = jnp.sum(value, axis=0, keepdims=True)
        vec[j : j + 1, :] += part

    @pl.when(step == steps - 1)
    def _():
        vec[8:12, :] = bupg_ref[...]
        if permuted:
            columns = permute_rows(vec[...].T, order_a, rows)
        else:
            columns = lax.dot_general(
                shuffle_ref[...], vec[...], NT, precision=lax.Precision.HIGHEST,
                preferred_element_type=F32,
            )
        half = columns.shape[0] // 2
        acc_columns = slice(0, LANES)
        vec_columns = slice(LANES, 2 * LANES)
        for side in range(2):

            @pl.when(side_ref[0] == side)
            def _():
                mine = slice(side * half, (side + 1) * half)
                other = slice((1 - side) * half, (2 - side) * half)
                keep_ref[:, acc_columns] = acc[mine, :].astype(BF)
                send_ref[:, acc_columns] = acc[other, :].astype(BF)
                keep_ref[:, vec_columns] = columns[mine].astype(BF)
                send_ref[:, vec_columns] = columns[other].astype(BF)


def partners(size, mask):
    return [(i, i ^ mask) for i in range(size)]


class Stream:
    def __init__(self, arrays, count, resident, width):
        self.terms = [(array, resident, 0, at, ()) for array, at in arrays]
        self.count, self.resident, self.width = count, resident, width
        self.rows = arrays[0][0].shape[1]

    def halve(self, bit):
        count = self.count = self.count // 2
        mine, other = [], []
        for array, resident, column, at, adds in self.terms:
            mine.append((array, resident, column, at, adds + ((bit, count),)))
            other.append((array, resident, column, at + count, adds + ((bit, -count),)))
        self.terms = mine
        return other


def first_block(term, where_ref):
    at = term[3]
    for (axis, bit), weight in term[4]:
        at = at + ((where_ref[axis] >> bit) & 1) * weight
    return at


def term_spec(term, width, group):
    if term[1]:
        return pl.BlockSpec(memory_space=pltpu.VMEM)
    return pl.BlockSpec(
        (group, term[0].shape[1], width),
        lambda i, where_ref: (first_block(term, where_ref) // group + i, 0, term[2]),
    )


def in_hbm(value):
    return pltpu.with_memory_space_constraint(value, pltpu.HBM)


def operands_of(terms):
    return [term[0] if term[1] else in_hbm(term[0]) for term in terms]


def read_terms(terms, refs, width, group, where_ref):
    total = None
    for term, ref in zip(terms, refs):
        if term[1]:
            at = first_block(term, where_ref) + pl.program_id(0) * group
            value = ref[pl.ds(at, group), :, term[2] * width : (term[2] + 1) * width]
        else:
            value = ref[...]
        value = value.astype(F32)
        total = value if total is None else total + value
    return total


def call_on_terms(
    body, name, where, after, steps, in_specs, operands, out_specs, out_shape, length
):
    return pl.pallas_call(
        body,
        grid_spec=pltpu.PrefetchScalarGridSpec(
            num_scalar_prefetch=1, grid=(steps,), in_specs=in_specs, out_specs=out_specs
        ),
        out_shape=out_shape,
        compiler_params=params(limit=24),
        cost_estimate=length,
        name=name,
    )(ordered_after(where, *after), *operands)


def sums_to_send(picks, streams, joined, where, after, length):
    count, width, rows = streams[0].count, streams[0].width, streams[0].rows
    resident = streams[0].resident
    group = count
    while group > 1 and group * width > 4 * 3072 and not resident:
        group //= 2
    terms = [term for pick in picks for term in pick]
    outputs = 1 if joined else len(picks)
    shape = (rows, width * len(picks) // outputs)

    def body(where_ref, *refs):
        at = 0
        for j, pick in enumerate(picks):
            total = read_terms(pick, refs[at : at + len(pick)], width, group, where_ref).astype(BF)
            if joined:
                refs[-1][:, :, j * width : (j + 1) * width] = total
            else:
                refs[len(terms) + j][...] = total
            at += len(pick)

    if resident:
        out_spec = pl.BlockSpec(memory_space=pltpu.VMEM)
    else:
        out_spec = pl.BlockSpec((group,) + shape, lambda i, _: (i, 0, 0))
    return call_on_terms(
        body, "combine", where, after, count // group,
        [term_spec(term, width, group) for term in terms],
        operands_of(terms),
        [out_spec] * outputs,
        [jax.ShapeDtypeStruct((count,) + shape, BF)] * outputs,
        length or short(2 * count * rows * width * len(terms)),
    )


def own_sums(streams, where, after=()):
    terms = [term for stream in streams for term in stream.terms]

    def body(where_ref, *refs):
        at = 0
        for stream, output in zip(streams, refs[len(terms) :]):
            size = len(stream.terms)
            output[...] = read_terms(
                stream.terms, refs[at : at + size], stream.width, 1, where_ref
            )[0]
            at += size

    return call_on_terms(
        body, "own", where, after, 1,
        [term_spec(term, stream.width, 1) for stream in streams for term in stream.terms],
        operands_of(terms),
        [whole((stream.rows, stream.width)) for stream in streams],
        [jax.ShapeDtypeStruct((stream.rows, stream.width), F32) for stream in streams],
        short(2 * len(terms) * streams[0].rows * streams[0].width),
    )


def ordered_after(value, *others):
    if not others:
        return value
    return lax.optimization_barrier((value, others))[0]


AXES = ("seq", "batch")


def reduce_level(streams, bits, where, after=(), length=None):
    picks = [stream.halve(bit) for stream, bit in zip(streams, bits)]
    joined = len(set(bits)) == 1
    sends = sums_to_send(picks, streams, joined, where, after, length)
    recvs = []
    for (axis, bit), send in zip(bits, sends):
        recvs.append(
            lax.ppermute(send, AXES[axis], partners(lax.axis_size(AXES[axis]), 1 << bit))
        )
    for j, stream in enumerate(streams):
        column = j if joined else 0
        stream.terms.append((recvs[0 if joined else j], stream.resident, column, 0, ()))
    return sends, recvs


def on_device(
    tokens, segment_ids, attn_gain, attn_shift, mlp_gain, mlp_shift, w_query, b_query,
    w_keyvalue, w_out, b_out, w_up, b_up, w_down, b_down, out_grad,
):
    row_count, length, width = tokens.shape
    head_size = w_keyvalue.shape[1] // 2
    heads = width // head_size
    hidden = w_up.shape[1]
    token_count = row_count * length
    seq_devices = lax.axis_size("seq")
    batch_devices = lax.axis_size("batch")
    devices = seq_devices * batch_devices
    seq_index = lax.axis_index("seq").astype(jnp.int32)
    batch_index = lax.axis_index("batch").astype(jnp.int32)
    side = (seq_index & 1).reshape(1)
    where = jnp.stack([seq_index, batch_index])
    rows = width // devices
    permuted = rows % 8 == 0
    seq_bits = list(range(seq_devices.bit_length() - 1))

    def reversed_bits(value, count):
        return sum(((value >> j) & 1) << (count - 1 - j) for j in range(count))

    batch_order = [
        reversed_bits(z, batch_devices.bit_length() - 1) for z in range(batch_devices)
    ]

    def device_order(bits):
        order = []
        for k in range(seq_devices):
            at = 0
            for j, bit in enumerate(bits):
                at |= ((k >> (len(bits) - 1 - j)) & 1) << bit
            order += [z * seq_devices + at for z in batch_order]
        return order

    order_a = device_order(seq_bits)
    order_b = device_order(seq_bits[:1] + seq_bits[:0:-1])

    def ordered(values, order):
        if permuted:
            return values
        shaped = values.reshape(values.shape[:-2] + (devices, rows, values.shape[-1]))
        return jnp.take(shaped, jnp.array(order), axis=-3).reshape(values.shape)

    positions = (seq_index * length + jnp.arange(length)).astype(F32)
    inverse = 10000.0 ** (-(jnp.arange(HALF_ROT).astype(F32) * (2.0 / ROT_DIMS)))
    angles = inverse[:, None] * positions[None, :]
    cosine, sine = jnp.cos(angles), jnp.sin(angles)
    segments_spec = whole((row_count, length))
    turn_spec = whole((HALF_ROT, length))
    width_spec = whole((width,))

    def row_block(shape, first=0):
        return pl.BlockSpec((1,) + shape, lambda r, *_: (first + r, 0, 0))

    token_block = pl.BlockSpec((length, width), lambda r, *_: (r, 0))
    whole_lanes = length % LANES == 0

    def column_block(first=0):
        if whole_lanes:
            return pl.BlockSpec((width, length), lambda r, *_: (0, first + r))
        return pl.BlockSpec((None, width, length), lambda r, *_: (first + r, 0, 0))

    columns = jax.ShapeDtypeStruct(
        (width, token_count) if whole_lanes else (row_count, width, length), BF
    )

    def joined(values):
        if whole_lanes:
            return values
        return jnp.transpose(values, (1, 0, 2)).reshape(width, token_count)

    lanes = heads * length
    mlp_in, bg, mlp_t, bg_t, attn_t, q_t, g_t, keyvalue, payload = pl.pallas_call(
        functools.partial(entry_kernel, head_size, order_a, order_b, rows, permuted),
        grid=(row_count,),
        in_specs=[
            row_block((length, width)), row_block((length, width)), segments_spec,
            width_spec, width_spec, width_spec, width_spec, width_spec,
            whole((width, width)), whole((width, 2 * head_size)), whole((width, width)),
            turn_spec, turn_spec,
        ],
        out_specs=[
            token_block, token_block, column_block(), column_block(), column_block(),
            row_block((head_size, lanes)), row_block((head_size, lanes)),
            row_block((length, 2 * head_size)), row_block((length + COUNT_ROWS, 2 * head_size)),
        ],
        out_shape=[
            jax.ShapeDtypeStruct((token_count, width), BF),
            jax.ShapeDtypeStruct((token_count, width), BF),
            columns,
            columns,
            columns,
            jax.ShapeDtypeStruct((row_count, head_size, lanes), BF),
            jax.ShapeDtypeStruct((row_count, head_size, lanes), BF),
            jax.ShapeDtypeStruct((row_count, length, 2 * head_size), BF),
            jax.ShapeDtypeStruct((row_count, length + COUNT_ROWS, 2 * head_size), BF),
        ],
        compiler_params=params(60),
        cost_estimate=LONG,
        name="entry",
    )(
        tokens, out_grad, segment_ids, attn_gain, attn_shift, mlp_gain, mlp_shift, b_query,
        w_query, w_keyvalue, w_out, cosine, sine,
    )
    mlp_t, attn_t = ordered(mlp_t, order_a), ordered(attn_t, order_a)
    bg_t = ordered(bg_t, order_b)

    gathered = [payload]
    for mask in range(2, seq_devices, 2):
        gathered.append(lax.ppermute(payload, "seq", partners(seq_devices, mask)))

    tile = math.gcd(512, hidden)
    half = width // 2
    pair_cols = pl.BlockSpec((2, half, tile), lambda f, *_: (0, 0, f))
    pair_shape = jax.ShapeDtypeStruct((2, half, hidden), BF)
    keep, send, mlp_out, mlp_din, b_up_part = pl.pallas_call(
        functools.partial(mlp_kernel, token_count),
        grid_spec=pltpu.PrefetchScalarGridSpec(
            num_scalar_prefetch=1,
            grid=(hidden // tile,),
            in_specs=[
                whole((token_count, width)), whole((token_count, width)),
                whole((width, token_count)), whole((width, token_count)),
                pl.BlockSpec((width, tile), lambda f, *_: (0, f)),
                pl.BlockSpec((1, tile), lambda f, *_: (0, f)),
                pl.BlockSpec((tile, width), lambda f, *_: (f, 0)),
            ],
            out_specs=[
                pair_cols, pair_cols, whole((token_count, width)), whole((token_count, width)),
                pl.BlockSpec((1, tile), lambda f, *_: (0, f)),
            ],
            scratch_shapes=[
                pltpu.VMEM((token_count, tile), BF), pltpu.VMEM((token_count, tile), BF),
            ],
        ),
        out_shape=[
            pair_shape, pair_shape,
            jax.ShapeDtypeStruct((token_count, width), F32),
            jax.ShapeDtypeStruct((token_count, width), F32),
            jax.ShapeDtypeStruct((1, hidden), F32),
        ],
        compiler_params=params(60),
        cost_estimate=LONG,
        name="mlp",
    )(side, mlp_in, bg, joined(mlp_t), joined(bg_t), w_up, b_up.reshape(1, hidden), w_down)

    even = jnp.stack(ordered_after(tuple(gathered), b_up_part))
    odd = lax.ppermute(even, "seq", partners(seq_devices, 1))

    bits = [(0, bit) for bit in range(1, seq_devices.bit_length() - 1)]
    batch_bits = [(1, bit) for bit in range(batch_devices.bit_length() - 1)]
    blocks = devices // 2

    def pair_streams(keep, send, resident):
        shape = (2 * blocks, rows, keep.shape[2])
        keep = keep.reshape(shape)
        recv = lax.ppermute(send.reshape(shape), "seq", partners(seq_devices, 1))
        return [
            Stream([(keep, at), (recv, at)], blocks, resident, keep.shape[2])
            for at in (0, blocks)
        ]

    mlp_streams = pair_streams(keep, send, False)

    half_seq = seq_devices // 2
    key_blocks = length * seq_devices // KEY_BLOCK
    stat_rows = -(-heads // 8) * 8

    def attention(first, count, after, before):
        kv_rows = pl.BlockSpec(
            (half_seq, 1, length + COUNT_ROWS, 2 * head_size), lambda r, *_: (0, first + r, 0, 0)
        )
        dkv_rows = pl.BlockSpec(
            (half_seq, 1, length, 2 * head_size), lambda r, *_: (0, first + r, 0, 0)
        )
        dkv_shape = jax.ShapeDtypeStruct((half_seq, row_count, length, 2 * head_size), BF)
        return pl.pallas_call(
            functools.partial(attention_kernel, heads, head_size, seq_devices, first),
            grid_spec=pltpu.PrefetchScalarGridSpec(
                num_scalar_prefetch=1,
                grid=(count,),
                in_specs=[
                    segments_spec, row_block((head_size, lanes), first),
                    row_block((head_size, lanes), first), kv_rows, kv_rows, turn_spec, turn_spec,
                ]
                + [pl.BlockSpec(memory_space=pl.ANY)] * len(before),
                out_specs=[column_block(first), column_block(first), dkv_rows, dkv_rows],
                scratch_shapes=[
                    pltpu.VMEM((key_blocks * KEY_BLOCK, 2 * head_size), BF),
                    pltpu.VMEM((key_blocks, 2 * head_size, KEY_BLOCK), BF),
                    pltpu.VMEM((KEY_BLOCK, length), F32),
                    pltpu.VMEM((key_blocks, KEY_BLOCK, lanes), BF),
                    pltpu.VMEM((KEY_BLOCK, lanes), BF),
                    pltpu.VMEM((head_size, lanes), BF),
                    pltpu.VMEM((head_size, lanes), F32),
                    pltpu.VMEM((head_size, lanes), F32),
                    pltpu.VMEM((key_blocks * KEY_BLOCK, 2 * head_size), BF),
                    pltpu.VMEM((stat_rows, length), F32),
                    pltpu.VMEM((stat_rows, length), F32),
                    pltpu.VMEM((stat_rows, length), F32),
                    pltpu.VMEM((key_blocks, stat_rows, length), F32),
                ],
            ),
            out_shape=[columns, columns, dkv_shape, dkv_shape],
            input_output_aliases={8 + j: j for j in range(len(before))},
            compiler_params=params(60),
            cost_estimate=LONG,
        name="attention",
        )(
            ordered_after(where, *after), segment_ids, q_t, g_t, in_hbm(even), in_hbm(odd), cosine,
            sine, *before,
        )

    pair_levels = [(bits[i], bits[-1 - i]) for i in range(len(bits))]
    batch_levels = [(bit, bit) for bit in batch_bits]
    mlp_levels = iter(pair_levels + batch_levels)
    results, first_row = [b_up_part], 0
    for share in (row_count // 4, row_count - row_count // 4):
        after = results[:1]
        if first_row:
            after, _ = reduce_level(mlp_streams, next(mlp_levels), where, after)
        results = attention(first_row, share, after, results if first_row else [])
        first_row += share
    mix_t, qpg_t, dkv_keep, dkv_send = results
    dkv_recv = lax.ppermute(dkv_send, "seq", partners(seq_devices, 1))
    after, mlp_recv = reduce_level(mlp_streams, next(mlp_levels), where, [mix_t], LONG)

    dkv_recv = ordered_after(dkv_recv, *after)
    dkv_low = (dkv_keep.astype(F32) + dkv_recv.astype(F32)).astype(BF)
    dkv_parts = [dkv_low[0]]
    for j in range(1, half_seq):
        dkv_parts.append(lax.ppermute(dkv_low[j], "seq", partners(seq_devices, 2 * j)))

    pair_spec = pl.BlockSpec(memory_space=pltpu.VMEM)
    pair_width = jax.ShapeDtypeStruct((2, half, width), BF)
    output, keep, send = pl.pallas_call(
        mix_kernel,
        grid_spec=pltpu.PrefetchScalarGridSpec(
            num_scalar_prefetch=1,
            grid=(row_count,),
            in_specs=[
                row_block((length, width)), segments_spec, column_block(), column_block(),
                column_block(), column_block(), token_block, whole((width, width)),
                width_spec, width_spec,
            ],
            out_specs=[row_block((length, width)), pair_spec, pair_spec],
            scratch_shapes=[pltpu.VMEM((width, width), F32), pltpu.VMEM((width, width), F32)],
        ),
        out_shape=[
            jax.ShapeDtypeStruct((row_count, length, width), BF), pair_width, pair_width,
        ],
        compiler_params=params(56),
        cost_estimate=LONG,
        name="mix",
    )(
        ordered_after(side, dkv_parts[0]), tokens, segment_ids, mix_t, qpg_t, attn_t, bg_t,
        mlp_out, w_out, b_out, b_down,
    )
    mix_streams = pair_streams(keep, send, True)
    after = [keep, *mlp_recv, *dkv_parts[1:]]
    after, _ = reduce_level(mlp_streams, next(mlp_levels), where, after, LONG)
    mix_levels = iter(pair_levels + batch_levels)
    after, _ = reduce_level(mix_streams, next(mix_levels), where, after)

    dkv_count = len(dkv_parts)

    def exit_body(*refs):
        fixed, rest = refs[:15], refs[15:]
        exit_kernel(order_a, rows, permuted, *fixed, rest[:dkv_count], *rest[dkv_count:])

    if permuted:
        shuffle = jnp.zeros((8, LANES), F32)
    else:
        places = (jnp.array(order_a)[:, None] * rows + jnp.arange(rows)[None, :]).reshape(width, 1)
        shuffle = (places == jnp.arange(width)[None, :]).astype(F32)
    extra_spec = pl.BlockSpec(memory_space=pltpu.VMEM)
    extra_shape = jax.ShapeDtypeStruct((half, 2 * LANES), BF)
    tokens_grad, keep, send = pl.pallas_call(
        exit_body,
        grid_spec=pltpu.PrefetchScalarGridSpec(
            num_scalar_prefetch=1,
            grid=(row_count,),
            in_specs=[
                row_block((length, width)), row_block((length, width)), segments_spec,
                column_block(), column_block(), token_block, whole((width, width)),
                whole((width, 2 * head_size)), width_spec, width_spec, turn_spec, turn_spec,
                whole((hidden // width, width)), whole(shuffle.shape),
            ]
            + [row_block((length, 2 * head_size))] * dkv_count,
            out_specs=[row_block((length, width)), extra_spec, extra_spec],
            scratch_shapes=[
                pltpu.VMEM((width, 2 * head_size), F32), pltpu.VMEM((LANES, width), F32),
            ],
        ),
        out_shape=[
            jax.ShapeDtypeStruct((row_count, length, width), BF), extra_shape, extra_shape,
        ],
        compiler_params=params(56),
        cost_estimate=LONG,
        name="exit",
    )(
        ordered_after(side, *after), tokens, out_grad, segment_ids, qpg_t, attn_t, mlp_din, w_query, w_keyvalue,
        attn_gain, mlp_gain, cosine, sine, b_up_part.reshape(width, hidden // width).T, shuffle,
        *dkv_parts,
    )

    shape = (blocks, rows, 2 * LANES)
    keep = keep.reshape(shape)
    recv = lax.ppermute(send.reshape(shape), "seq", partners(seq_devices, 1))
    extra_streams = [Stream([(keep, 0), (recv, 0)], blocks, True, 2 * LANES)]
    extra_levels = [(bit,) for bit in bits + batch_bits]
    after = [keep]
    for level in mlp_levels:
        after, _ = reduce_level(mlp_streams, level, where, after, LONG)
    for level in extra_levels:
        reduce_level(extra_streams, level, where, after)
        after = []
        level = next(mix_levels, None)
        if level:
            reduce_level(mix_streams, level, where)
    sums = []
    for streams in (mlp_streams, mix_streams, extra_streams):
        sums += own_sums(streams, where)
    w_up_grad, w_down_grad_t, w_query_grad, w_out_grad_t, extra = sums
    vectors = extra[:, LANES:]
    return (
        output,
        keyvalue,
        tokens_grad,
        vectors[:, 0],
        vectors[:, 1],
        vectors[:, 2],
        vectors[:, 3],
        w_query_grad,
        vectors[:, 4],
        extra[:, :LANES],
        w_out_grad_t.T,
        vectors[:, 5],
        w_up_grad,
        vectors[:, 8 : 8 + hidden // width].reshape(-1),
        w_down_grad_t.T,
        vectors[:, 5],
    )


def solution(mesh):
    row_spec = P("batch", "seq", None)
    split = P(("batch", "seq"))
    first = P(("batch", "seq"), None)
    last = P(None, ("batch", "seq"))
    return jax.shard_map(
        on_device,
        mesh=mesh,
        in_specs=(row_spec, P("batch", "seq")) + (P(),) * 13 + (row_spec,),
        out_specs=(
            row_spec, row_spec, row_spec, split, split, split, split, first, split, first, last,
            split, first, split, last, split,
        ),
        check_vma=False,
    )
```

```python
import functools
import math

import jax
import jax.numpy as jnp
from jax import lax
from jax.experimental import pallas as pl
from jax.experimental.pallas import tpu as pltpu
from jax.sharding import PartitionSpec as P

ROT_DIMS = 16
HALF_ROT = ROT_DIMS // 2
DOCS = 6
EPSILON = 1e-05
KEY_BLOCK = 256
COUNT_ROWS = 16
LANES = 128
NEGATIVE = -1e30
BF = jnp.bfloat16
F32 = jnp.float32
NN = (((1,), (0,)), ((), ()))
NT = (((1,), (1,)), ((), ()))
TN = (((0,), (0,)), ((), ()))


def matmul(left, right, dims=NN):
    return lax.dot_general(left, right, dims, preferred_element_type=F32)


def params(limit):
    return pltpu.CompilerParams(
        dimension_semantics=("arbitrary",), vmem_limit_bytes=limit * 1024 * 1024
    )


LONG = pl.CostEstimate(flops=4 * 10**10, transcendentals=0, bytes_accessed=10**7)

LONGEST = pl.CostEstimate(flops=3 * 10**11, transcendentals=0, bytes_accessed=10**7)


def short(size):
    return pl.CostEstimate(flops=0, transcendentals=0, bytes_accessed=size)


def whole(shape):
    return pl.BlockSpec(shape, lambda *_: (0,) * len(shape))


def permute_rows(values, order, rows):
    return jnp.concatenate([values[b * rows : (b + 1) * rows] for b in order], axis=0)


def row_of(ref):
    return ref[...].astype(F32).reshape(1, ref.shape[0])


def valid_column(segment_row):
    length = segment_row.shape[-1]
    row = jnp.broadcast_to((segment_row >= 0).astype(F32), (LANES, length))
    return row.T[:, :1]


def norm_parts(values):
    center = values - jnp.mean(values, axis=-1, keepdims=True)
    spread = jnp.mean(center * center, axis=-1, keepdims=True)
    scale = lax.rsqrt(spread + EPSILON)
    return center * scale, scale


def turn(values, cosine, sine):
    leading = values[:HALF_ROT]
    trailing = values[HALF_ROT:ROT_DIMS]
    return jnp.concatenate(
        [leading * cosine - trailing * sine, trailing * cosine + leading * sine, values[ROT_DIMS:]],
        axis=0,
    )


def entry_kernel(
    head_size, order_a, order_b, rows, permuted,
    tok_ref, og_ref, seg_ref, ag_ref, as_ref, mg_ref, ms_ref, bq_ref, wq_ref, wkv_ref, wo_ref,
    cos_ref, sin_ref, mlp_ref, bg_ref, mlp_t_ref, bg_t_ref, attn_t_ref, q_t_ref, g_t_ref, kv_ref, pay_ref,
):
    x = tok_ref[0].astype(F32)
    length, width = x.shape
    n, _ = norm_parts(x)
    attn_in = (n * row_of(ag_ref) + row_of(as_ref)).astype(BF)
    mlp_in = (n * row_of(mg_ref) + row_of(ms_ref)).astype(BF)
    segments = seg_ref[pl.ds(pl.program_id(0), 1), :]
    bg = (og_ref[0].astype(F32) * valid_column(segments)).astype(BF)
    mlp_ref[...] = mlp_in
    bg_ref[...] = bg

    def turned(values, order):
        flipped = values.astype(F32).T
        if permuted:
            flipped = permute_rows(flipped, order, rows)
        return flipped.astype(BF)

    mlp_t_ref[...] = turned(mlp_in, order_a)
    attn_t_ref[...] = turned(attn_in, order_a)
    bg_t_ref[...] = turned(bg, order_b)

    cosine, sine = cos_ref[...], sin_ref[...]
    score_scale = 1.0 / math.sqrt(head_size)
    query_t = (matmul(attn_in, wq_ref[...]) + row_of(bq_ref)).T
    grad_t = matmul(wo_ref[...], bg, NT)
    for h in range(width // head_size):
        part = query_t[h * head_size : (h + 1) * head_size]
        q_t_ref[0, :, h * length : (h + 1) * length] = (
            turn(part, cosine, sine) * score_scale
        ).astype(BF)
        g_t_ref[0, :, h * length : (h + 1) * length] = grad_t[
            h * head_size : (h + 1) * head_size
        ].astype(BF)
    kv_t = matmul(attn_in, wkv_ref[...]).T
    kv = turn(kv_t, cosine, sine).T.astype(BF)
    kv_ref[0] = kv
    pay_ref[0, :length] = kv
    lane = lax.broadcasted_iota(jnp.int32, (1, LANES), 1)
    counts = jnp.zeros((1, LANES), F32)
    for c in range(DOCS):
        total = jnp.sum((segments == c).astype(F32), axis=1, keepdims=True)
        counts = counts + jnp.where(lane == c, total, 0.0)
    pay_ref[0, length:] = jnp.broadcast_to(counts, (COUNT_ROWS, LANES)).astype(BF)


def gelu_parts(hidden):
    cdf = 0.5 * (1.0 + lax.erf(hidden * math.sqrt(0.5)))
    bell = jnp.exp(-0.5 * (hidden * hidden)) * (1.0 / math.sqrt(2 * math.pi))
    return hidden * cdf, cdf + hidden * bell


def mlp_kernel(
    chunk, side_ref, mlp_ref, bg_ref, mlp_t_ref, bg_t_ref, up_ref, bup_ref, down_ref,
    keep_ref, send_ref, out_ref, din_ref, bupg_ref, act_s, hg_s,
):
    tokens, width = mlp_ref.shape

    @pl.when(pl.program_id(0) == 0)
    def _():
        out_ref[...] = jnp.zeros_like(out_ref)
        din_ref[...] = jnp.zeros_like(din_ref)

    bupg_ref[...] = jnp.zeros_like(bupg_ref)
    bias = bup_ref[...].astype(F32)

    def step(i, carry):
        at = pl.ds(pl.multiple_of(i * chunk, chunk), chunk)
        hidden = matmul(mlp_ref[at, :], up_ref[...]) + bias
        back = matmul(bg_ref[at, :], down_ref[...], NT)
        act, slope = gelu_parts(hidden)
        act = act.astype(BF)
        hg = (back * slope).astype(BF)
        act_s[at, :] = act
        hg_s[at, :] = hg
        bupg_ref[...] += jnp.sum(hg.astype(F32), axis=0, keepdims=True)
        out_ref[at, :] += matmul(act, down_ref[...])
        din_ref[at, :] += matmul(hg, up_ref[...], NT)
        return carry

    lax.fori_loop(0, tokens // chunk, step, 0)
    half = width // 2
    side = side_ref[0]
    mine = pl.ds(pl.multiple_of(side * half, half), half)
    other = pl.ds(pl.multiple_of((1 - side) * half, half), half)
    send_ref[0] = matmul(mlp_t_ref[other, :], hg_s[...]).astype(BF)
    send_ref[1] = matmul(bg_t_ref[other, :], act_s[...]).astype(BF)
    keep_ref[0] = matmul(mlp_t_ref[mine, :], hg_s[...]).astype(BF)
    keep_ref[1] = matmul(bg_t_ref[mine, :], act_s[...]).astype(BF)


def attention_kernel(
    heads, head_size, seq_devices, first_row, where_ref, seg_ref, q_t_ref, g_t_ref, even_ref,
    odd_ref, cos_ref, sin_ref, *refs,
):
    (mix_t_ref, qpg_t_ref, dkeep_ref, dsend_ref, kv_s, kv_t_s, bias_s, p_s, ds_s, gk_s, o_s, dq_s,
     dkv_s, m_s, l_s, d_s, mk_s) = refs[-17:]
    length = seg_ref.shape[-1]
    me = where_ref[0]
    start = me * length
    group = math.gcd(heads, 3)

    def columns(h, count=1):
        return slice(h * length, (h + count) * length)

    def head(h):
        return slice(h * head_size, (h + 1) * head_size)

    counts = jnp.zeros((1, LANES), F32)
    for m in range(seq_devices):
        ref = (even_ref, odd_ref)[m % 2]
        at = pl.multiple_of((me ^ m) * length, length)
        kv_s[pl.ds(at, length), :] = ref[m // 2, 0, :length]
        counts = counts + ref[m // 2, 0, length : length + COUNT_ROWS].astype(F32)[:1]

    segments = seg_ref[pl.ds(first_row + pl.program_id(0), 1), :]
    low = jnp.zeros((1, length), F32)
    for c in range(DOCS):
        later = (segments > c) | (segments < 0)
        low = low + jnp.where(later, counts[:, c : c + 1], 0.0)
    low = low.astype(jnp.int32)
    first_block = jnp.min(low) // KEY_BLOCK
    end_block = (start + length - 1) // KEY_BLOCK + 1
    place = start + lax.broadcasted_iota(jnp.int32, (1, length), 1)

    m_s[...] = jnp.full_like(m_s, NEGATIVE)
    l_s[...] = jnp.zeros_like(l_s)
    o_s[...] = jnp.zeros_like(o_s)
    dq_s[...] = jnp.zeros_like(dq_s)
    dkv_s[...] = jnp.zeros_like(dkv_s)

    def forward(b, carry):
        at = pl.multiple_of(b * KEY_BLOCK, KEY_BLOCK)
        kv = kv_s[pl.ds(at, KEY_BLOCK), :]
        keys = kv[:, :head_size]
        kv_t = kv.astype(F32).T.astype(BF)
        kv_t_s[b] = kv_t
        summed = jnp.concatenate([kv_t[head_size:], jnp.ones((16, KEY_BLOCK), BF)], axis=0)
        key_place = at + lax.broadcasted_iota(jnp.int32, (KEY_BLOCK, length), 0)
        allowed = (key_place <= place) & (key_place >= low)
        bias_s[...] = jnp.where(allowed, 0.0, NEGATIVE)
        bias = bias_s[...]
        shrinks = {}

        def scores(h):
            return matmul(keys, q_t_ref[0, :, columns(h, group)])

        def mix(h):
            o = matmul(summed, p_s[b, :, columns(h, group)])
            for j in range(group):
                row = slice(h + j, h + j + 1)
                part = o[:, columns(j)]
                shrink = shrinks.pop(h + j)
                o_s[:, columns(h + j)] = o_s[:, columns(h + j)] * shrink + part[:head_size]
                l_s[row, :] = l_s[row, :] * shrink + part[head_size : head_size + 1]

        ready = scores(0)
        for h in range(0, heads, group):
            now_scores = ready
            if h + group < heads:
                ready = scores(h + group)
            for j in range(group):
                row = slice(h + j, h + j + 1)
                s = now_scores[:, columns(j)] + bias
                before = m_s[row, :]
                now = jnp.maximum(before, jnp.max(s, axis=0, keepdims=True))
                p_s[b, :, columns(h + j)] = jnp.exp(s - now).astype(BF)
                shrinks[h + j] = jnp.exp(before - now)
                m_s[row, :] = now
                mk_s[b, row, :] = now
            if h > 0:
                mix(h - group)
        mix(heads - group)
        return carry

    lax.fori_loop(first_block, end_block, forward, 0)

    for h in range(heads):
        row = slice(h, h + 1)
        inverse = 1.0 / l_s[row, :]
        mixed = o_s[:, columns(h)] * inverse
        mix_t_ref[head(h), :] = mixed.astype(BF)
        d_s[row, :] = jnp.sum(
            mixed * g_t_ref[0, :, columns(h)].astype(F32), axis=0, keepdims=True
        )
        l_s[row, :] = inverse

    def backward(b, carry):
        at = pl.multiple_of(b * KEY_BLOCK, KEY_BLOCK)
        values = kv_s[pl.ds(at, KEY_BLOCK), :][:, head_size:]
        keys_t = kv_t_s[b][:head_size]
        inners = {}

        def prob_grads(h):
            for j in range(group):
                row = slice(h + j, h + j + 1)
                factor = jnp.exp(mk_s[b, row, :] - m_s[row, :]) * l_s[row, :]
                scaled = g_t_ref[0, :, columns(h + j)].astype(F32) * factor
                gk_s[:, columns(h + j)] = scaled.astype(BF)
                inners[h + j] = d_s[row, :] * factor
            return matmul(values, gk_s[:, columns(h, group)])

        ready = prob_grads(0)
        for h in range(0, heads, group):
            now_grads = ready
            if h + group < heads:
                ready = prob_grads(h + group)
            for j in range(group):
                p = p_s[b, :, columns(h + j)].astype(F32)
                ds_s[:, columns(h + j)] = (
                    p * (now_grads[:, columns(j)] - inners.pop(h + j))
                ).astype(BF)
        dq_s[...] += matmul(keys_t, ds_s[...])
        dk = matmul(ds_s[...], q_t_ref[0], NT)
        dv = matmul(p_s[b], gk_s[...], NT)
        dkv_s[pl.ds(at, KEY_BLOCK), :] = jnp.concatenate([dk, dv], axis=1).astype(BF)
        return carry

    lax.fori_loop(first_block, end_block, backward, 0)

    cosine, sine = cos_ref[...], sin_ref[...]
    score_scale = 1.0 / math.sqrt(head_size)
    for h in range(heads):
        qpg_t_ref[head(h), :] = turn(
            dq_s[:, columns(h)] * score_scale, cosine, -sine
        ).astype(BF)
    for m in range(seq_devices):
        ref = (dkeep_ref, dsend_ref)[m % 2]
        at = pl.multiple_of((me ^ m) * length, length)
        ref[m // 2, 0] = dkv_s[pl.ds(at, length), :]


def mix_kernel(
    side_ref, tok_ref, seg_ref, mix_t_ref, qpg_t_ref, attn_t_ref, bg_t_ref, mlp_ref, wo_ref,
    bo_ref, bd_ref, out_ref, keep_ref, send_ref, acc_q, acc_o,
):
    step, steps = pl.program_id(0), pl.num_programs(0)

    @pl.when(step == 0)
    def _():
        acc_q[...] = jnp.zeros_like(acc_q)
        acc_o[...] = jnp.zeros_like(acc_o)

    mix_t = mix_t_ref[...]
    branch = matmul(mix_t, wo_ref[...], TN) + (row_of(bo_ref) + row_of(bd_ref)) + mlp_ref[...]
    valid = valid_column(seg_ref[pl.ds(step, 1), :])
    out_ref[0] = (tok_ref[0].astype(F32) + valid * branch).astype(BF)
    acc_q[...] += matmul(attn_t_ref[...], qpg_t_ref[...], NT)
    acc_o[...] += matmul(bg_t_ref[...], mix_t, NT)

    @pl.when(step == steps - 1)
    def _():
        half = acc_q.shape[0] // 2
        side = side_ref[0]
        mine = pl.ds(pl.multiple_of(side * half, half), half)
        other = pl.ds(pl.multiple_of((1 - side) * half, half), half)
        for j, acc in enumerate((acc_q, acc_o)):
            keep_ref[j] = acc[mine, :].astype(BF)
            send_ref[j] = acc[other, :].astype(BF)


def exit_kernel(
    order_a, rows, permuted,
    side_ref, tok_ref, og_ref, seg_ref, qpg_t_ref, attn_t_ref, din_ref, wq_ref, wkv_ref,
    ag_ref, mg_ref, cos_ref, sin_ref, bupg_ref, shuffle_ref, dkv_refs,
    tg_ref, keep_ref, send_ref, acc, vec,
):
    step, steps = pl.program_id(0), pl.num_programs(0)

    @pl.when(step == 0)
    def _():
        acc[...] = jnp.zeros_like(acc)
        vec[...] = jnp.zeros_like(vec)

    dkv = sum((ref[0].astype(F32) for ref in dkv_refs[1:]), dkv_refs[0][0].astype(F32))
    kvpg_t = turn(dkv.T, cos_ref[...], -sin_ref[...]).astype(BF)
    acc[...] += matmul(attn_t_ref[...], kvpg_t, NT)
    qpg_t = qpg_t_ref[...]
    d_attn = (matmul(wq_ref[...], qpg_t) + matmul(wkv_ref[...], kvpg_t)).T
    d_mlp = din_ref[...]
    n, scale = norm_parts(tok_ref[0].astype(F32))
    og = og_ref[0].astype(F32)
    e = d_attn * row_of(ag_ref) + d_mlp * row_of(mg_ref)
    inner = jnp.mean(e * n, axis=-1, keepdims=True)
    tg_ref[0] = (og + scale * (e - jnp.mean(e, axis=-1, keepdims=True) - n * inner)).astype(BF)
    ones = jnp.ones((8, qpg_t.shape[1]), BF)
    bg = (og * valid_column(seg_ref[pl.ds(step, 1), :])).astype(BF)
    sums = [d_attn * n, d_attn, d_mlp * n, d_mlp, None, bg.astype(F32)]
    for j, value in enumerate(sums):
        if value is None:
            part = matmul(ones, qpg_t, NT)[:1]
        else:
            part = jnp.sum(value, axis=0, keepdims=True)
        vec[j : j + 1, :] += part

    @pl.when(step == steps - 1)
    def _():
        vec[8:12, :] = bupg_ref[...]
        if permuted:
            columns = permute_rows(vec[...].T, order_a, rows)
        else:
            columns = lax.dot_general(
                shuffle_ref[...], vec[...], NT, precision=lax.Precision.HIGHEST,
                preferred_element_type=F32,
            )
        half = columns.shape[0] // 2
        acc_columns = slice(0, LANES)
        vec_columns = slice(LANES, 2 * LANES)
        for side in range(2):

            @pl.when(side_ref[0] == side)
            def _():
                mine = slice(side * half, (side + 1) * half)
                other = slice((1 - side) * half, (2 - side) * half)
                keep_ref[:, acc_columns] = acc[mine, :].astype(BF)
                send_ref[:, acc_columns] = acc[other, :].astype(BF)
                keep_ref[:, vec_columns] = columns[mine].astype(BF)
                send_ref[:, vec_columns] = columns[other].astype(BF)


def partners(size, mask):
    return [(i, i ^ mask) for i in range(size)]


class Stream:
    def __init__(self, arrays, count, resident, width):
        self.terms = [(array, resident, 0, at, ()) for array, at in arrays]
        self.count, self.resident, self.width = count, resident, width
        self.rows = arrays[0][0].shape[1]

    def halve(self, bit):
        count = self.count = self.count // 2
        mine, other = [], []
        for array, resident, column, at, adds in self.terms:
            mine.append((array, resident, column, at, adds + ((bit, count),)))
            other.append((array, resident, column, at + count, adds + ((bit, -count),)))
        self.terms = mine
        return other


def first_block(term, where_ref):
    at = term[3]
    for (axis, bit), weight in term[4]:
        at = at + ((where_ref[axis] >> bit) & 1) * weight
    return at


def term_spec(term, width, group):
    if term[1]:
        return pl.BlockSpec(memory_space=pltpu.VMEM)
    return pl.BlockSpec(
        (group, term[0].shape[1], width),
        lambda i, where_ref: (first_block(term, where_ref) // group + i, 0, term[2]),
    )


def in_hbm(value):
    return pltpu.with_memory_space_constraint(value, pltpu.HBM)


def operands_of(terms):
    return [term[0] if term[1] else in_hbm(term[0]) for term in terms]


def read_terms(terms, refs, width, group, where_ref):
    total = None
    for term, ref in zip(terms, refs):
        if term[1]:
            at = first_block(term, where_ref) + pl.program_id(0) * group
            value = ref[pl.ds(at, group), :, term[2] * width : (term[2] + 1) * width]
        else:
            value = ref[...]
        value = value.astype(F32)
        total = value if total is None else total + value
    return total


def call_on_terms(
    body, name, where, after, steps, in_specs, operands, out_specs, out_shape, length
):
    return pl.pallas_call(
        body,
        grid_spec=pltpu.PrefetchScalarGridSpec(
            num_scalar_prefetch=1, grid=(steps,), in_specs=in_specs, out_specs=out_specs
        ),
        out_shape=out_shape,
        compiler_params=params(limit=24),
        cost_estimate=length,
        name=name,
    )(ordered_after(where, *after), *operands)


def sums_to_send(picks, streams, joined, where, after, length):
    count, width, rows = streams[0].count, streams[0].width, streams[0].rows
    resident = streams[0].resident
    group = count
    while group > 1 and group * width > 4 * 3072 and not resident:
        group //= 2
    terms = [term for pick in picks for term in pick]
    outputs = len(picks) // joined
    shape = (rows, width * joined)

    def body(where_ref, *refs):
        at = 0
        for j, pick in enumerate(picks):
            total = read_terms(pick, refs[at : at + len(pick)], width, group, where_ref).astype(BF)
            column = j % joined
            output = refs[len(terms) + j // joined]
            output[:, :, column * width : (column + 1) * width] = total
            at += len(pick)

    if resident:
        out_spec = pl.BlockSpec(memory_space=pltpu.VMEM)
    else:
        out_spec = pl.BlockSpec((group,) + shape, lambda i, _: (i, 0, 0))
    return call_on_terms(
        body, "combine", where, after, count // group,
        [term_spec(term, width, group) for term in terms],
        operands_of(terms),
        [out_spec] * outputs,
        [jax.ShapeDtypeStruct((count,) + shape, BF)] * outputs,
        length or short(2 * count * rows * width * len(terms)),
    )


def own_sums(streams, where, after=(), length=None):
    terms = [term for stream in streams for term in stream.terms]

    def body(where_ref, *refs):
        at = 0
        for stream, output in zip(streams, refs[len(terms) :]):
            size = len(stream.terms)
            output[...] = read_terms(
                stream.terms, refs[at : at + size], stream.width, 1, where_ref
            )[0]
            at += size

    return call_on_terms(
        body, "own", where, after, 1,
        [term_spec(term, stream.width, 1) for stream in streams for term in stream.terms],
        operands_of(terms),
        [whole((stream.rows, stream.width)) for stream in streams],
        [jax.ShapeDtypeStruct((stream.rows, stream.width), F32) for stream in streams],
        length or short(2 * len(terms) * streams[0].rows * streams[0].width),
    )


def ordered_after(value, *others):
    if not others:
        return value
    return lax.optimization_barrier((value, others))[0]


AXES = ("seq", "batch")


def reduce_level(streams, bits, where, after=(), length=None):
    picks = [stream.halve(bit) for stream, bit in zip(streams, bits)]
    joined = len(set(bits)) == 1
    sends = sums_to_send(picks, streams, len(streams) if joined else 1, where, after, length)
    recvs = []
    for (axis, bit), send in zip(bits, sends):
        recvs.append(
            lax.ppermute(send, AXES[axis], partners(lax.axis_size(AXES[axis]), 1 << bit))
        )
    for j, stream in enumerate(streams):
        column = j if joined else 0
        stream.terms.append((recvs[0 if joined else j], stream.resident, column, 0, ()))
    return sends, recvs


def exchange(streams, bits, where, after=()):
    axis = AXES[bits[0][0]]
    picks, recvs = [], []
    for mask in range(1, 1 << len(bits)):
        for stream in streams:
            count, terms = stream.count, stream.terms
            for j, bit in enumerate(bits):
                count //= 2
                sign, shift = (-1, count) if (mask >> j) & 1 else (1, 0)
                terms = [
                    (a, r, c, at + shift, adds + ((bit, sign * count),))
                    for a, r, c, at, adds in terms
                ]
            picks.append(terms)
    for stream in streams:
        for bit in bits:
            stream.halve(bit)
    sends = sums_to_send(picks, streams, len(streams), where, after, None)
    for mask, send in enumerate(sends, 1):
        partner = sum(((mask >> j) & 1) << bit[1] for j, bit in enumerate(bits))
        recv = lax.ppermute(send, axis, partners(lax.axis_size(axis), partner))
        for column, stream in enumerate(streams):
            stream.terms.append((recv, stream.resident, column, 0, ()))
    return sends


def on_device(
    tokens, segment_ids, attn_gain, attn_shift, mlp_gain, mlp_shift, w_query, b_query,
    w_keyvalue, w_out, b_out, w_up, b_up, w_down, b_down, out_grad,
):
    row_count, length, width = tokens.shape
    head_size = w_keyvalue.shape[1] // 2
    heads = width // head_size
    hidden = w_up.shape[1]
    token_count = row_count * length
    seq_devices = lax.axis_size("seq")
    batch_devices = lax.axis_size("batch")
    devices = seq_devices * batch_devices
    seq_index = lax.axis_index("seq").astype(jnp.int32)
    batch_index = lax.axis_index("batch").astype(jnp.int32)
    side = (seq_index & 1).reshape(1)
    where = jnp.stack([seq_index, batch_index])
    rows = width // devices
    permuted = rows % 8 == 0
    seq_bits = list(range(seq_devices.bit_length() - 1))

    def reversed_bits(value, count):
        return sum(((value >> j) & 1) << (count - 1 - j) for j in range(count))

    batch_order = [
        reversed_bits(z, batch_devices.bit_length() - 1) for z in range(batch_devices)
    ]

    def device_order(bits):
        order = []
        for k in range(seq_devices):
            at = 0
            for j, bit in enumerate(bits):
                at |= ((k >> (len(bits) - 1 - j)) & 1) << bit
            order += [z * seq_devices + at for z in batch_order]
        return order

    order_a = device_order(seq_bits)
    order_b = device_order(seq_bits[:1] + seq_bits[:0:-1])

    def ordered(values, order):
        if permuted:
            return values
        shaped = values.reshape(values.shape[:-2] + (devices, rows, values.shape[-1]))
        return jnp.take(shaped, jnp.array(order), axis=-3).reshape(values.shape)

    positions = (seq_index * length + jnp.arange(length)).astype(F32)
    inverse = 10000.0 ** (-(jnp.arange(HALF_ROT).astype(F32) * (2.0 / ROT_DIMS)))
    angles = inverse[:, None] * positions[None, :]
    cosine, sine = jnp.cos(angles), jnp.sin(angles)
    segments_spec = whole((row_count, length))
    turn_spec = whole((HALF_ROT, length))
    width_spec = whole((width,))

    def row_block(shape, first=0):
        return pl.BlockSpec((1,) + shape, lambda r, *_: (first + r, 0, 0))

    token_block = pl.BlockSpec((length, width), lambda r, *_: (r, 0))
    whole_lanes = length % LANES == 0

    def column_block(first=0):
        if whole_lanes:
            return pl.BlockSpec((width, length), lambda r, *_: (0, first + r))
        return pl.BlockSpec((None, width, length), lambda r, *_: (first + r, 0, 0))

    columns = jax.ShapeDtypeStruct(
        (width, token_count) if whole_lanes else (row_count, width, length), BF
    )

    def joined(values):
        if whole_lanes:
            return values
        return jnp.transpose(values, (1, 0, 2)).reshape(width, token_count)

    lanes = heads * length
    mlp_in, bg, mlp_t, bg_t, attn_t, q_t, g_t, keyvalue, payload = pl.pallas_call(
        functools.partial(entry_kernel, head_size, order_a, order_b, rows, permuted),
        grid=(row_count,),
        in_specs=[
            row_block((length, width)), row_block((length, width)), segments_spec,
            width_spec, width_spec, width_spec, width_spec, width_spec,
            whole((width, width)), whole((width, 2 * head_size)), whole((width, width)),
            turn_spec, turn_spec,
        ],
        out_specs=[
            token_block, token_block, column_block(), column_block(), column_block(),
            row_block((head_size, lanes)), row_block((head_size, lanes)),
            row_block((length, 2 * head_size)), row_block((length + COUNT_ROWS, 2 * head_size)),
        ],
        out_shape=[
            jax.ShapeDtypeStruct((token_count, width), BF),
            jax.ShapeDtypeStruct((token_count, width), BF),
            columns,
            columns,
            columns,
            jax.ShapeDtypeStruct((row_count, head_size, lanes), BF),
            jax.ShapeDtypeStruct((row_count, head_size, lanes), BF),
            jax.ShapeDtypeStruct((row_count, length, 2 * head_size), BF),
            jax.ShapeDtypeStruct((row_count, length + COUNT_ROWS, 2 * head_size), BF),
        ],
        compiler_params=params(60),
        cost_estimate=LONG,
        name="entry",
    )(
        tokens, out_grad, segment_ids, attn_gain, attn_shift, mlp_gain, mlp_shift, b_query,
        w_query, w_keyvalue, w_out, cosine, sine,
    )
    mlp_t, attn_t = ordered(mlp_t, order_a), ordered(attn_t, order_a)
    bg_t = ordered(bg_t, order_b)

    gathered = [payload]
    for mask in range(2, seq_devices, 2):
        gathered.append(lax.ppermute(payload, "seq", partners(seq_devices, mask)))

    tile = math.gcd(512, hidden)
    half = width // 2
    pair_cols = pl.BlockSpec((2, half, tile), lambda f, *_: (0, 0, f))
    pair_shape = jax.ShapeDtypeStruct((2, half, hidden), BF)
    keep, send, mlp_out, mlp_din, b_up_part = pl.pallas_call(
        functools.partial(mlp_kernel, token_count),
        grid_spec=pltpu.PrefetchScalarGridSpec(
            num_scalar_prefetch=1,
            grid=(hidden // tile,),
            in_specs=[
                whole((token_count, width)), whole((token_count, width)),
                whole((width, token_count)), whole((width, token_count)),
                pl.BlockSpec((width, tile), lambda f, *_: (0, f)),
                pl.BlockSpec((1, tile), lambda f, *_: (0, f)),
                pl.BlockSpec((tile, width), lambda f, *_: (f, 0)),
            ],
            out_specs=[
                pair_cols, pair_cols, whole((token_count, width)), whole((token_count, width)),
                pl.BlockSpec((1, tile), lambda f, *_: (0, f)),
            ],
            scratch_shapes=[
                pltpu.VMEM((token_count, tile), BF), pltpu.VMEM((token_count, tile), BF),
            ],
        ),
        out_shape=[
            pair_shape, pair_shape,
            jax.ShapeDtypeStruct((token_count, width), F32),
            jax.ShapeDtypeStruct((token_count, width), F32),
            jax.ShapeDtypeStruct((1, hidden), F32),
        ],
        compiler_params=params(60),
        cost_estimate=LONG,
        name="mlp",
    )(side, mlp_in, bg, joined(mlp_t), joined(bg_t), w_up, b_up.reshape(1, hidden), w_down)

    gathered = ordered_after(tuple(gathered), b_up_part)

    def stack_body(*refs):
        for j, ref in enumerate(refs[:-1]):
            refs[-1][j] = ref[...]

    even = pl.pallas_call(
        stack_body,
        in_specs=[pl.BlockSpec(memory_space=pltpu.VMEM)] * len(gathered),
        out_specs=pl.BlockSpec(memory_space=pltpu.VMEM),
        out_shape=jax.ShapeDtypeStruct((len(gathered),) + payload.shape, BF),
        compiler_params=pltpu.CompilerParams(vmem_limit_bytes=24 * 1024 * 1024),
        cost_estimate=LONGEST,
        name="stack",
    )(*gathered)
    odd = lax.ppermute(even, "seq", partners(seq_devices, 1))

    bits = [(0, bit) for bit in range(1, seq_devices.bit_length() - 1)]
    batch_bits = [(1, bit) for bit in range(batch_devices.bit_length() - 1)]
    blocks = devices // 2

    def pair_streams(keep, send, resident):
        shape = (2 * blocks, rows, keep.shape[2])
        keep = keep.reshape(shape)
        recv = lax.ppermute(send.reshape(shape), "seq", partners(seq_devices, 1))
        return [
            Stream([(keep, at), (recv, at)], blocks, resident, keep.shape[2])
            for at in (0, blocks)
        ]

    mlp_streams = pair_streams(keep, send, False)

    half_seq = seq_devices // 2
    key_blocks = length * seq_devices // KEY_BLOCK
    stat_rows = -(-heads // 8) * 8

    def attention(first, count, after, before):
        kv_rows = pl.BlockSpec(
            (half_seq, 1, length + COUNT_ROWS, 2 * head_size), lambda r, *_: (0, first + r, 0, 0)
        )
        dkv_rows = pl.BlockSpec(
            (half_seq, 1, length, 2 * head_size), lambda r, *_: (0, first + r, 0, 0)
        )
        dkv_shape = jax.ShapeDtypeStruct((half_seq, row_count, length, 2 * head_size), BF)
        return pl.pallas_call(
            functools.partial(attention_kernel, heads, head_size, seq_devices, first),
            grid_spec=pltpu.PrefetchScalarGridSpec(
                num_scalar_prefetch=1,
                grid=(count,),
                in_specs=[
                    segments_spec, row_block((head_size, lanes), first),
                    row_block((head_size, lanes), first), kv_rows, kv_rows, turn_spec, turn_spec,
                ]
                + [pl.BlockSpec(memory_space=pl.ANY)] * len(before),
                out_specs=[column_block(first), column_block(first), dkv_rows, dkv_rows],
                scratch_shapes=[
                    pltpu.VMEM((key_blocks * KEY_BLOCK, 2 * head_size), BF),
                    pltpu.VMEM((key_blocks, 2 * head_size, KEY_BLOCK), BF),
                    pltpu.VMEM((KEY_BLOCK, length), F32),
                    pltpu.VMEM((key_blocks, KEY_BLOCK, lanes), BF),
                    pltpu.VMEM((KEY_BLOCK, lanes), BF),
                    pltpu.VMEM((head_size, lanes), BF),
                    pltpu.VMEM((head_size, lanes), F32),
                    pltpu.VMEM((head_size, lanes), F32),
                    pltpu.VMEM((key_blocks * KEY_BLOCK, 2 * head_size), BF),
                    pltpu.VMEM((stat_rows, length), F32),
                    pltpu.VMEM((stat_rows, length), F32),
                    pltpu.VMEM((stat_rows, length), F32),
                    pltpu.VMEM((key_blocks, stat_rows, length), F32),
                ],
            ),
            out_shape=[columns, columns, dkv_shape, dkv_shape],
            input_output_aliases={8 + j: j for j in range(len(before))},
            compiler_params=params(60),
            cost_estimate=LONG,
        name="attention",
        )(
            ordered_after(where, *after), segment_ids, q_t, g_t, in_hbm(even), in_hbm(odd), cosine,
            sine, *before,
        )

    pair_levels = [(bits[i], bits[-1 - i]) for i in range(len(bits))]
    batch_levels = [(bit, bit) for bit in batch_bits]
    mlp_levels = iter(pair_levels + batch_levels)
    results, first_row = [b_up_part], 0
    last_share = max(row_count // 4, 1)
    for share in (row_count - last_share, last_share):
        after = results[:1] if first_row else [even]
        after, _ = reduce_level(mlp_streams, next(mlp_levels), where, after, LONG)
        results = attention(first_row, share, after, results if first_row else [])
        first_row += share
    mix_t, qpg_t, dkv_keep, dkv_send = results
    dkv_recv = lax.ppermute(dkv_send, "seq", partners(seq_devices, 1))
    after, mlp_recv = reduce_level(mlp_streams, next(mlp_levels), where, [mix_t], LONG)

    dkv_recv = ordered_after(dkv_recv, *after)
    dkv_low = (dkv_keep.astype(F32) + dkv_recv.astype(F32)).astype(BF)
    dkv_parts = [dkv_low[0]]
    for j in range(1, half_seq):
        dkv_parts.append(lax.ppermute(dkv_low[j], "seq", partners(seq_devices, 2 * j)))

    pair_spec = pl.BlockSpec(memory_space=pltpu.VMEM)
    pair_width = jax.ShapeDtypeStruct((2, half, width), BF)
    output, keep, send = pl.pallas_call(
        mix_kernel,
        grid_spec=pltpu.PrefetchScalarGridSpec(
            num_scalar_prefetch=1,
            grid=(row_count,),
            in_specs=[
                row_block((length, width)), segments_spec, column_block(), column_block(),
                column_block(), column_block(), token_block, whole((width, width)),
                width_spec, width_spec,
            ],
            out_specs=[row_block((length, width)), pair_spec, pair_spec],
            scratch_shapes=[pltpu.VMEM((width, width), F32), pltpu.VMEM((width, width), F32)],
        ),
        out_shape=[
            jax.ShapeDtypeStruct((row_count, length, width), BF), pair_width, pair_width,
        ],
        compiler_params=params(56),
        cost_estimate=LONG,
        name="mix",
    )(
        ordered_after(side, dkv_parts[0]), tokens, segment_ids, mix_t, qpg_t, attn_t, bg_t,
        mlp_out, w_out, b_out, b_down,
    )
    mix_streams = pair_streams(keep, send, True)
    after = [keep, *mlp_recv, *dkv_parts[1:]]
    after, _ = reduce_level(mlp_streams, next(mlp_levels), where, after, LONG)
    after, _ = reduce_level(mix_streams, pair_levels[0], where, after)

    dkv_count = len(dkv_parts)

    def exit_body(*refs):
        fixed, rest = refs[:15], refs[15:]
        exit_kernel(order_a, rows, permuted, *fixed, rest[:dkv_count], *rest[dkv_count:])

    if permuted:
        shuffle = jnp.zeros((8, LANES), F32)
    else:
        places = (jnp.array(order_a)[:, None] * rows + jnp.arange(rows)[None, :]).reshape(width, 1)
        shuffle = (places == jnp.arange(width)[None, :]).astype(F32)
    extra_spec = pl.BlockSpec(memory_space=pltpu.VMEM)
    extra_shape = jax.ShapeDtypeStruct((half, 2 * LANES), BF)
    tokens_grad, keep, send = pl.pallas_call(
        exit_body,
        grid_spec=pltpu.PrefetchScalarGridSpec(
            num_scalar_prefetch=1,
            grid=(row_count,),
            in_specs=[
                row_block((length, width)), row_block((length, width)), segments_spec,
                column_block(), column_block(), token_block, whole((width, width)),
                whole((width, 2 * head_size)), width_spec, width_spec, turn_spec, turn_spec,
                whole((hidden // width, width)), whole(shuffle.shape),
            ]
            + [row_block((length, 2 * head_size))] * dkv_count,
            out_specs=[row_block((length, width)), extra_spec, extra_spec],
            scratch_shapes=[
                pltpu.VMEM((width, 2 * head_size), F32), pltpu.VMEM((LANES, width), F32),
            ],
        ),
        out_shape=[
            jax.ShapeDtypeStruct((row_count, length, width), BF), extra_shape, extra_shape,
        ],
        compiler_params=params(56),
        cost_estimate=LONG,
        name="exit",
    )(
        ordered_after(side, *after), tokens, out_grad, segment_ids, qpg_t, attn_t, mlp_din, w_query, w_keyvalue,
        attn_gain, mlp_gain, cosine, sine, b_up_part.reshape(width, hidden // width).T, shuffle,
        *dkv_parts,
    )

    shape = (blocks, rows, 2 * LANES)
    keep = keep.reshape(shape)
    recv = lax.ppermute(send.reshape(shape), "seq", partners(seq_devices, 1))
    extra_streams = [Stream([(keep, 0), (recv, 0)], blocks, True, 2 * LANES)]
    after = [keep]
    for level in pair_levels[1:]:
        after, _ = reduce_level(mix_streams, level, where, after)
    after = exchange(extra_streams, bits, where, after)[:1]
    for level in batch_levels[:-1]:
        after, _ = reduce_level(mix_streams, level, where, after)
    for level in mlp_levels:
        after, _ = reduce_level(mlp_streams, level, where, after)
    mlp_sums = own_sums(mlp_streams, where, after, LONG)
    after = exchange(extra_streams, batch_bits, where, mlp_sums[:1])[:1]
    for level in batch_levels[-1:]:
        after, _ = reduce_level(mix_streams, level, where, after)
    extra_sums = own_sums(extra_streams, where, after)
    sums = mlp_sums + own_sums(mix_streams, where, extra_sums) + extra_sums
    w_up_grad, w_down_grad_t, w_query_grad, w_out_grad_t, extra = sums
    vectors = extra[:, LANES:]
    return (
        output,
        keyvalue,
        tokens_grad,
        vectors[:, 0],
        vectors[:, 1],
        vectors[:, 2],
        vectors[:, 3],
        w_query_grad,
        vectors[:, 4],
        extra[:, :LANES],
        w_out_grad_t.T,
        vectors[:, 5],
        w_up_grad,
        vectors[:, 8 : 8 + hidden // width].reshape(-1),
        w_down_grad_t.T,
        vectors[:, 5],
    )


def solution(mesh):
    row_spec = P("batch", "seq", None)
    split = P(("batch", "seq"))
    first = P(("batch", "seq"), None)
    last = P(None, ("batch", "seq"))
    return jax.shard_map(
        on_device,
        mesh=mesh,
        in_specs=(row_spec, P("batch", "seq")) + (P(),) * 13 + (row_spec,),
        out_specs=(
            row_spec, row_spec, row_spec, split, split, split, split, first, split, first, last,
            split, first, split, last, split,
        ),
        check_vma=False,
    )
```

```python
import functools
import math

import jax
import jax.numpy as jnp
from jax import lax
from jax.experimental import pallas as pl
from jax.experimental.pallas import tpu as pltpu
from jax.sharding import PartitionSpec as P

ROT_DIMS = 16
HALF_ROT = ROT_DIMS // 2
DOCS = 6
EPSILON = 1e-05
KEY_BLOCK = 256
COUNT_ROWS = 16
LANES = 128
NEGATIVE = -1e30
BF = jnp.bfloat16
F32 = jnp.float32
NN = (((1,), (0,)), ((), ()))
NT = (((1,), (1,)), ((), ()))
TN = (((0,), (0,)), ((), ()))


def matmul(left, right, dims=NN):
    return lax.dot_general(left, right, dims, preferred_element_type=F32)


def params(limit):
    return pltpu.CompilerParams(
        dimension_semantics=("arbitrary",), vmem_limit_bytes=limit * 1024 * 1024
    )


LONG = pl.CostEstimate(flops=4 * 10**10, transcendentals=0, bytes_accessed=10**7)

LONGEST = pl.CostEstimate(flops=3 * 10**11, transcendentals=0, bytes_accessed=10**7)


def short(size):
    return pl.CostEstimate(flops=0, transcendentals=0, bytes_accessed=size)


def whole(shape):
    return pl.BlockSpec(shape, lambda *_: (0,) * len(shape))


def permute_rows(values, order, rows):
    return jnp.concatenate([values[b * rows : (b + 1) * rows] for b in order], axis=0)


def row_of(ref):
    return ref[...].astype(F32).reshape(1, ref.shape[0])


def valid_column(segment_row):
    length = segment_row.shape[-1]
    row = jnp.broadcast_to((segment_row >= 0).astype(F32), (LANES, length))
    return row.T[:, :1]


def norm_parts(values):
    center = values - jnp.mean(values, axis=-1, keepdims=True)
    spread = jnp.mean(center * center, axis=-1, keepdims=True)
    scale = lax.rsqrt(spread + EPSILON)
    return center * scale, scale


def turn(values, cosine, sine):
    leading = values[:HALF_ROT]
    trailing = values[HALF_ROT:ROT_DIMS]
    return jnp.concatenate(
        [leading * cosine - trailing * sine, trailing * cosine + leading * sine, values[ROT_DIMS:]],
        axis=0,
    )


def entry_kernel(
    head_size, order_a, order_b, rows, permuted,
    tok_ref, og_ref, seg_ref, ag_ref, as_ref, mg_ref, ms_ref, bq_ref, wq_ref, wkv_ref, wo_ref,
    cos_ref, sin_ref, mlp_ref, bg_ref, mlp_t_ref, bg_t_ref, attn_t_ref, q_t_ref, g_t_ref, kv_ref, pay_ref,
):
    x = tok_ref[0].astype(F32)
    length, width = x.shape
    n, _ = norm_parts(x)
    attn_in = (n * row_of(ag_ref) + row_of(as_ref)).astype(BF)
    mlp_in = (n * row_of(mg_ref) + row_of(ms_ref)).astype(BF)
    segments = seg_ref[pl.ds(pl.program_id(0), 1), :]
    bg = (og_ref[0].astype(F32) * valid_column(segments)).astype(BF)
    mlp_ref[...] = mlp_in
    bg_ref[...] = bg

    def turned(values, order):
        flipped = values.astype(F32).T
        if permuted:
            flipped = permute_rows(flipped, order, rows)
        return flipped.astype(BF)

    mlp_t_ref[...] = turned(mlp_in, order_a)
    attn_t_ref[...] = turned(attn_in, order_a)
    bg_t_ref[...] = turned(bg, order_b)

    cosine, sine = cos_ref[...], sin_ref[...]
    score_scale = 1.0 / math.sqrt(head_size)
    query_t = (matmul(attn_in, wq_ref[...]) + row_of(bq_ref)).T
    grad_t = matmul(wo_ref[...], bg, NT)
    for h in range(width // head_size):
        part = query_t[h * head_size : (h + 1) * head_size]
        q_t_ref[0, :, h * length : (h + 1) * length] = (
            turn(part, cosine, sine) * score_scale
        ).astype(BF)
        g_t_ref[0, :, h * length : (h + 1) * length] = grad_t[
            h * head_size : (h + 1) * head_size
        ].astype(BF)
    kv_t = matmul(attn_in, wkv_ref[...]).T
    kv = turn(kv_t, cosine, sine).T.astype(BF)
    kv_ref[0] = kv
    pay_ref[0, :length] = kv
    lane = lax.broadcasted_iota(jnp.int32, (1, LANES), 1)
    counts = jnp.zeros((1, LANES), F32)
    for c in range(DOCS):
        total = jnp.sum((segments == c).astype(F32), axis=1, keepdims=True)
        counts = counts + jnp.where(lane == c, total, 0.0)
    pay_ref[0, length:] = jnp.broadcast_to(counts, (COUNT_ROWS, LANES)).astype(BF)


def gelu_parts(hidden):
    cdf = 0.5 * (1.0 + lax.erf(hidden * math.sqrt(0.5)))
    bell = jnp.exp(-0.5 * (hidden * hidden)) * (1.0 / math.sqrt(2 * math.pi))
    return hidden * cdf, cdf + hidden * bell


def mlp_kernel(
    chunk, side_ref, mlp_ref, bg_ref, mlp_t_ref, bg_t_ref, up_ref, bup_ref, down_ref,
    keep_ref, send_ref, out_ref, din_ref, bupg_ref, act_s, hg_s,
):
    tokens, width = mlp_ref.shape

    @pl.when(pl.program_id(0) == 0)
    def _():
        out_ref[...] = jnp.zeros_like(out_ref)
        din_ref[...] = jnp.zeros_like(din_ref)

    bupg_ref[...] = jnp.zeros_like(bupg_ref)
    bias = bup_ref[...].astype(F32)

    def step(i, carry):
        at = pl.ds(pl.multiple_of(i * chunk, chunk), chunk)
        hidden = matmul(mlp_ref[at, :], up_ref[...]) + bias
        back = matmul(bg_ref[at, :], down_ref[...], NT)
        act, slope = gelu_parts(hidden)
        act = act.astype(BF)
        hg = (back * slope).astype(BF)
        act_s[at, :] = act
        hg_s[at, :] = hg
        bupg_ref[...] += jnp.sum(hg.astype(F32), axis=0, keepdims=True)
        out_ref[at, :] += matmul(act, down_ref[...])
        din_ref[at, :] += matmul(hg, up_ref[...], NT)
        return carry

    lax.fori_loop(0, tokens // chunk, step, 0)
    half = width // 2
    side = side_ref[0]
    mine = pl.ds(pl.multiple_of(side * half, half), half)
    other = pl.ds(pl.multiple_of((1 - side) * half, half), half)
    send_ref[0] = matmul(mlp_t_ref[other, :], hg_s[...]).astype(BF)
    send_ref[1] = matmul(bg_t_ref[other, :], act_s[...]).astype(BF)
    keep_ref[0] = matmul(mlp_t_ref[mine, :], hg_s[...]).astype(BF)
    keep_ref[1] = matmul(bg_t_ref[mine, :], act_s[...]).astype(BF)


def attention_kernel(
    heads, head_size, seq_devices, first_row, where_ref, seg_ref, q_t_ref, g_t_ref, even_ref,
    odd_ref, cos_ref, sin_ref, *refs,
):
    (mix_t_ref, qpg_t_ref, dkeep_ref, dsend_ref, kv_s, kv_t_s, bias_s, p_s, ds_s, gk_s, o_s, dq_s,
     dkv_s, m_s, l_s, d_s, mk_s) = refs[-17:]
    length = seg_ref.shape[-1]
    me = where_ref[0]
    start = me * length
    group = math.gcd(heads, 3)

    def columns(h, count=1):
        return slice(h * length, (h + count) * length)

    def head(h):
        return slice(h * head_size, (h + 1) * head_size)

    counts = jnp.zeros((1, LANES), F32)
    for m in range(seq_devices):
        ref = (even_ref, odd_ref)[m % 2]
        at = pl.multiple_of((me ^ m) * length, length)
        kv_s[pl.ds(at, length), :] = ref[m // 2, 0, :length]
        counts = counts + ref[m // 2, 0, length : length + COUNT_ROWS].astype(F32)[:1]

    segments = seg_ref[pl.ds(first_row + pl.program_id(0), 1), :]
    low = jnp.zeros((1, length), F32)
    for c in range(DOCS):
        later = (segments > c) | (segments < 0)
        low = low + jnp.where(later, counts[:, c : c + 1], 0.0)
    low = low.astype(jnp.int32)
    first_block = jnp.min(low) // KEY_BLOCK
    end_block = (start + length - 1) // KEY_BLOCK + 1
    place = start + lax.broadcasted_iota(jnp.int32, (1, length), 1)

    m_s[...] = jnp.full_like(m_s, NEGATIVE)
    l_s[...] = jnp.zeros_like(l_s)
    o_s[...] = jnp.zeros_like(o_s)
    dq_s[...] = jnp.zeros_like(dq_s)
    dkv_s[...] = jnp.zeros_like(dkv_s)

    def forward(b, carry):
        at = pl.multiple_of(b * KEY_BLOCK, KEY_BLOCK)
        kv = kv_s[pl.ds(at, KEY_BLOCK), :]
        keys = kv[:, :head_size]
        kv_t = kv.astype(F32).T.astype(BF)
        kv_t_s[b] = kv_t
        summed = jnp.concatenate([kv_t[head_size:], jnp.ones((16, KEY_BLOCK), BF)], axis=0)
        key_place = at + lax.broadcasted_iota(jnp.int32, (KEY_BLOCK, length), 0)
        allowed = (key_place <= place) & (key_place >= low)
        bias_s[...] = jnp.where(allowed, 0.0, NEGATIVE)
        bias = bias_s[...]
        shrinks = {}

        def scores(h):
            return matmul(keys, q_t_ref[0, :, columns(h, group)])

        def mix(h):
            o = matmul(summed, p_s[b, :, columns(h, group)])
            for j in range(group):
                row = slice(h + j, h + j + 1)
                part = o[:, columns(j)]
                shrink = shrinks.pop(h + j)
                o_s[:, columns(h + j)] = o_s[:, columns(h + j)] * shrink + part[:head_size]
                l_s[row, :] = l_s[row, :] * shrink + part[head_size : head_size + 1]

        ready = scores(0)
        for h in range(0, heads, group):
            now_scores = ready
            if h + group < heads:
                ready = scores(h + group)
            for j in range(group):
                row = slice(h + j, h + j + 1)
                s = now_scores[:, columns(j)] + bias
                before = m_s[row, :]
                now = jnp.maximum(before, jnp.max(s, axis=0, keepdims=True))
                p_s[b, :, columns(h + j)] = jnp.exp(s - now).astype(BF)
                shrinks[h + j] = jnp.exp(before - now)
                m_s[row, :] = now
                mk_s[b, row, :] = now
            if h > 0:
                mix(h - group)
        mix(heads - group)
        return carry

    lax.fori_loop(first_block, end_block, forward, 0)

    for h in range(heads):
        row = slice(h, h + 1)
        inverse = 1.0 / l_s[row, :]
        mixed = o_s[:, columns(h)] * inverse
        mix_t_ref[head(h), :] = mixed.astype(BF)
        d_s[row, :] = jnp.sum(
            mixed * g_t_ref[0, :, columns(h)].astype(F32), axis=0, keepdims=True
        )
        l_s[row, :] = inverse

    def backward(b, carry):
        at = pl.multiple_of(b * KEY_BLOCK, KEY_BLOCK)
        values = kv_s[pl.ds(at, KEY_BLOCK), :][:, head_size:]
        keys_t = kv_t_s[b][:head_size]
        inners = {}

        def prob_grads(h):
            for j in range(group):
                row = slice(h + j, h + j + 1)
                factor = jnp.exp(mk_s[b, row, :] - m_s[row, :]) * l_s[row, :]
                scaled = g_t_ref[0, :, columns(h + j)].astype(F32) * factor
                gk_s[:, columns(h + j)] = scaled.astype(BF)
                inners[h + j] = d_s[row, :] * factor
            return matmul(values, gk_s[:, columns(h, group)])

        ready = prob_grads(0)
        for h in range(0, heads, group):
            now_grads = ready
            if h + group < heads:
                ready = prob_grads(h + group)
            for j in range(group):
                p = p_s[b, :, columns(h + j)].astype(F32)
                ds_s[:, columns(h + j)] = (
                    p * (now_grads[:, columns(j)] - inners.pop(h + j))
                ).astype(BF)
        dq_s[...] += matmul(keys_t, ds_s[...])
        dk = matmul(ds_s[...], q_t_ref[0], NT)
        dv = matmul(p_s[b], gk_s[...], NT)
        dkv_s[pl.ds(at, KEY_BLOCK), :] = jnp.concatenate([dk, dv], axis=1).astype(BF)
        return carry

    lax.fori_loop(first_block, end_block, backward, 0)

    cosine, sine = cos_ref[...], sin_ref[...]
    score_scale = 1.0 / math.sqrt(head_size)
    for h in range(heads):
        qpg_t_ref[head(h), :] = turn(
            dq_s[:, columns(h)] * score_scale, cosine, -sine
        ).astype(BF)
    for m in range(seq_devices):
        ref = (dkeep_ref, dsend_ref)[m % 2]
        at = pl.multiple_of((me ^ m) * length, length)
        ref[m // 2, 0] = dkv_s[pl.ds(at, length), :]


def mix_kernel(
    side_ref, tok_ref, seg_ref, mix_t_ref, qpg_t_ref, attn_t_ref, bg_t_ref, mlp_ref, wo_ref,
    bo_ref, bd_ref, out_ref, keep_ref, send_ref, acc_q, acc_o,
):
    step, steps = pl.program_id(0), pl.num_programs(0)

    @pl.when(step == 0)
    def _():
        acc_q[...] = jnp.zeros_like(acc_q)
        acc_o[...] = jnp.zeros_like(acc_o)

    mix_t = mix_t_ref[...]
    branch = matmul(mix_t, wo_ref[...], TN) + (row_of(bo_ref) + row_of(bd_ref)) + mlp_ref[...]
    valid = valid_column(seg_ref[pl.ds(step, 1), :])
    out_ref[0] = (tok_ref[0].astype(F32) + valid * branch).astype(BF)
    acc_q[...] += matmul(attn_t_ref[...], qpg_t_ref[...], NT)
    acc_o[...] += matmul(bg_t_ref[...], mix_t, NT)

    @pl.when(step == steps - 1)
    def _():
        half = acc_q.shape[0] // 2
        side = side_ref[0]
        mine = pl.ds(pl.multiple_of(side * half, half), half)
        other = pl.ds(pl.multiple_of((1 - side) * half, half), half)
        for j, acc in enumerate((acc_q, acc_o)):
            keep_ref[j] = acc[mine, :].astype(BF)
            send_ref[j] = acc[other, :].astype(BF)


def exit_kernel(
    order_a, rows, permuted,
    side_ref, tok_ref, og_ref, seg_ref, qpg_t_ref, attn_t_ref, din_ref, wq_ref, wkv_ref,
    ag_ref, mg_ref, cos_ref, sin_ref, bupg_ref, shuffle_ref, dkv_refs,
    tg_ref, keep_ref, send_ref, acc, vec,
):
    step, steps = pl.program_id(0), pl.num_programs(0)

    @pl.when(step == 0)
    def _():
        acc[...] = jnp.zeros_like(acc)
        vec[...] = jnp.zeros_like(vec)

    dkv = sum((ref[0].astype(F32) for ref in dkv_refs[1:]), dkv_refs[0][0].astype(F32))
    kvpg_t = turn(dkv.T, cos_ref[...], -sin_ref[...]).astype(BF)
    acc[...] += matmul(attn_t_ref[...], kvpg_t, NT)
    qpg_t = qpg_t_ref[...]
    d_attn = (matmul(wq_ref[...], qpg_t) + matmul(wkv_ref[...], kvpg_t)).T
    d_mlp = din_ref[...]
    n, scale = norm_parts(tok_ref[0].astype(F32))
    og = og_ref[0].astype(F32)
    e = d_attn * row_of(ag_ref) + d_mlp * row_of(mg_ref)
    inner = jnp.mean(e * n, axis=-1, keepdims=True)
    tg_ref[0] = (og + scale * (e - jnp.mean(e, axis=-1, keepdims=True) - n * inner)).astype(BF)
    ones = jnp.ones((8, qpg_t.shape[1]), BF)
    bg = (og * valid_column(seg_ref[pl.ds(step, 1), :])).astype(BF)
    sums = [d_attn * n, d_attn, d_mlp * n, d_mlp, None, bg.astype(F32)]
    for j, value in enumerate(sums):
        if value is None:
            part = matmul(ones, qpg_t, NT)[:1]
        else:
            part = jnp.sum(value, axis=0, keepdims=True)
        vec[j : j + 1, :] += part

    @pl.when(step == steps - 1)
    def _():
        vec[8:12, :] = bupg_ref[...]
        if permuted:
            columns = permute_rows(vec[...].T, order_a, rows)
        else:
            columns = lax.dot_general(
                shuffle_ref[...], vec[...], NT, precision=lax.Precision.HIGHEST,
                preferred_element_type=F32,
            )
        half = columns.shape[0] // 2
        acc_columns = slice(0, LANES)
        vec_columns = slice(LANES, 2 * LANES)
        for side in range(2):

            @pl.when(side_ref[0] == side)
            def _():
                mine = slice(side * half, (side + 1) * half)
                other = slice((1 - side) * half, (2 - side) * half)
                keep_ref[:, acc_columns] = acc[mine, :].astype(BF)
                send_ref[:, acc_columns] = acc[other, :].astype(BF)
                keep_ref[:, vec_columns] = columns[mine].astype(BF)
                send_ref[:, vec_columns] = columns[other].astype(BF)


def partners(size, mask):
    return [(i, i ^ mask) for i in range(size)]


class Stream:
    def __init__(self, arrays, count, resident, width):
        self.terms = [(array, resident, 0, at, ()) for array, at in arrays]
        self.count, self.resident, self.width = count, resident, width
        self.rows = arrays[0][0].shape[1]

    def halve(self, bit):
        count = self.count = self.count // 2
        mine, other = [], []
        for array, resident, column, at, adds in self.terms:
            mine.append((array, resident, column, at, adds + ((bit, count),)))
            other.append((array, resident, column, at + count, adds + ((bit, -count),)))
        self.terms = mine
        return other


def first_block(term, where_ref):
    at = term[3]
    for (axis, bit), weight in term[4]:
        at = at + ((where_ref[axis] >> bit) & 1) * weight
    return at


def term_spec(term, width, group):
    if term[1]:
        return pl.BlockSpec(memory_space=pltpu.VMEM)
    return pl.BlockSpec(
        (group, term[0].shape[1], width),
        lambda i, where_ref: (first_block(term, where_ref) // group + i, 0, term[2] // width),
    )


def in_hbm(value):
    return pltpu.with_memory_space_constraint(value, pltpu.HBM)


def operands_of(terms):
    return [term[0] if term[1] else in_hbm(term[0]) for term in terms]


def read_terms(terms, refs, width, group, where_ref):
    total = None
    for term, ref in zip(terms, refs):
        if term[1]:
            at = first_block(term, where_ref) + pl.program_id(0) * group
            value = ref[pl.ds(at, group), :, term[2] : term[2] + width]
        else:
            value = ref[...]
        value = value.astype(F32)
        total = value if total is None else total + value
    return total


def call_on_terms(
    body, name, where, after, steps, in_specs, operands, out_specs, out_shape, length
):
    return pl.pallas_call(
        body,
        grid_spec=pltpu.PrefetchScalarGridSpec(
            num_scalar_prefetch=1, grid=(steps,), in_specs=in_specs, out_specs=out_specs
        ),
        out_shape=out_shape,
        compiler_params=params(limit=24),
        cost_estimate=length,
        name=name,
    )(ordered_after(where, *after), *operands)


def sums_to_send(picks, streams, joined, where, after, length):
    count, rows, resident = streams[0].count, streams[0].rows, streams[0].resident
    widths = [streams[j % len(streams)].width for j in range(len(picks))]
    group = count
    while group > 1 and group * widths[0] > 4 * 3072 and not resident:
        group //= 2
    terms = [term for pick in picks for term in pick]
    outputs = len(picks) // joined
    shapes = [(rows, sum(widths[j * joined : (j + 1) * joined])) for j in range(outputs)]

    def body(where_ref, *refs):
        at = 0
        for j, (pick, width) in enumerate(zip(picks, widths)):
            total = read_terms(pick, refs[at : at + len(pick)], width, group, where_ref).astype(BF)
            column = sum(widths[j - j % joined : j])
            refs[len(terms) + j // joined][:, :, column : column + width] = total
            at += len(pick)

    if resident:
        out_specs = [pl.BlockSpec(memory_space=pltpu.VMEM) for _ in shapes]
    else:
        out_specs = [pl.BlockSpec((group,) + shape, lambda i, _: (i, 0, 0)) for shape in shapes]
    return call_on_terms(
        body, "combine", where, after, count // group,
        [term_spec(term, width, group) for pick, width in zip(picks, widths) for term in pick],
        operands_of(terms),
        out_specs,
        [jax.ShapeDtypeStruct((count,) + shape, BF) for shape in shapes],
        length or short(2 * count * rows * sum(len(p) * w for p, w in zip(picks, widths))),
    )


def own_sums(streams, where, after=(), length=None, vectors=()):
    terms = [term for stream in streams for term in stream.terms]
    shapes = [(stream.rows, stream.width) for stream in streams]
    if vectors:
        shapes[-1] = (shapes[-1][0], shapes[-1][1] - LANES)
        shapes += [(streams[-1].rows,)] * len(vectors)

    def body(where_ref, *refs):
        at = 0
        for stream, output in zip(streams, refs[len(terms) :]):
            size = len(stream.terms)
            total = read_terms(stream.terms, refs[at : at + size], stream.width, 1, where_ref)[0]
            output[...] = total[:, : output.shape[1]]
            at += size
        if vectors:
            turned = total[:, -LANES:].T
            for row, output in zip(vectors, refs[len(terms) + len(streams) :]):
                output[...] = turned[row : row + 1].reshape(output.shape)

    return call_on_terms(
        body, "own", where, after, 1,
        [term_spec(term, stream.width, 1) for stream in streams for term in stream.terms],
        operands_of(terms),
        [whole(shape) for shape in shapes],
        [jax.ShapeDtypeStruct(shape, F32) for shape in shapes],
        length or short(2 * len(terms) * streams[0].rows * streams[0].width),
    )


def ordered_after(value, *others):
    if not others:
        return value
    return lax.optimization_barrier((value, others))[0]


AXES = ("seq", "batch")


def reduce_level(streams, bits, where, after=(), length=None):
    picks = [stream.halve(bit) for stream, bit in zip(streams, bits)]
    joined = len(set(bits)) == 1
    sends = sums_to_send(picks, streams, len(streams) if joined else 1, where, after, length)
    recvs = []
    for (axis, bit), send in zip(bits, sends):
        recvs.append(
            lax.ppermute(send, AXES[axis], partners(lax.axis_size(AXES[axis]), 1 << bit))
        )
    for j, stream in enumerate(streams):
        column = j * stream.width if joined else 0
        resident = stream.resident or stream.count <= 4
        stream.terms.append((recvs[0 if joined else j], resident, column, 0, ()))
    return sends, recvs


def exchange(streams, bits, where, after=()):
    axis = AXES[bits[0][0]]
    picks, recvs = [], []
    for mask in range(1, 1 << len(bits)):
        for stream in streams:
            count, terms = stream.count, stream.terms
            for j, bit in enumerate(bits):
                count //= 2
                sign, shift = (-1, count) if (mask >> j) & 1 else (1, 0)
                terms = [
                    (a, r, c, at + shift, adds + ((bit, sign * count),))
                    for a, r, c, at, adds in terms
                ]
            picks.append(terms)
    for stream in streams:
        for bit in bits:
            stream.halve(bit)
    sends = sums_to_send(picks, streams, len(streams), where, after, None)
    for mask, send in enumerate(sends, 1):
        partner = sum(((mask >> j) & 1) << bit[1] for j, bit in enumerate(bits))
        recv = lax.ppermute(send, axis, partners(lax.axis_size(axis), partner))
        column = 0
        for stream in streams:
            stream.terms.append((recv, stream.resident, column, 0, ()))
            column += stream.width
    return sends


def on_device(
    tokens, segment_ids, attn_gain, attn_shift, mlp_gain, mlp_shift, w_query, b_query,
    w_keyvalue, w_out, b_out, w_up, b_up, w_down, b_down, out_grad,
):
    row_count, length, width = tokens.shape
    head_size = w_keyvalue.shape[1] // 2
    heads = width // head_size
    hidden = w_up.shape[1]
    token_count = row_count * length
    seq_devices = lax.axis_size("seq")
    batch_devices = lax.axis_size("batch")
    devices = seq_devices * batch_devices
    seq_index = lax.axis_index("seq").astype(jnp.int32)
    batch_index = lax.axis_index("batch").astype(jnp.int32)
    side = (seq_index & 1).reshape(1)
    where = jnp.stack([seq_index, batch_index])
    rows = width // devices
    permuted = rows % 8 == 0
    seq_bits = list(range(seq_devices.bit_length() - 1))

    def reversed_bits(value, count):
        return sum(((value >> j) & 1) << (count - 1 - j) for j in range(count))

    batch_order = [
        reversed_bits(z, batch_devices.bit_length() - 1) for z in range(batch_devices)
    ]

    def device_order(bits):
        order = []
        for k in range(seq_devices):
            at = 0
            for j, bit in enumerate(bits):
                at |= ((k >> (len(bits) - 1 - j)) & 1) << bit
            order += [z * seq_devices + at for z in batch_order]
        return order

    order_a = device_order(seq_bits)
    order_b = device_order(seq_bits[:1] + seq_bits[:0:-1])

    def ordered(values, order):
        if permuted:
            return values
        shaped = values.reshape(values.shape[:-2] + (devices, rows, values.shape[-1]))
        return jnp.take(shaped, jnp.array(order), axis=-3).reshape(values.shape)

    positions = (seq_index * length + jnp.arange(length)).astype(F32)
    inverse = 10000.0 ** (-(jnp.arange(HALF_ROT).astype(F32) * (2.0 / ROT_DIMS)))
    angles = inverse[:, None] * positions[None, :]
    cosine, sine = jnp.cos(angles), jnp.sin(angles)
    segments_spec = whole((row_count, length))
    turn_spec = whole((HALF_ROT, length))
    width_spec = whole((width,))

    def row_block(shape, first=0):
        return pl.BlockSpec((1,) + shape, lambda r, *_: (first + r, 0, 0))

    token_block = pl.BlockSpec((length, width), lambda r, *_: (r, 0))
    whole_lanes = length % LANES == 0

    def column_block(first=0):
        if whole_lanes:
            return pl.BlockSpec((width, length), lambda r, *_: (0, first + r))
        return pl.BlockSpec((None, width, length), lambda r, *_: (first + r, 0, 0))

    columns = jax.ShapeDtypeStruct(
        (width, token_count) if whole_lanes else (row_count, width, length), BF
    )

    def joined(values):
        if whole_lanes:
            return values
        return jnp.transpose(values, (1, 0, 2)).reshape(width, token_count)

    lanes = heads * length
    mlp_in, bg, mlp_t, bg_t, attn_t, q_t, g_t, keyvalue, payload = pl.pallas_call(
        functools.partial(entry_kernel, head_size, order_a, order_b, rows, permuted),
        grid=(row_count,),
        in_specs=[
            row_block((length, width)), row_block((length, width)), segments_spec,
            width_spec, width_spec, width_spec, width_spec, width_spec,
            whole((width, width)), whole((width, 2 * head_size)), whole((width, width)),
            turn_spec, turn_spec,
        ],
        out_specs=[
            token_block, token_block, column_block(), column_block(), column_block(),
            row_block((head_size, lanes)), row_block((head_size, lanes)),
            row_block((length, 2 * head_size)), row_block((length + COUNT_ROWS, 2 * head_size)),
        ],
        out_shape=[
            jax.ShapeDtypeStruct((token_count, width), BF),
            jax.ShapeDtypeStruct((token_count, width), BF),
            columns,
            columns,
            columns,
            jax.ShapeDtypeStruct((row_count, head_size, lanes), BF),
            jax.ShapeDtypeStruct((row_count, head_size, lanes), BF),
            jax.ShapeDtypeStruct((row_count, length, 2 * head_size), BF),
            jax.ShapeDtypeStruct((row_count, length + COUNT_ROWS, 2 * head_size), BF),
        ],
        compiler_params=params(60),
        cost_estimate=LONG,
        name="entry",
    )(
        tokens, out_grad, segment_ids, attn_gain, attn_shift, mlp_gain, mlp_shift, b_query,
        w_query, w_keyvalue, w_out, cosine, sine,
    )
    mlp_t, attn_t = ordered(mlp_t, order_a), ordered(attn_t, order_a)
    bg_t = ordered(bg_t, order_b)

    gathered = [payload]
    for mask in range(2, seq_devices, 2):
        gathered.append(lax.ppermute(payload, "seq", partners(seq_devices, mask)))

    tile = math.gcd(512, hidden)
    half = width // 2
    pair_cols = pl.BlockSpec((2, half, tile), lambda f, *_: (0, 0, f))
    pair_shape = jax.ShapeDtypeStruct((2, half, hidden), BF)
    keep, send, mlp_out, mlp_din, b_up_part = pl.pallas_call(
        functools.partial(mlp_kernel, token_count),
        grid_spec=pltpu.PrefetchScalarGridSpec(
            num_scalar_prefetch=1,
            grid=(hidden // tile,),
            in_specs=[
                whole((token_count, width)), whole((token_count, width)),
                whole((width, token_count)), whole((width, token_count)),
                pl.BlockSpec((width, tile), lambda f, *_: (0, f)),
                pl.BlockSpec((1, tile), lambda f, *_: (0, f)),
                pl.BlockSpec((tile, width), lambda f, *_: (f, 0)),
            ],
            out_specs=[
                pair_cols, pair_cols, whole((token_count, width)), whole((token_count, width)),
                pl.BlockSpec((1, tile), lambda f, *_: (0, f)),
            ],
            scratch_shapes=[
                pltpu.VMEM((token_count, tile), BF), pltpu.VMEM((token_count, tile), BF),
            ],
        ),
        out_shape=[
            pair_shape, pair_shape,
            jax.ShapeDtypeStruct((token_count, width), F32),
            jax.ShapeDtypeStruct((token_count, width), F32),
            jax.ShapeDtypeStruct((1, hidden), F32),
        ],
        compiler_params=params(60),
        cost_estimate=LONG,
        name="mlp",
    )(side, mlp_in, bg, joined(mlp_t), joined(bg_t), w_up, b_up.reshape(1, hidden), w_down)

    gathered = ordered_after(tuple(gathered), b_up_part)

    def stack_body(*refs):
        for j, ref in enumerate(refs[:-1]):
            refs[-1][j] = ref[...]

    even = pl.pallas_call(
        stack_body,
        in_specs=[pl.BlockSpec(memory_space=pltpu.VMEM)] * len(gathered),
        out_specs=pl.BlockSpec(memory_space=pltpu.VMEM),
        out_shape=jax.ShapeDtypeStruct((len(gathered),) + payload.shape, BF),
        compiler_params=pltpu.CompilerParams(vmem_limit_bytes=24 * 1024 * 1024),
        cost_estimate=LONGEST,
        name="stack",
    )(*gathered)
    odd = lax.ppermute(even, "seq", partners(seq_devices, 1))

    bits = [(0, bit) for bit in range(1, seq_devices.bit_length() - 1)]
    batch_bits = [(1, bit) for bit in range(batch_devices.bit_length() - 1)]
    blocks = devices // 2

    def pair_streams(keep, send, resident):
        shape = (2 * blocks, rows, keep.shape[2])
        keep = keep.reshape(shape)
        recv = lax.ppermute(send.reshape(shape), "seq", partners(seq_devices, 1))
        return [
            Stream([(keep, at), (recv, at)], blocks, resident, keep.shape[2])
            for at in (0, blocks)
        ]

    mlp_streams = pair_streams(keep, send, False)

    half_seq = seq_devices // 2
    key_blocks = length * seq_devices // KEY_BLOCK
    stat_rows = -(-heads // 8) * 8

    def attention(first, count, after, before):
        kv_rows = pl.BlockSpec(
            (half_seq, 1, length + COUNT_ROWS, 2 * head_size), lambda r, *_: (0, first + r, 0, 0)
        )
        dkv_rows = pl.BlockSpec(
            (half_seq, 1, length, 2 * head_size), lambda r, *_: (0, first + r, 0, 0)
        )
        dkv_shape = jax.ShapeDtypeStruct((half_seq, row_count, length, 2 * head_size), BF)
        return pl.pallas_call(
            functools.partial(attention_kernel, heads, head_size, seq_devices, first),
            grid_spec=pltpu.PrefetchScalarGridSpec(
                num_scalar_prefetch=1,
                grid=(count,),
                in_specs=[
                    segments_spec, row_block((head_size, lanes), first),
                    row_block((head_size, lanes), first), kv_rows, kv_rows, turn_spec, turn_spec,
                ]
                + [pl.BlockSpec(memory_space=pl.ANY)] * len(before),
                out_specs=[column_block(first), column_block(first), dkv_rows, dkv_rows],
                scratch_shapes=[
                    pltpu.VMEM((key_blocks * KEY_BLOCK, 2 * head_size), BF),
                    pltpu.VMEM((key_blocks, 2 * head_size, KEY_BLOCK), BF),
                    pltpu.VMEM((KEY_BLOCK, length), F32),
                    pltpu.VMEM((key_blocks, KEY_BLOCK, lanes), BF),
                    pltpu.VMEM((KEY_BLOCK, lanes), BF),
                    pltpu.VMEM((head_size, lanes), BF),
                    pltpu.VMEM((head_size, lanes), F32),
                    pltpu.VMEM((head_size, lanes), F32),
                    pltpu.VMEM((key_blocks * KEY_BLOCK, 2 * head_size), BF),
                    pltpu.VMEM((stat_rows, length), F32),
                    pltpu.VMEM((stat_rows, length), F32),
                    pltpu.VMEM((stat_rows, length), F32),
                    pltpu.VMEM((key_blocks, stat_rows, length), F32),
                ],
            ),
            out_shape=[columns, columns, dkv_shape, dkv_shape],
            input_output_aliases={8 + j: j for j in range(len(before))},
            compiler_params=params(60),
            cost_estimate=LONG,
        name="attention",
        )(
            ordered_after(where, *after), segment_ids, q_t, g_t, in_hbm(even), in_hbm(odd), cosine,
            sine, *before,
        )

    pair_levels = [(bits[i], bits[-1 - i]) for i in range(len(bits))]
    batch_levels = [(bit, bit) for bit in batch_bits]
    mlp_levels = iter(pair_levels + batch_levels)
    results, first_row = [b_up_part], 0
    last_share = max(row_count // 4, 1)
    for share in (row_count - last_share, last_share):
        after = results[:1] if first_row else [even]
        after, _ = reduce_level(mlp_streams, next(mlp_levels), where, after, LONG)
        results = attention(first_row, share, after, results if first_row else [])
        first_row += share
    mix_t, qpg_t, dkv_keep, dkv_send = results
    dkv_recv = lax.ppermute(dkv_send, "seq", partners(seq_devices, 1))
    after, mlp_recv = reduce_level(mlp_streams, next(mlp_levels), where, [mix_t], LONG)

    def share_body(where_ref, keep_ref, recv_ref, *out_refs):
        for j, out_ref in enumerate(out_refs):
            out_ref[...] = (keep_ref[j].astype(F32) + recv_ref[j].astype(F32)).astype(BF)

    shares = call_on_terms(
        share_body, "share", where, after, 1,
        [pl.BlockSpec(memory_space=pltpu.VMEM)] * 2, [dkv_keep, dkv_recv],
        [pl.BlockSpec(memory_space=pltpu.VMEM)] * half_seq,
        [jax.ShapeDtypeStruct(dkv_keep.shape[1:], BF)] * half_seq,
        short(6 * dkv_keep.size),
    )
    dkv_parts = [shares[0]]
    for j in range(1, half_seq):
        dkv_parts.append(lax.ppermute(shares[j], "seq", partners(seq_devices, 2 * j)))

    pair_spec = pl.BlockSpec(memory_space=pltpu.VMEM)
    pair_width = jax.ShapeDtypeStruct((2, half, width), BF)
    output, keep, send = pl.pallas_call(
        mix_kernel,
        grid_spec=pltpu.PrefetchScalarGridSpec(
            num_scalar_prefetch=1,
            grid=(row_count,),
            in_specs=[
                row_block((length, width)), segments_spec, column_block(), column_block(),
                column_block(), column_block(), token_block, whole((width, width)),
                width_spec, width_spec,
            ],
            out_specs=[row_block((length, width)), pair_spec, pair_spec],
            scratch_shapes=[pltpu.VMEM((width, width), F32), pltpu.VMEM((width, width), F32)],
        ),
        out_shape=[
            jax.ShapeDtypeStruct((row_count, length, width), BF), pair_width, pair_width,
        ],
        compiler_params=params(56),
        cost_estimate=LONG,
        name="mix",
    )(
        ordered_after(side, dkv_parts[0]), tokens, segment_ids, mix_t, qpg_t, attn_t, bg_t,
        mlp_out, w_out, b_out, b_down,
    )
    mix_streams = pair_streams(keep, send, True)
    after = [keep, *mlp_recv, *dkv_parts[1:]]
    after, _ = reduce_level(mlp_streams, next(mlp_levels), where, after, LONG)
    after, _ = reduce_level(mix_streams, pair_levels[0], where, after)

    dkv_count = len(dkv_parts)

    def exit_body(*refs):
        fixed, rest = refs[:15], refs[15:]
        exit_kernel(order_a, rows, permuted, *fixed, rest[:dkv_count], *rest[dkv_count:])

    if permuted:
        shuffle = jnp.zeros((8, LANES), F32)
    else:
        places = (jnp.array(order_a)[:, None] * rows + jnp.arange(rows)[None, :]).reshape(width, 1)
        shuffle = (places == jnp.arange(width)[None, :]).astype(F32)
    b_up_rows = jnp.transpose(
        b_up_part.reshape(devices, hidden // width, rows), (1, 0, 2)
    ).reshape(hidden // width, width)
    extra_spec = pl.BlockSpec(memory_space=pltpu.VMEM)
    extra_shape = jax.ShapeDtypeStruct((half, 2 * LANES), BF)
    tokens_grad, keep, send = pl.pallas_call(
        exit_body,
        grid_spec=pltpu.PrefetchScalarGridSpec(
            num_scalar_prefetch=1,
            grid=(row_count,),
            in_specs=[
                row_block((length, width)), row_block((length, width)), segments_spec,
                column_block(), column_block(), token_block, whole((width, width)),
                whole((width, 2 * head_size)), width_spec, width_spec, turn_spec, turn_spec,
                whole((hidden // width, width)), whole(shuffle.shape),
            ]
            + [row_block((length, 2 * head_size))] * dkv_count,
            out_specs=[row_block((length, width)), extra_spec, extra_spec],
            scratch_shapes=[
                pltpu.VMEM((width, 2 * head_size), F32), pltpu.VMEM((LANES, width), F32),
            ],
        ),
        out_shape=[
            jax.ShapeDtypeStruct((row_count, length, width), BF), extra_shape, extra_shape,
        ],
        compiler_params=params(56),
        cost_estimate=LONG,
        name="exit",
    )(
        ordered_after(side, *after), tokens, out_grad, segment_ids, qpg_t, attn_t, mlp_din, w_query, w_keyvalue,
        attn_gain, mlp_gain, cosine, sine, b_up_rows, shuffle,
        *dkv_parts,
    )

    shape = (blocks, rows, 2 * LANES)
    keep = keep.reshape(shape)
    recv = lax.ppermute(send.reshape(shape), "seq", partners(seq_devices, 1))
    extra_streams = [Stream([(keep, 0), (recv, 0)], blocks, True, 2 * LANES)]
    after = [keep]
    for level in pair_levels[1:]:
        after, _ = reduce_level(mix_streams, level, where, after)
    after = exchange(extra_streams, bits, where, after)[:1]
    for level in mlp_levels:
        after, _ = reduce_level(mlp_streams, level, where, after)
    sums = own_sums(mlp_streams, where, after, LONG)
    small_streams = mix_streams + extra_streams
    exchange(small_streams, batch_bits, where, sums[:1])
    several = hidden // width
    sums += own_sums(small_streams, where, vectors=[*range(6), *range(8, 8 + several)])
    w_up_grad, w_down_grad_t, w_query_grad, w_out_grad_t, w_keyvalue_grad, *vectors = sums
    return (
        output,
        keyvalue,
        tokens_grad,
        vectors[0],
        vectors[1],
        vectors[2],
        vectors[3],
        w_query_grad,
        vectors[4],
        w_keyvalue_grad,
        w_out_grad_t.T,
        vectors[5],
        w_up_grad,
        jnp.concatenate(vectors[6:]),
        w_down_grad_t.T,
        vectors[5],
    )


def solution(mesh):
    row_spec = P("batch", "seq", None)
    split = P(("batch", "seq"))
    first = P(("batch", "seq"), None)
    last = P(None, ("batch", "seq"))
    return jax.shard_map(
        on_device,
        mesh=mesh,
        in_specs=(row_spec, P("batch", "seq")) + (P(),) * 13 + (row_spec,),
        out_specs=(
            row_spec, row_spec, row_spec, split, split, split, split, first, split, first, last,
            split, first, split, last, split,
        ),
        check_vma=False,
    )
```

```python
import functools
import math

import jax
import jax.numpy as jnp
from jax import lax
from jax.experimental import pallas as pl
from jax.experimental.pallas import tpu as pltpu
from jax.sharding import PartitionSpec as P

ROT_DIMS = 16
HALF_ROT = ROT_DIMS // 2
DOCS = 6
EPSILON = 1e-05
KEY_BLOCK = 256
COUNT_ROWS = 16
LANES = 128
NEGATIVE = -1e30
BF = jnp.bfloat16
F32 = jnp.float32
NN = (((1,), (0,)), ((), ()))
NT = (((1,), (1,)), ((), ()))
TN = (((0,), (0,)), ((), ()))


def matmul(left, right, dims=NN):
    return lax.dot_general(left, right, dims, preferred_element_type=F32)


def params(limit):
    return pltpu.CompilerParams(
        dimension_semantics=("arbitrary",), vmem_limit_bytes=limit * 1024 * 1024
    )


LONG = pl.CostEstimate(flops=4 * 10**10, transcendentals=0, bytes_accessed=10**7)

LONGEST = pl.CostEstimate(flops=3 * 10**11, transcendentals=0, bytes_accessed=10**7)


def short(size):
    return pl.CostEstimate(flops=0, transcendentals=0, bytes_accessed=size)


def whole(shape):
    return pl.BlockSpec(shape, lambda *_: (0,) * len(shape))


def permute_rows(values, order, rows):
    return jnp.concatenate([values[b * rows : (b + 1) * rows] for b in order], axis=0)


def row_of(ref):
    return ref[...].astype(F32).reshape(1, ref.shape[0])


def valid_column(segment_row):
    length = segment_row.shape[-1]
    row = jnp.broadcast_to((segment_row >= 0).astype(F32), (LANES, length))
    return row.T[:, :1]


def norm_parts(values):
    center = values - jnp.mean(values, axis=-1, keepdims=True)
    spread = jnp.mean(center * center, axis=-1, keepdims=True)
    scale = lax.rsqrt(spread + EPSILON)
    return center * scale, scale


def turn(values, cosine, sine):
    leading = values[:HALF_ROT]
    trailing = values[HALF_ROT:ROT_DIMS]
    return jnp.concatenate(
        [leading * cosine - trailing * sine, trailing * cosine + leading * sine, values[ROT_DIMS:]],
        axis=0,
    )


def entry_kernel(
    head_size, order_a, order_b, rows, permuted,
    tok_ref, og_ref, seg_ref, ag_ref, as_ref, mg_ref, ms_ref, bq_ref, wq_ref, wkv_ref, wo_ref,
    cos_ref, sin_ref, mlp_ref, bg_ref, mlp_t_ref, bg_t_ref, attn_t_ref, q_t_ref, g_t_ref, kv_ref, pay_ref,
):
    x = tok_ref[0].astype(F32)
    length, width = x.shape
    n, _ = norm_parts(x)
    attn_in = (n * row_of(ag_ref) + row_of(as_ref)).astype(BF)
    mlp_in = (n * row_of(mg_ref) + row_of(ms_ref)).astype(BF)
    segments = seg_ref[pl.ds(pl.program_id(0), 1), :]
    bg = (og_ref[0].astype(F32) * valid_column(segments)).astype(BF)
    mlp_ref[...] = mlp_in
    bg_ref[...] = bg

    def turned(values, order):
        flipped = values.astype(F32).T
        if permuted:
            flipped = permute_rows(flipped, order, rows)
        return flipped.astype(BF)

    mlp_t_ref[...] = turned(mlp_in, order_a)
    attn_t_ref[...] = turned(attn_in, order_a)
    bg_t_ref[...] = turned(bg, order_b)

    cosine, sine = cos_ref[...], sin_ref[...]
    score_scale = 1.0 / math.sqrt(head_size)
    query_t = (matmul(attn_in, wq_ref[...]) + row_of(bq_ref)).T
    grad_t = matmul(wo_ref[...], bg, NT)
    for h in range(width // head_size):
        part = query_t[h * head_size : (h + 1) * head_size]
        q_t_ref[0, :, h * length : (h + 1) * length] = (
            turn(part, cosine, sine) * score_scale
        ).astype(BF)
        g_t_ref[0, :, h * length : (h + 1) * length] = grad_t[
            h * head_size : (h + 1) * head_size
        ].astype(BF)
    kv_t = matmul(attn_in, wkv_ref[...]).T
    kv = turn(kv_t, cosine, sine).T.astype(BF)
    kv_ref[0] = kv
    pay_ref[0, :length] = kv
    lane = lax.broadcasted_iota(jnp.int32, (1, LANES), 1)
    counts = jnp.zeros((1, LANES), F32)
    for c in range(DOCS):
        total = jnp.sum((segments == c).astype(F32), axis=1, keepdims=True)
        counts = counts + jnp.where(lane == c, total, 0.0)
    pay_ref[0, length:] = jnp.broadcast_to(counts, (COUNT_ROWS, LANES)).astype(BF)


def gelu_parts(hidden):
    cdf = 0.5 * (1.0 + lax.erf(hidden * math.sqrt(0.5)))
    bell = jnp.exp(-0.5 * (hidden * hidden)) * (1.0 / math.sqrt(2 * math.pi))
    return hidden * cdf, cdf + hidden * bell


def mlp_kernel(
    chunk, side_ref, mlp_ref, bg_ref, mlp_t_ref, bg_t_ref, up_ref, bup_ref, down_ref,
    keep_ref, send_ref, out_ref, din_ref, bupg_ref, act_s, hg_s,
):
    tokens, width = mlp_ref.shape

    @pl.when(pl.program_id(0) == 0)
    def _():
        out_ref[...] = jnp.zeros_like(out_ref)
        din_ref[...] = jnp.zeros_like(din_ref)

    bupg_ref[...] = jnp.zeros_like(bupg_ref)
    bias = bup_ref[...].astype(F32)

    def step(i, carry):
        at = pl.ds(pl.multiple_of(i * chunk, chunk), chunk)
        hidden = matmul(mlp_ref[at, :], up_ref[...]) + bias
        back = matmul(bg_ref[at, :], down_ref[...], NT)
        act, slope = gelu_parts(hidden)
        act = act.astype(BF)
        hg = (back * slope).astype(BF)
        act_s[at, :] = act
        hg_s[at, :] = hg
        bupg_ref[...] += jnp.sum(hg.astype(F32), axis=0, keepdims=True)
        out_ref[at, :] += matmul(act, down_ref[...])
        din_ref[at, :] += matmul(hg, up_ref[...], NT)
        return carry

    lax.fori_loop(0, tokens // chunk, step, 0)
    half = width // 2
    side = side_ref[0]
    mine = pl.ds(pl.multiple_of(side * half, half), half)
    other = pl.ds(pl.multiple_of((1 - side) * half, half), half)
    send_ref[0] = matmul(mlp_t_ref[other, :], hg_s[...]).astype(BF)
    send_ref[1] = matmul(bg_t_ref[other, :], act_s[...]).astype(BF)
    keep_ref[0] = matmul(mlp_t_ref[mine, :], hg_s[...]).astype(BF)
    keep_ref[1] = matmul(bg_t_ref[mine, :], act_s[...]).astype(BF)


def attention_kernel(
    heads, head_size, seq_devices, first_row, where_ref, seg_ref, q_t_ref, g_t_ref, even_ref,
    odd_ref, cos_ref, sin_ref, *refs,
):
    (mix_t_ref, qpg_t_ref, dkeep_ref, dsend_ref, kv_s, kv_t_s, bias_s, p_s, ds_s, gk_s, o_s, dq_s,
     dkv_s, m_s, l_s, d_s, mk_s) = refs[-17:]
    length = seg_ref.shape[-1]
    me = where_ref[0]
    start = me * length
    group = math.gcd(heads, 3)

    def columns(h, count=1):
        return slice(h * length, (h + count) * length)

    def head(h):
        return slice(h * head_size, (h + 1) * head_size)

    counts = jnp.zeros((1, LANES), F32)
    for m in range(seq_devices):
        ref = (even_ref, odd_ref)[m % 2]
        at = pl.multiple_of((me ^ m) * length, length)
        kv_s[pl.ds(at, length), :] = ref[m // 2, 0, :length]
        counts = counts + ref[m // 2, 0, length : length + COUNT_ROWS].astype(F32)[:1]

    segments = seg_ref[pl.ds(first_row + pl.program_id(0), 1), :]
    low = jnp.zeros((1, length), F32)
    for c in range(DOCS):
        later = (segments > c) | (segments < 0)
        low = low + jnp.where(later, counts[:, c : c + 1], 0.0)
    low = low.astype(jnp.int32)
    first_block = jnp.min(low) // KEY_BLOCK
    end_block = (start + length - 1) // KEY_BLOCK + 1
    place = start + lax.broadcasted_iota(jnp.int32, (1, length), 1)

    m_s[...] = jnp.full_like(m_s, NEGATIVE)
    l_s[...] = jnp.zeros_like(l_s)
    o_s[...] = jnp.zeros_like(o_s)
    dq_s[...] = jnp.zeros_like(dq_s)
    dkv_s[...] = jnp.zeros_like(dkv_s)

    def forward(b, carry):
        at = pl.multiple_of(b * KEY_BLOCK, KEY_BLOCK)
        kv = kv_s[pl.ds(at, KEY_BLOCK), :]
        keys = kv[:, :head_size]
        kv_t = kv.astype(F32).T.astype(BF)
        kv_t_s[b] = kv_t
        summed = jnp.concatenate([kv_t[head_size:], jnp.ones((16, KEY_BLOCK), BF)], axis=0)
        key_place = at + lax.broadcasted_iota(jnp.int32, (KEY_BLOCK, length), 0)
        allowed = (key_place <= place) & (key_place >= low)
        bias_s[...] = jnp.where(allowed, 0.0, NEGATIVE)
        bias = bias_s[...]
        shrinks = {}

        def scores(h):
            return matmul(keys, q_t_ref[0, :, columns(h, group)])

        def mix(h):
            o = matmul(summed, p_s[b, :, columns(h, group)])
            for j in range(group):
                row = slice(h + j, h + j + 1)
                part = o[:, columns(j)]
                shrink = shrinks.pop(h + j)
                o_s[:, columns(h + j)] = o_s[:, columns(h + j)] * shrink + part[:head_size]
                l_s[row, :] = l_s[row, :] * shrink + part[head_size : head_size + 1]

        ready = scores(0)
        for h in range(0, heads, group):
            now_scores = ready
            if h + group < heads:
                ready = scores(h + group)
            for j in range(group):
                row = slice(h + j, h + j + 1)
                s = now_scores[:, columns(j)] + bias
                before = m_s[row, :]
                now = jnp.maximum(before, jnp.max(s, axis=0, keepdims=True))
                p_s[b, :, columns(h + j)] = jnp.exp(s - now).astype(BF)
                shrinks[h + j] = jnp.exp(before - now)
                m_s[row, :] = now
                mk_s[b, row, :] = now
            if h > 0:
                mix(h - group)
        mix(heads - group)
        return carry

    lax.fori_loop(first_block, end_block, forward, 0)

    for h in range(heads):
        row = slice(h, h + 1)
        inverse = 1.0 / l_s[row, :]
        mixed = o_s[:, columns(h)] * inverse
        mix_t_ref[head(h), :] = mixed.astype(BF)
        d_s[row, :] = jnp.sum(
            mixed * g_t_ref[0, :, columns(h)].astype(F32), axis=0, keepdims=True
        )
        l_s[row, :] = inverse

    def backward(b, carry):
        at = pl.multiple_of(b * KEY_BLOCK, KEY_BLOCK)
        values = kv_s[pl.ds(at, KEY_BLOCK), :][:, head_size:]
        keys_t = kv_t_s[b][:head_size]
        inners = {}

        def prob_grads(h):
            for j in range(group):
                row = slice(h + j, h + j + 1)
                factor = jnp.exp(mk_s[b, row, :] - m_s[row, :]) * l_s[row, :]
                scaled = g_t_ref[0, :, columns(h + j)].astype(F32) * factor
                gk_s[:, columns(h + j)] = scaled.astype(BF)
                inners[h + j] = d_s[row, :] * factor
            return matmul(values, gk_s[:, columns(h, group)])

        ready = prob_grads(0)
        for h in range(0, heads, group):
            now_grads = ready
            if h + group < heads:
                ready = prob_grads(h + group)
            for j in range(group):
                p = p_s[b, :, columns(h + j)].astype(F32)
                ds_s[:, columns(h + j)] = (
                    p * (now_grads[:, columns(j)] - inners.pop(h + j))
                ).astype(BF)
        dq_s[...] += matmul(keys_t, ds_s[...])
        dk = matmul(ds_s[...], q_t_ref[0], NT)
        dv = matmul(p_s[b], gk_s[...], NT)
        dkv_s[pl.ds(at, KEY_BLOCK), :] = jnp.concatenate([dk, dv], axis=1).astype(BF)
        return carry

    lax.fori_loop(first_block, end_block, backward, 0)

    cosine, sine = cos_ref[...], sin_ref[...]
    score_scale = 1.0 / math.sqrt(head_size)
    for h in range(heads):
        qpg_t_ref[head(h), :] = turn(
            dq_s[:, columns(h)] * score_scale, cosine, -sine
        ).astype(BF)
    for m in range(seq_devices):
        ref = (dkeep_ref, dsend_ref)[m % 2]
        at = pl.multiple_of((me ^ m) * length, length)
        ref[m // 2, 0] = dkv_s[pl.ds(at, length), :]


def mix_kernel(
    side_ref, tok_ref, seg_ref, mix_t_ref, qpg_t_ref, attn_t_ref, bg_t_ref, mlp_ref, wo_ref,
    bo_ref, bd_ref, out_ref, keep_ref, send_ref, acc_q, acc_o,
):
    step, steps = pl.program_id(0), pl.num_programs(0)

    @pl.when(step == 0)
    def _():
        acc_q[...] = jnp.zeros_like(acc_q)
        acc_o[...] = jnp.zeros_like(acc_o)

    mix_t = mix_t_ref[...]
    branch = matmul(mix_t, wo_ref[...], TN) + (row_of(bo_ref) + row_of(bd_ref)) + mlp_ref[...]
    valid = valid_column(seg_ref[pl.ds(step, 1), :])
    out_ref[0] = (tok_ref[0].astype(F32) + valid * branch).astype(BF)
    acc_q[...] += matmul(attn_t_ref[...], qpg_t_ref[...], NT)
    acc_o[...] += matmul(bg_t_ref[...], mix_t, NT)

    @pl.when(step == steps - 1)
    def _():
        half = acc_q.shape[0] // 2
        side = side_ref[0]
        mine = pl.ds(pl.multiple_of(side * half, half), half)
        other = pl.ds(pl.multiple_of((1 - side) * half, half), half)
        for j, acc in enumerate((acc_q, acc_o)):
            keep_ref[j] = acc[mine, :].astype(BF)
            send_ref[j] = acc[other, :].astype(BF)


def exit_kernel(
    order_a, rows, permuted,
    side_ref, tok_ref, og_ref, seg_ref, qpg_t_ref, attn_t_ref, din_ref, wq_ref, wkv_ref,
    ag_ref, mg_ref, cos_ref, sin_ref, bupg_ref, shuffle_ref, dkv_refs,
    tg_ref, keep_ref, send_ref, acc, vec,
):
    step, steps = pl.program_id(0), pl.num_programs(0)

    @pl.when(step == 0)
    def _():
        acc[...] = jnp.zeros_like(acc)
        vec[...] = jnp.zeros_like(vec)

    dkv = sum((ref[0].astype(F32) for ref in dkv_refs[1:]), dkv_refs[0][0].astype(F32))
    kvpg_t = turn(dkv.T, cos_ref[...], -sin_ref[...]).astype(BF)
    acc[...] += matmul(attn_t_ref[...], kvpg_t, NT)
    qpg_t = qpg_t_ref[...]
    d_attn = (matmul(wq_ref[...], qpg_t) + matmul(wkv_ref[...], kvpg_t)).T
    d_mlp = din_ref[...]
    n, scale = norm_parts(tok_ref[0].astype(F32))
    og = og_ref[0].astype(F32)
    e = d_attn * row_of(ag_ref) + d_mlp * row_of(mg_ref)
    inner = jnp.mean(e * n, axis=-1, keepdims=True)
    tg_ref[0] = (og + scale * (e - jnp.mean(e, axis=-1, keepdims=True) - n * inner)).astype(BF)
    ones = jnp.ones((8, qpg_t.shape[1]), BF)
    bg = (og * valid_column(seg_ref[pl.ds(step, 1), :])).astype(BF)
    sums = [d_attn * n, d_attn, d_mlp * n, d_mlp, None, bg.astype(F32)]
    for j, value in enumerate(sums):
        if value is None:
            part = matmul(ones, qpg_t, NT)[:1]
        else:
            part = jnp.sum(value, axis=0, keepdims=True)
        vec[j : j + 1, :] += part

    @pl.when(step == steps - 1)
    def _():
        vec[8:12, :] = bupg_ref[...]
        if permuted:
            columns = permute_rows(vec[...].T, order_a, rows)
        else:
            columns = lax.dot_general(
                shuffle_ref[...], vec[...], NT, precision=lax.Precision.HIGHEST,
                preferred_element_type=F32,
            )
        half = columns.shape[0] // 2
        acc_columns = slice(0, LANES)
        vec_columns = slice(LANES, 2 * LANES)
        for side in range(2):

            @pl.when(side_ref[0] == side)
            def _():
                mine = slice(side * half, (side + 1) * half)
                other = slice((1 - side) * half, (2 - side) * half)
                keep_ref[:, acc_columns] = acc[mine, :].astype(BF)
                send_ref[:, acc_columns] = acc[other, :].astype(BF)
                keep_ref[:, vec_columns] = columns[mine].astype(BF)
                send_ref[:, vec_columns] = columns[other].astype(BF)


def partners(size, mask):
    return [(i, i ^ mask) for i in range(size)]


class Stream:
    def __init__(self, arrays, count, resident, width):
        self.terms = [(array, resident, 0, at, ()) for array, at in arrays]
        self.count, self.resident, self.width = count, resident, width
        self.rows = arrays[0][0].shape[1]

    def halve(self, bit):
        count = self.count = self.count // 2
        mine, other = [], []
        for array, resident, column, at, adds in self.terms:
            mine.append((array, resident, column, at, adds + ((bit, count),)))
            other.append((array, resident, column, at + count, adds + ((bit, -count),)))
        self.terms = mine
        return other


def first_block(term, where_ref):
    at = term[3]
    for (axis, bit), weight in term[4]:
        at = at + ((where_ref[axis] >> bit) & 1) * weight
    return at


def term_spec(term, width, group):
    if term[1]:
        return pl.BlockSpec(memory_space=pltpu.VMEM)
    return pl.BlockSpec(
        (group, term[0].shape[1], width),
        lambda i, where_ref: (first_block(term, where_ref) // group + i, 0, term[2] // width),
    )


def in_hbm(value):
    return pltpu.with_memory_space_constraint(value, pltpu.HBM)


def operands_of(terms):
    return [term[0] if term[1] else in_hbm(term[0]) for term in terms]


def read_terms(terms, refs, width, group, where_ref):
    total = None
    for term, ref in zip(terms, refs):
        if term[1]:
            at = first_block(term, where_ref) + pl.program_id(0) * group
            value = ref[pl.ds(at, group), :, term[2] : term[2] + width]
        else:
            value = ref[...]
        value = value.astype(F32)
        total = value if total is None else total + value
    return total


def call_on_terms(
    body, name, where, after, steps, in_specs, operands, out_specs, out_shape, length
):
    return pl.pallas_call(
        body,
        grid_spec=pltpu.PrefetchScalarGridSpec(
            num_scalar_prefetch=1, grid=(steps,), in_specs=in_specs, out_specs=out_specs
        ),
        out_shape=out_shape,
        compiler_params=params(limit=24),
        cost_estimate=length,
        name=name,
    )(ordered_after(where, *after), *operands)


def sums_to_send(picks, streams, joined, where, after, length):
    count, rows, resident = streams[0].count, streams[0].rows, streams[0].resident
    widths = [streams[j % len(streams)].width for j in range(len(picks))]
    group = count
    while group > 1 and group * widths[0] > 4 * 3072 and not resident:
        group //= 2
    terms = [term for pick in picks for term in pick]
    outputs = len(picks) // joined
    shapes = [(rows, sum(widths[j * joined : (j + 1) * joined])) for j in range(outputs)]

    def body(where_ref, *refs):
        at = 0
        for j, (pick, width) in enumerate(zip(picks, widths)):
            total = read_terms(pick, refs[at : at + len(pick)], width, group, where_ref).astype(BF)
            column = sum(widths[j - j % joined : j])
            refs[len(terms) + j // joined][:, :, column : column + width] = total
            at += len(pick)

    if resident:
        out_specs = [pl.BlockSpec(memory_space=pltpu.VMEM) for _ in shapes]
    else:
        out_specs = [pl.BlockSpec((group,) + shape, lambda i, _: (i, 0, 0)) for shape in shapes]
    return call_on_terms(
        body, "combine", where, after, count // group,
        [term_spec(term, width, group) for pick, width in zip(picks, widths) for term in pick],
        operands_of(terms),
        out_specs,
        [jax.ShapeDtypeStruct((count,) + shape, BF) for shape in shapes],
        length or short(2 * count * rows * sum(len(p) * w for p, w in zip(picks, widths))),
    )


def own_sums(streams, where, after=(), length=None, vectors=()):
    terms = [term for stream in streams for term in stream.terms]
    shapes = [(stream.rows, stream.width) for stream in streams]
    if vectors:
        shapes[-1] = (shapes[-1][0], shapes[-1][1] - LANES)
        shapes += [(streams[-1].rows * len(columns),) for columns in vectors]

    def body(where_ref, *refs):
        at = 0
        for stream, output in zip(streams, refs[len(terms) :]):
            size = len(stream.terms)
            total = read_terms(stream.terms, refs[at : at + size], stream.width, 1, where_ref)[0]
            output[...] = total[:, : output.shape[1]]
            at += size
        if vectors:
            turned = total[:, -LANES:].T
            for columns, output in zip(vectors, refs[len(terms) + len(streams) :]):
                row = jnp.concatenate([turned[c : c + 1] for c in columns], axis=1)
                output[...] = row.reshape(output.shape)

    return call_on_terms(
        body, "own", where, after, 1,
        [term_spec(term, stream.width, 1) for stream in streams for term in stream.terms],
        operands_of(terms),
        [whole(shape) for shape in shapes],
        [jax.ShapeDtypeStruct(shape, F32) for shape in shapes],
        length or short(2 * len(terms) * streams[0].rows * streams[0].width),
    )


def ordered_after(value, *others):
    if not others:
        return value
    return lax.optimization_barrier((value, others))[0]


AXES = ("seq", "batch")


def reduce_level(streams, bits, where, after=(), length=None):
    picks = [stream.halve(bit) for stream, bit in zip(streams, bits)]
    joined = len(set(bits)) == 1
    sends = sums_to_send(picks, streams, len(streams) if joined else 1, where, after, length)
    recvs = []
    for (axis, bit), send in zip(bits, sends):
        recvs.append(
            lax.ppermute(send, AXES[axis], partners(lax.axis_size(AXES[axis]), 1 << bit))
        )
    for j, stream in enumerate(streams):
        column = j * stream.width if joined else 0
        resident = stream.resident or stream.count <= 4
        stream.terms.append((recvs[0 if joined else j], resident, column, 0, ()))
    return sends, recvs


def exchange(streams, bits, where, after=()):
    axis = AXES[bits[0][0]]
    picks, recvs = [], []
    for mask in range(1, 1 << len(bits)):
        for stream in streams:
            count, terms = stream.count, stream.terms
            for j, bit in enumerate(bits):
                count //= 2
                sign, shift = (-1, count) if (mask >> j) & 1 else (1, 0)
                terms = [
                    (a, r, c, at + shift, adds + ((bit, sign * count),))
                    for a, r, c, at, adds in terms
                ]
            picks.append(terms)
    for stream in streams:
        for bit in bits:
            stream.halve(bit)
    sends = sums_to_send(picks, streams, len(streams), where, after, None)
    for mask, send in enumerate(sends, 1):
        partner = sum(((mask >> j) & 1) << bit[1] for j, bit in enumerate(bits))
        recv = lax.ppermute(send, axis, partners(lax.axis_size(axis), partner))
        column = 0
        for stream in streams:
            stream.terms.append((recv, stream.resident, column, 0, ()))
            column += stream.width
    return sends


def on_device(
    tokens, segment_ids, attn_gain, attn_shift, mlp_gain, mlp_shift, w_query, b_query,
    w_keyvalue, w_out, b_out, w_up, b_up, w_down, b_down, out_grad,
):
    row_count, length, width = tokens.shape
    head_size = w_keyvalue.shape[1] // 2
    heads = width // head_size
    hidden = w_up.shape[1]
    token_count = row_count * length
    seq_devices = lax.axis_size("seq")
    batch_devices = lax.axis_size("batch")
    devices = seq_devices * batch_devices
    seq_index = lax.axis_index("seq").astype(jnp.int32)
    batch_index = lax.axis_index("batch").astype(jnp.int32)
    side = (seq_index & 1).reshape(1)
    where = jnp.stack([seq_index, batch_index])
    rows = width // devices
    permuted = rows % 8 == 0
    seq_bits = list(range(seq_devices.bit_length() - 1))

    def reversed_bits(value, count):
        return sum(((value >> j) & 1) << (count - 1 - j) for j in range(count))

    batch_order = [
        reversed_bits(z, batch_devices.bit_length() - 1) for z in range(batch_devices)
    ]

    def device_order(bits):
        order = []
        for k in range(seq_devices):
            at = 0
            for j, bit in enumerate(bits):
                at |= ((k >> (len(bits) - 1 - j)) & 1) << bit
            order += [z * seq_devices + at for z in batch_order]
        return order

    order_a = device_order(seq_bits)
    order_b = device_order(seq_bits[:1] + seq_bits[:0:-1])

    def ordered(values, order):
        if permuted:
            return values
        shaped = values.reshape(values.shape[:-2] + (devices, rows, values.shape[-1]))
        return jnp.take(shaped, jnp.array(order), axis=-3).reshape(values.shape)

    positions = (seq_index * length + jnp.arange(length)).astype(F32)
    inverse = 10000.0 ** (-(jnp.arange(HALF_ROT).astype(F32) * (2.0 / ROT_DIMS)))
    angles = inverse[:, None] * positions[None, :]
    cosine, sine = jnp.cos(angles), jnp.sin(angles)
    segments_spec = whole((row_count, length))
    turn_spec = whole((HALF_ROT, length))
    width_spec = whole((width,))

    def row_block(shape, first=0):
        return pl.BlockSpec((1,) + shape, lambda r, *_: (first + r, 0, 0))

    token_block = pl.BlockSpec((length, width), lambda r, *_: (r, 0))
    whole_lanes = length % LANES == 0

    def column_block(first=0):
        if whole_lanes:
            return pl.BlockSpec((width, length), lambda r, *_: (0, first + r))
        return pl.BlockSpec((None, width, length), lambda r, *_: (first + r, 0, 0))

    columns = jax.ShapeDtypeStruct(
        (width, token_count) if whole_lanes else (row_count, width, length), BF
    )

    def joined(values):
        if whole_lanes:
            return values
        return jnp.transpose(values, (1, 0, 2)).reshape(width, token_count)

    lanes = heads * length
    mlp_in, bg, mlp_t, bg_t, attn_t, q_t, g_t, keyvalue, payload = pl.pallas_call(
        functools.partial(entry_kernel, head_size, order_a, order_b, rows, permuted),
        grid=(row_count,),
        in_specs=[
            row_block((length, width)), row_block((length, width)), segments_spec,
            width_spec, width_spec, width_spec, width_spec, width_spec,
            whole((width, width)), whole((width, 2 * head_size)), whole((width, width)),
            turn_spec, turn_spec,
        ],
        out_specs=[
            token_block, token_block, column_block(), column_block(), column_block(),
            row_block((head_size, lanes)), row_block((head_size, lanes)),
            row_block((length, 2 * head_size)), row_block((length + COUNT_ROWS, 2 * head_size)),
        ],
        out_shape=[
            jax.ShapeDtypeStruct((token_count, width), BF),
            jax.ShapeDtypeStruct((token_count, width), BF),
            columns,
            columns,
            columns,
            jax.ShapeDtypeStruct((row_count, head_size, lanes), BF),
            jax.ShapeDtypeStruct((row_count, head_size, lanes), BF),
            jax.ShapeDtypeStruct((row_count, length, 2 * head_size), BF),
            jax.ShapeDtypeStruct((row_count, length + COUNT_ROWS, 2 * head_size), BF),
        ],
        compiler_params=params(60),
        cost_estimate=LONG,
        name="entry",
    )(
        tokens, out_grad, segment_ids, attn_gain, attn_shift, mlp_gain, mlp_shift, b_query,
        w_query, w_keyvalue, w_out, cosine, sine,
    )
    mlp_t, attn_t = ordered(mlp_t, order_a), ordered(attn_t, order_a)
    bg_t = ordered(bg_t, order_b)

    gathered = [payload]
    for mask in range(2, seq_devices, 2):
        gathered.append(lax.ppermute(payload, "seq", partners(seq_devices, mask)))

    tile = math.gcd(512, hidden)
    half = width // 2
    pair_cols = pl.BlockSpec((2, half, tile), lambda f, *_: (0, 0, f))
    pair_shape = jax.ShapeDtypeStruct((2, half, hidden), BF)
    keep, send, mlp_out, mlp_din, b_up_part = pl.pallas_call(
        functools.partial(mlp_kernel, token_count),
        grid_spec=pltpu.PrefetchScalarGridSpec(
            num_scalar_prefetch=1,
            grid=(hidden // tile,),
            in_specs=[
                whole((token_count, width)), whole((token_count, width)),
                whole((width, token_count)), whole((width, token_count)),
                pl.BlockSpec((width, tile), lambda f, *_: (0, f)),
                pl.BlockSpec((1, tile), lambda f, *_: (0, f)),
                pl.BlockSpec((tile, width), lambda f, *_: (f, 0)),
            ],
            out_specs=[
                pair_cols, pair_cols, whole((token_count, width)), whole((token_count, width)),
                pl.BlockSpec((1, tile), lambda f, *_: (0, f)),
            ],
            scratch_shapes=[
                pltpu.VMEM((token_count, tile), BF), pltpu.VMEM((token_count, tile), BF),
            ],
        ),
        out_shape=[
            pair_shape, pair_shape,
            jax.ShapeDtypeStruct((token_count, width), F32),
            jax.ShapeDtypeStruct((token_count, width), F32),
            jax.ShapeDtypeStruct((1, hidden), F32),
        ],
        compiler_params=params(60),
        cost_estimate=LONG,
        name="mlp",
    )(side, mlp_in, bg, joined(mlp_t), joined(bg_t), w_up, b_up.reshape(1, hidden), w_down)

    gathered = ordered_after(tuple(gathered), b_up_part)

    def stack_body(*refs):
        for j, ref in enumerate(refs[:-1]):
            refs[-1][j] = ref[...]

    even = pl.pallas_call(
        stack_body,
        in_specs=[pl.BlockSpec(memory_space=pltpu.VMEM)] * len(gathered),
        out_specs=pl.BlockSpec(memory_space=pltpu.VMEM),
        out_shape=jax.ShapeDtypeStruct((len(gathered),) + payload.shape, BF),
        compiler_params=pltpu.CompilerParams(vmem_limit_bytes=24 * 1024 * 1024),
        cost_estimate=LONGEST,
        name="stack",
    )(*gathered)
    odd = lax.ppermute(even, "seq", partners(seq_devices, 1))

    bits = [(0, bit) for bit in range(1, seq_devices.bit_length() - 1)]
    batch_bits = [(1, bit) for bit in range(batch_devices.bit_length() - 1)]
    blocks = devices // 2

    def pair_streams(keep, send, resident):
        shape = (2 * blocks, rows, keep.shape[2])
        keep = keep.reshape(shape)
        recv = lax.ppermute(send.reshape(shape), "seq", partners(seq_devices, 1))
        return [
            Stream([(keep, at), (recv, at)], blocks, resident, keep.shape[2])
            for at in (0, blocks)
        ]

    mlp_streams = pair_streams(keep, send, False)

    half_seq = seq_devices // 2
    key_blocks = length * seq_devices // KEY_BLOCK
    stat_rows = -(-heads // 8) * 8

    def attention(first, count, after, before):
        kv_rows = pl.BlockSpec(
            (half_seq, 1, length + COUNT_ROWS, 2 * head_size), lambda r, *_: (0, first + r, 0, 0)
        )
        dkv_rows = pl.BlockSpec(
            (half_seq, 1, length, 2 * head_size), lambda r, *_: (0, first + r, 0, 0)
        )
        dkv_shape = jax.ShapeDtypeStruct((half_seq, row_count, length, 2 * head_size), BF)
        return pl.pallas_call(
            functools.partial(attention_kernel, heads, head_size, seq_devices, first),
            grid_spec=pltpu.PrefetchScalarGridSpec(
                num_scalar_prefetch=1,
                grid=(count,),
                in_specs=[
                    segments_spec, row_block((head_size, lanes), first),
                    row_block((head_size, lanes), first), kv_rows, kv_rows, turn_spec, turn_spec,
                ]
                + [pl.BlockSpec(memory_space=pl.ANY)] * len(before),
                out_specs=[column_block(first), column_block(first), dkv_rows, dkv_rows],
                scratch_shapes=[
                    pltpu.VMEM((key_blocks * KEY_BLOCK, 2 * head_size), BF),
                    pltpu.VMEM((key_blocks, 2 * head_size, KEY_BLOCK), BF),
                    pltpu.VMEM((KEY_BLOCK, length), F32),
                    pltpu.VMEM((key_blocks, KEY_BLOCK, lanes), BF),
                    pltpu.VMEM((KEY_BLOCK, lanes), BF),
                    pltpu.VMEM((head_size, lanes), BF),
                    pltpu.VMEM((head_size, lanes), F32),
                    pltpu.VMEM((head_size, lanes), F32),
                    pltpu.VMEM((key_blocks * KEY_BLOCK, 2 * head_size), BF),
                    pltpu.VMEM((stat_rows, length), F32),
                    pltpu.VMEM((stat_rows, length), F32),
                    pltpu.VMEM((stat_rows, length), F32),
                    pltpu.VMEM((key_blocks, stat_rows, length), F32),
                ],
            ),
            out_shape=[columns, columns, dkv_shape, dkv_shape],
            input_output_aliases={8 + j: j for j in range(len(before))},
            compiler_params=params(60),
            cost_estimate=LONG,
        name="attention",
        )(
            ordered_after(where, *after), segment_ids, q_t, g_t, in_hbm(even), in_hbm(odd), cosine,
            sine, *before,
        )

    pair_levels = [(bits[i], bits[-1 - i]) for i in range(len(bits))]
    batch_levels = [(bit, bit) for bit in batch_bits]
    mlp_levels = iter(pair_levels + batch_levels)
    results, first_row = [b_up_part], 0
    last_share = max(row_count // 4, 1)
    for share in (row_count - last_share, last_share):
        after = results[:1] if first_row else [even]
        after, _ = reduce_level(mlp_streams, next(mlp_levels), where, after, LONG)
        results = attention(first_row, share, after, results if first_row else [])
        first_row += share
    mix_t, qpg_t, dkv_keep, dkv_send = results
    dkv_recv = lax.ppermute(dkv_send, "seq", partners(seq_devices, 1))
    after, mlp_recv = reduce_level(mlp_streams, next(mlp_levels), where, [mix_t], LONG)

    def share_body(where_ref, keep_ref, recv_ref, *out_refs):
        for j, out_ref in enumerate(out_refs):
            out_ref[...] = (keep_ref[j].astype(F32) + recv_ref[j].astype(F32)).astype(BF)

    shares = call_on_terms(
        share_body, "share", where, after, 1,
        [pl.BlockSpec(memory_space=pltpu.VMEM)] * 2, [dkv_keep, dkv_recv],
        [pl.BlockSpec(memory_space=pltpu.VMEM)] * half_seq,
        [jax.ShapeDtypeStruct(dkv_keep.shape[1:], BF)] * half_seq,
        short(6 * dkv_keep.size),
    )
    dkv_parts = [shares[0]]
    for j in range(1, half_seq):
        dkv_parts.append(lax.ppermute(shares[j], "seq", partners(seq_devices, 2 * j)))

    pair_spec = pl.BlockSpec(memory_space=pltpu.VMEM)
    pair_width = jax.ShapeDtypeStruct((2, half, width), BF)
    output, keep, send = pl.pallas_call(
        mix_kernel,
        grid_spec=pltpu.PrefetchScalarGridSpec(
            num_scalar_prefetch=1,
            grid=(row_count,),
            in_specs=[
                row_block((length, width)), segments_spec, column_block(), column_block(),
                column_block(), column_block(), token_block, whole((width, width)),
                width_spec, width_spec,
            ],
            out_specs=[row_block((length, width)), pair_spec, pair_spec],
            scratch_shapes=[pltpu.VMEM((width, width), F32), pltpu.VMEM((width, width), F32)],
        ),
        out_shape=[
            jax.ShapeDtypeStruct((row_count, length, width), BF), pair_width, pair_width,
        ],
        compiler_params=params(56),
        cost_estimate=LONG,
        name="mix",
    )(
        ordered_after(side, dkv_parts[0]), tokens, segment_ids, mix_t, qpg_t, attn_t, bg_t,
        mlp_out, w_out, b_out, b_down,
    )
    mix_streams = pair_streams(keep, send, True)
    after = [keep, *mlp_recv, *dkv_parts[1:]]
    after, _ = reduce_level(mlp_streams, next(mlp_levels), where, after, LONG)
    after, _ = reduce_level(mix_streams, pair_levels[0], where, after)

    dkv_count = len(dkv_parts)

    def exit_body(*refs):
        fixed, rest = refs[:15], refs[15:]
        exit_kernel(order_a, rows, permuted, *fixed, rest[:dkv_count], *rest[dkv_count:])

    if permuted:
        shuffle = cosine
    else:
        places = (jnp.array(order_a)[:, None] * rows + jnp.arange(rows)[None, :]).reshape(width, 1)
        shuffle = (places == jnp.arange(width)[None, :]).astype(F32)
    b_up_rows = jnp.transpose(
        b_up_part.reshape(devices, hidden // width, rows), (1, 0, 2)
    ).reshape(hidden // width, width)
    extra_spec = pl.BlockSpec(memory_space=pltpu.VMEM)
    extra_shape = jax.ShapeDtypeStruct((half, 2 * LANES), BF)
    tokens_grad, keep, send = pl.pallas_call(
        exit_body,
        grid_spec=pltpu.PrefetchScalarGridSpec(
            num_scalar_prefetch=1,
            grid=(row_count,),
            in_specs=[
                row_block((length, width)), row_block((length, width)), segments_spec,
                column_block(), column_block(), token_block, whole((width, width)),
                whole((width, 2 * head_size)), width_spec, width_spec, turn_spec, turn_spec,
                whole((hidden // width, width)), whole(shuffle.shape),
            ]
            + [row_block((length, 2 * head_size))] * dkv_count,
            out_specs=[row_block((length, width)), extra_spec, extra_spec],
            scratch_shapes=[
                pltpu.VMEM((width, 2 * head_size), F32), pltpu.VMEM((LANES, width), F32),
            ],
        ),
        out_shape=[
            jax.ShapeDtypeStruct((row_count, length, width), BF), extra_shape, extra_shape,
        ],
        compiler_params=params(56),
        cost_estimate=LONG,
        name="exit",
    )(
        ordered_after(side, *after), tokens, out_grad, segment_ids, qpg_t, attn_t, mlp_din, w_query, w_keyvalue,
        attn_gain, mlp_gain, cosine, sine, b_up_rows, shuffle,
        *dkv_parts,
    )

    shape = (blocks, rows, 2 * LANES)
    keep = keep.reshape(shape)
    recv = lax.ppermute(send.reshape(shape), "seq", partners(seq_devices, 1))
    extra_streams = [Stream([(keep, 0), (recv, 0)], blocks, True, 2 * LANES)]
    after = [keep]
    for level in pair_levels[1:]:
        after, _ = reduce_level(mix_streams, level, where, after)
    after = exchange(extra_streams, bits, where, after)[:1]
    for level in mlp_levels:
        after, _ = reduce_level(mlp_streams, level, where, after)
    sums = own_sums(mlp_streams, where, after, LONG)
    small_streams = mix_streams + extra_streams
    exchange(small_streams, batch_bits, where, sums[:1])
    several = tuple(range(8, 8 + hidden // width))
    sums += own_sums(small_streams, where, vectors=[(0,), (1,), (2,), (3,), (4,), (5,), (5,), several])
    w_up_grad, w_down_grad_t, w_query_grad, w_out_grad_t, w_keyvalue_grad, *vectors = sums
    return (
        output,
        keyvalue,
        tokens_grad,
        vectors[0],
        vectors[1],
        vectors[2],
        vectors[3],
        w_query_grad,
        vectors[4],
        w_keyvalue_grad,
        w_out_grad_t.T,
        vectors[5],
        w_up_grad,
        vectors[7],
        w_down_grad_t.T,
        vectors[6],
    )


def solution(mesh):
    row_spec = P("batch", "seq", None)
    split = P(("batch", "seq"))
    first = P(("batch", "seq"), None)
    last = P(None, ("batch", "seq"))
    return jax.shard_map(
        on_device,
        mesh=mesh,
        in_specs=(row_spec, P("batch", "seq")) + (P(),) * 13 + (row_spec,),
        out_specs=(
            row_spec, row_spec, row_spec, split, split, split, split, first, split, first, last,
            split, first, split, last, split,
        ),
        check_vma=False,
    )
```

```python
import functools
import math

import jax
import jax.numpy as jnp
from jax import lax
from jax.experimental import pallas as pl
from jax.experimental.pallas import tpu as pltpu
from jax.sharding import PartitionSpec as P

ROT_DIMS = 16
HALF_ROT = ROT_DIMS // 2
DOCS = 6
EPSILON = 1e-05
KEY_BLOCK = 256
COUNT_ROWS = 16
LANES = 128
NEGATIVE = -1e30
BF = jnp.bfloat16
F32 = jnp.float32
NN = (((1,), (0,)), ((), ()))
NT = (((1,), (1,)), ((), ()))
TN = (((0,), (0,)), ((), ()))


def matmul(left, right, dims=NN):
    return lax.dot_general(left, right, dims, preferred_element_type=F32)


def params(limit):
    return pltpu.CompilerParams(
        dimension_semantics=("arbitrary",), vmem_limit_bytes=limit * 1024 * 1024
    )


LONG = pl.CostEstimate(flops=4 * 10**10, transcendentals=0, bytes_accessed=10**7)

LONGEST = pl.CostEstimate(flops=3 * 10**11, transcendentals=0, bytes_accessed=10**7)


def short(size):
    return pl.CostEstimate(flops=0, transcendentals=0, bytes_accessed=size)


def whole(shape):
    return pl.BlockSpec(shape, lambda *_: (0,) * len(shape))


def permute_rows(values, order, rows):
    return jnp.concatenate([values[b * rows : (b + 1) * rows] for b in order], axis=0)


def row_of(ref):
    return ref[...].astype(F32).reshape(1, ref.shape[0])


def valid_column(segment_row):
    length = segment_row.shape[-1]
    row = jnp.broadcast_to((segment_row >= 0).astype(F32), (LANES, length))
    return row.T[:, :1]


def norm_parts(values):
    center = values - jnp.mean(values, axis=-1, keepdims=True)
    spread = jnp.mean(center * center, axis=-1, keepdims=True)
    scale = lax.rsqrt(spread + EPSILON)
    return center * scale, scale


def turn(values, cosine, sine):
    leading = values[:HALF_ROT]
    trailing = values[HALF_ROT:ROT_DIMS]
    return jnp.concatenate(
        [leading * cosine - trailing * sine, trailing * cosine + leading * sine, values[ROT_DIMS:]],
        axis=0,
    )


def entry_kernel(
    head_size, order_a, order_b, rows, permuted,
    tok_ref, og_ref, seg_ref, ag_ref, as_ref, mg_ref, ms_ref, bq_ref, wq_ref, wkv_ref, wo_ref,
    cos_ref, sin_ref, mlp_ref, bg_ref, mlp_t_ref, bg_t_ref, attn_t_ref, q_t_ref, g_t_ref, kv_ref, pay_ref,
):
    x = tok_ref[0].astype(F32)
    length, width = x.shape
    n, _ = norm_parts(x)
    attn_in = (n * row_of(ag_ref) + row_of(as_ref)).astype(BF)
    mlp_in = (n * row_of(mg_ref) + row_of(ms_ref)).astype(BF)
    segments = seg_ref[pl.ds(pl.program_id(0), 1), :]
    bg = (og_ref[0].astype(F32) * valid_column(segments)).astype(BF)
    mlp_ref[...] = mlp_in
    bg_ref[...] = bg

    def turned(values, order):
        flipped = values.astype(F32).T
        if permuted:
            flipped = permute_rows(flipped, order, rows)
        return flipped.astype(BF)

    mlp_t_ref[...] = turned(mlp_in, order_a)
    attn_t_ref[...] = turned(attn_in, order_a)
    bg_t_ref[...] = turned(bg, order_b)

    cosine, sine = cos_ref[...], sin_ref[...]
    score_scale = 1.0 / math.sqrt(head_size)
    query_t = (matmul(attn_in, wq_ref[...]) + row_of(bq_ref)).T
    grad_t = matmul(wo_ref[...], bg, NT)
    for h in range(width // head_size):
        part = query_t[h * head_size : (h + 1) * head_size]
        q_t_ref[0, :, h * length : (h + 1) * length] = (
            turn(part, cosine, sine) * score_scale
        ).astype(BF)
        g_t_ref[0, :, h * length : (h + 1) * length] = grad_t[
            h * head_size : (h + 1) * head_size
        ].astype(BF)
    kv_t = matmul(attn_in, wkv_ref[...]).T
    kv = turn(kv_t, cosine, sine).T.astype(BF)
    kv_ref[0] = kv
    pay_ref[0, :length] = kv
    lane = lax.broadcasted_iota(jnp.int32, (1, LANES), 1)
    counts = jnp.zeros((1, LANES), F32)
    for c in range(DOCS):
        total = jnp.sum((segments == c).astype(F32), axis=1, keepdims=True)
        counts = counts + jnp.where(lane == c, total, 0.0)
    pay_ref[0, length:] = jnp.broadcast_to(counts, (COUNT_ROWS, LANES)).astype(BF)


def gelu_parts(hidden):
    cdf = 0.5 * (1.0 + lax.erf(hidden * math.sqrt(0.5)))
    bell = jnp.exp(-0.5 * (hidden * hidden)) * (1.0 / math.sqrt(2 * math.pi))
    return hidden * cdf, cdf + hidden * bell


def mlp_kernel(
    chunk, side_ref, mlp_ref, bg_ref, mlp_t_ref, bg_t_ref, up_ref, bup_ref, down_ref,
    keep_ref, send_ref, out_ref, din_ref, bupg_ref, act_s, hg_s,
):
    tokens, width = mlp_ref.shape

    @pl.when(pl.program_id(0) == 0)
    def _():
        out_ref[...] = jnp.zeros_like(out_ref)
        din_ref[...] = jnp.zeros_like(din_ref)

    bupg_ref[...] = jnp.zeros_like(bupg_ref)
    bias = bup_ref[pl.ds(pl.multiple_of(pl.program_id(0) * up_ref.shape[1], LANES), up_ref.shape[1])]
    bias = bias.astype(F32).reshape(1, up_ref.shape[1])

    def step(i, carry):
        at = pl.ds(pl.multiple_of(i * chunk, chunk), chunk)
        hidden = matmul(mlp_ref[at, :], up_ref[...]) + bias
        back = matmul(bg_ref[at, :], down_ref[...], NT)
        act, slope = gelu_parts(hidden)
        act = act.astype(BF)
        hg = (back * slope).astype(BF)
        act_s[at, :] = act
        hg_s[at, :] = hg
        bupg_ref[...] += jnp.sum(hg.astype(F32), axis=0, keepdims=True)
        out_ref[at, :] += matmul(act, down_ref[...])
        din_ref[at, :] += matmul(hg, up_ref[...], NT)
        return carry

    lax.fori_loop(0, tokens // chunk, step, 0)
    half = width // 2
    side = side_ref[0]
    mine = pl.ds(pl.multiple_of(side * half, half), half)
    other = pl.ds(pl.multiple_of((1 - side) * half, half), half)
    send_ref[0] = matmul(mlp_t_ref[other, :], hg_s[...]).astype(BF)
    send_ref[1] = matmul(bg_t_ref[other, :], act_s[...]).astype(BF)
    keep_ref[0] = matmul(mlp_t_ref[mine, :], hg_s[...]).astype(BF)
    keep_ref[1] = matmul(bg_t_ref[mine, :], act_s[...]).astype(BF)


def attention_kernel(
    heads, head_size, seq_devices, first_row, where_ref, seg_ref, q_t_ref, g_t_ref, even_ref,
    odd_ref, cos_ref, sin_ref, *refs,
):
    (mix_t_ref, qpg_t_ref, dkeep_ref, dsend_ref, kv_s, kv_t_s, bias_s, p_s, ds_s, gk_s, o_s, dq_s,
     dkv_s, m_s, l_s, d_s, mk_s) = refs[-17:]
    length = seg_ref.shape[-1]
    me = where_ref[0]
    start = me * length
    group = math.gcd(heads, 3)

    def columns(h, count=1):
        return slice(h * length, (h + count) * length)

    def head(h):
        return slice(h * head_size, (h + 1) * head_size)

    counts = jnp.zeros((1, LANES), F32)
    for m in range(seq_devices):
        ref = (even_ref, odd_ref)[m % 2]
        at = pl.multiple_of((me ^ m) * length, length)
        kv_s[pl.ds(at, length), :] = ref[m // 2, 0, :length]
        counts = counts + ref[m // 2, 0, length : length + COUNT_ROWS].astype(F32)[:1]

    segments = seg_ref[pl.ds(first_row + pl.program_id(0), 1), :]
    low = jnp.zeros((1, length), F32)
    for c in range(DOCS):
        later = (segments > c) | (segments < 0)
        low = low + jnp.where(later, counts[:, c : c + 1], 0.0)
    low = low.astype(jnp.int32)
    first_block = jnp.min(low) // KEY_BLOCK
    end_block = (start + length - 1) // KEY_BLOCK + 1
    place = start + lax.broadcasted_iota(jnp.int32, (1, length), 1)

    m_s[...] = jnp.full_like(m_s, NEGATIVE)
    l_s[...] = jnp.zeros_like(l_s)
    o_s[...] = jnp.zeros_like(o_s)
    dq_s[...] = jnp.zeros_like(dq_s)
    dkv_s[...] = jnp.zeros_like(dkv_s)

    def forward(b, carry):
        at = pl.multiple_of(b * KEY_BLOCK, KEY_BLOCK)
        kv = kv_s[pl.ds(at, KEY_BLOCK), :]
        keys = kv[:, :head_size]
        kv_t = kv.astype(F32).T.astype(BF)
        kv_t_s[b] = kv_t
        summed = jnp.concatenate([kv_t[head_size:], jnp.ones((16, KEY_BLOCK), BF)], axis=0)
        key_place = at + lax.broadcasted_iota(jnp.int32, (KEY_BLOCK, length), 0)
        allowed = (key_place <= place) & (key_place >= low)
        bias_s[...] = jnp.where(allowed, 0.0, NEGATIVE)
        bias = bias_s[...]
        shrinks = {}

        def scores(h):
            return matmul(keys, q_t_ref[0, :, columns(h, group)])

        def mix(h):
            o = matmul(summed, p_s[b, :, columns(h, group)])
            for j in range(group):
                row = slice(h + j, h + j + 1)
                part = o[:, columns(j)]
                shrink = shrinks.pop(h + j)
                o_s[:, columns(h + j)] = o_s[:, columns(h + j)] * shrink + part[:head_size]
                l_s[row, :] = l_s[row, :] * shrink + part[head_size : head_size + 1]

        ready = scores(0)
        for h in range(0, heads, group):
            now_scores = ready
            if h + group < heads:
                ready = scores(h + group)
            for j in range(group):
                row = slice(h + j, h + j + 1)
                s = now_scores[:, columns(j)] + bias
                before = m_s[row, :]
                now = jnp.maximum(before, jnp.max(s, axis=0, keepdims=True))
                p_s[b, :, columns(h + j)] = jnp.exp(s - now).astype(BF)
                shrinks[h + j] = jnp.exp(before - now)
                m_s[row, :] = now
                mk_s[b, row, :] = now
            if h > 0:
                mix(h - group)
        mix(heads - group)
        return carry

    lax.fori_loop(first_block, end_block, forward, 0)

    for h in range(heads):
        row = slice(h, h + 1)
        inverse = 1.0 / l_s[row, :]
        mixed = o_s[:, columns(h)] * inverse
        mix_t_ref[head(h), :] = mixed.astype(BF)
        d_s[row, :] = jnp.sum(
            mixed * g_t_ref[0, :, columns(h)].astype(F32), axis=0, keepdims=True
        )
        l_s[row, :] = inverse

    def backward(b, carry):
        at = pl.multiple_of(b * KEY_BLOCK, KEY_BLOCK)
        values = kv_s[pl.ds(at, KEY_BLOCK), :][:, head_size:]
        keys_t = kv_t_s[b][:head_size]
        inners = {}

        def prob_grads(h):
            for j in range(group):
                row = slice(h + j, h + j + 1)
                factor = jnp.exp(mk_s[b, row, :] - m_s[row, :]) * l_s[row, :]
                scaled = g_t_ref[0, :, columns(h + j)].astype(F32) * factor
                gk_s[:, columns(h + j)] = scaled.astype(BF)
                inners[h + j] = d_s[row, :] * factor
            return matmul(values, gk_s[:, columns(h, group)])

        ready = prob_grads(0)
        for h in range(0, heads, group):
            now_grads = ready
            if h + group < heads:
                ready = prob_grads(h + group)
            for j in range(group):
                p = p_s[b, :, columns(h + j)].astype(F32)
                ds_s[:, columns(h + j)] = (
                    p * (now_grads[:, columns(j)] - inners.pop(h + j))
                ).astype(BF)
        dq_s[...] += matmul(keys_t, ds_s[...])
        dk = matmul(ds_s[...], q_t_ref[0], NT)
        dv = matmul(p_s[b], gk_s[...], NT)
        dkv_s[pl.ds(at, KEY_BLOCK), :] = jnp.concatenate([dk, dv], axis=1).astype(BF)
        return carry

    lax.fori_loop(first_block, end_block, backward, 0)

    cosine, sine = cos_ref[...], sin_ref[...]
    score_scale = 1.0 / math.sqrt(head_size)
    for h in range(heads):
        qpg_t_ref[head(h), :] = turn(
            dq_s[:, columns(h)] * score_scale, cosine, -sine
        ).astype(BF)
    for m in range(seq_devices):
        ref = (dkeep_ref, dsend_ref)[m % 2]
        at = pl.multiple_of((me ^ m) * length, length)
        ref[m // 2, 0] = dkv_s[pl.ds(at, length), :]


def mix_kernel(
    side_ref, tok_ref, seg_ref, mix_t_ref, qpg_t_ref, attn_t_ref, bg_t_ref, mlp_ref, wo_ref,
    bo_ref, bd_ref, out_ref, keep_ref, send_ref, acc_q, acc_o,
):
    step, steps = pl.program_id(0), pl.num_programs(0)

    @pl.when(step == 0)
    def _():
        acc_q[...] = jnp.zeros_like(acc_q)
        acc_o[...] = jnp.zeros_like(acc_o)

    mix_t = mix_t_ref[...]
    branch = matmul(mix_t, wo_ref[...], TN) + (row_of(bo_ref) + row_of(bd_ref)) + mlp_ref[...]
    valid = valid_column(seg_ref[pl.ds(step, 1), :])
    out_ref[0] = (tok_ref[0].astype(F32) + valid * branch).astype(BF)
    acc_q[...] += matmul(attn_t_ref[...], qpg_t_ref[...], NT)
    acc_o[...] += matmul(bg_t_ref[...], mix_t, NT)

    @pl.when(step == steps - 1)
    def _():
        half = acc_q.shape[0] // 2
        side = side_ref[0]
        mine = pl.ds(pl.multiple_of(side * half, half), half)
        other = pl.ds(pl.multiple_of((1 - side) * half, half), half)
        for j, acc in enumerate((acc_q, acc_o)):
            keep_ref[j] = acc[mine, :].astype(BF)
            send_ref[j] = acc[other, :].astype(BF)


def exit_kernel(
    order_a, rows, permuted,
    side_ref, tok_ref, og_ref, seg_ref, qpg_t_ref, attn_t_ref, din_ref, wq_ref, wkv_ref,
    ag_ref, mg_ref, cos_ref, sin_ref, bupg_ref, shuffle_ref, dkv_refs,
    tg_ref, keep_ref, send_ref, acc, vec,
):
    step, steps = pl.program_id(0), pl.num_programs(0)

    @pl.when(step == 0)
    def _():
        acc[...] = jnp.zeros_like(acc)
        vec[...] = jnp.zeros_like(vec)

    dkv = sum((ref[0].astype(F32) for ref in dkv_refs[1:]), dkv_refs[0][0].astype(F32))
    kvpg_t = turn(dkv.T, cos_ref[...], -sin_ref[...]).astype(BF)
    acc[...] += matmul(attn_t_ref[...], kvpg_t, NT)
    qpg_t = qpg_t_ref[...]
    d_attn = (matmul(wq_ref[...], qpg_t) + matmul(wkv_ref[...], kvpg_t)).T
    d_mlp = din_ref[...]
    n, scale = norm_parts(tok_ref[0].astype(F32))
    og = og_ref[0].astype(F32)
    e = d_attn * row_of(ag_ref) + d_mlp * row_of(mg_ref)
    inner = jnp.mean(e * n, axis=-1, keepdims=True)
    tg_ref[0] = (og + scale * (e - jnp.mean(e, axis=-1, keepdims=True) - n * inner)).astype(BF)
    ones = jnp.ones((8, qpg_t.shape[1]), BF)
    bg = (og * valid_column(seg_ref[pl.ds(step, 1), :])).astype(BF)
    sums = [d_attn * n, d_attn, d_mlp * n, d_mlp, None, bg.astype(F32)]
    for j, value in enumerate(sums):
        if value is None:
            part = matmul(ones, qpg_t, NT)[:1]
        else:
            part = jnp.sum(value, axis=0, keepdims=True)
        vec[j : j + 1, :] += part

    @pl.when(step == steps - 1)
    def _():
        vec[8:12, :] = bupg_ref[...]
        if permuted:
            columns = permute_rows(vec[...].T, order_a, rows)
        else:
            columns = lax.dot_general(
                shuffle_ref[...], vec[...], NT, precision=lax.Precision.HIGHEST,
                preferred_element_type=F32,
            )
        half = columns.shape[0] // 2
        acc_columns = slice(0, LANES)
        vec_columns = slice(LANES, 2 * LANES)
        for side in range(2):

            @pl.when(side_ref[0] == side)
            def _():
                mine = slice(side * half, (side + 1) * half)
                other = slice((1 - side) * half, (2 - side) * half)
                keep_ref[:, acc_columns] = acc[mine, :].astype(BF)
                send_ref[:, acc_columns] = acc[other, :].astype(BF)
                keep_ref[:, vec_columns] = columns[mine].astype(BF)
                send_ref[:, vec_columns] = columns[other].astype(BF)


def partners(size, mask):
    return [(i, i ^ mask) for i in range(size)]


class Stream:
    def __init__(self, arrays, count, resident, width):
        self.terms = [(array, resident, 0, at, ()) for array, at in arrays]
        self.count, self.resident, self.width = count, resident, width
        self.rows = arrays[0][0].shape[1]

    def halve(self, bit):
        count = self.count = self.count // 2
        mine, other = [], []
        for array, resident, column, at, adds in self.terms:
            mine.append((array, resident, column, at, adds + ((bit, count),)))
            other.append((array, resident, column, at + count, adds + ((bit, -count),)))
        self.terms = mine
        return other


def first_block(term, where_ref):
    at = term[3]
    for (axis, bit), weight in term[4]:
        at = at + ((where_ref[axis] >> bit) & 1) * weight
    return at


def term_spec(term, width, group):
    if term[1]:
        return pl.BlockSpec(memory_space=pltpu.VMEM)
    return pl.BlockSpec(
        (group, term[0].shape[1], width),
        lambda i, where_ref: (first_block(term, where_ref) // group + i, 0, term[2] // width),
    )


def in_hbm(value):
    return pltpu.with_memory_space_constraint(value, pltpu.HBM)


def operands_of(terms):
    return [term[0] if term[1] else in_hbm(term[0]) for term in terms]


def read_terms(terms, refs, width, group, where_ref):
    total = None
    for term, ref in zip(terms, refs):
        if term[1]:
            at = first_block(term, where_ref) + pl.program_id(0) * group
            value = ref[pl.ds(at, group), :, term[2] : term[2] + width]
        else:
            value = ref[...]
        value = value.astype(F32)
        total = value if total is None else total + value
    return total


def call_on_terms(
    body, name, where, after, steps, in_specs, operands, out_specs, out_shape, length
):
    return pl.pallas_call(
        body,
        grid_spec=pltpu.PrefetchScalarGridSpec(
            num_scalar_prefetch=1, grid=(steps,), in_specs=in_specs, out_specs=out_specs
        ),
        out_shape=out_shape,
        compiler_params=params(limit=24),
        cost_estimate=length,
        name=name,
    )(ordered_after(where, *after), *operands)


def sums_to_send(picks, streams, joined, where, after, length):
    count, rows, resident = streams[0].count, streams[0].rows, streams[0].resident
    widths = [streams[j % len(streams)].width for j in range(len(picks))]
    group = count
    while group > 1 and group * widths[0] > 4 * 3072 and not resident:
        group //= 2
    terms = [term for pick in picks for term in pick]
    outputs = len(picks) // joined
    shapes = [(rows, sum(widths[j * joined : (j + 1) * joined])) for j in range(outputs)]

    def body(where_ref, *refs):
        at = 0
        for j, (pick, width) in enumerate(zip(picks, widths)):
            total = read_terms(pick, refs[at : at + len(pick)], width, group, where_ref).astype(BF)
            column = sum(widths[j - j % joined : j])
            refs[len(terms) + j // joined][:, :, column : column + width] = total
            at += len(pick)

    if resident:
        out_specs = [pl.BlockSpec(memory_space=pltpu.VMEM) for _ in shapes]
    else:
        out_specs = [pl.BlockSpec((group,) + shape, lambda i, _: (i, 0, 0)) for shape in shapes]
    return call_on_terms(
        body, "combine", where, after, count // group,
        [term_spec(term, width, group) for pick, width in zip(picks, widths) for term in pick],
        operands_of(terms),
        out_specs,
        [jax.ShapeDtypeStruct((count,) + shape, BF) for shape in shapes],
        length or short(2 * count * rows * sum(len(p) * w for p, w in zip(picks, widths))),
    )


def own_sums(streams, where, after=(), length=None, vectors=()):
    terms = [term for stream in streams for term in stream.terms]
    shapes = [(stream.rows, stream.width) for stream in streams]
    if vectors:
        shapes[-1] = (shapes[-1][0], shapes[-1][1] - LANES)
        shapes += [(streams[-1].rows * len(columns),) for columns in vectors]

    def body(where_ref, *refs):
        at = 0
        for stream, output in zip(streams, refs[len(terms) :]):
            size = len(stream.terms)
            total = read_terms(stream.terms, refs[at : at + size], stream.width, 1, where_ref)[0]
            output[...] = total[:, : output.shape[1]]
            at += size
        if vectors:
            turned = total[:, -LANES:].T
            for columns, output in zip(vectors, refs[len(terms) + len(streams) :]):
                row = jnp.concatenate([turned[c : c + 1] for c in columns], axis=1)
                output[...] = row.reshape(output.shape)

    return call_on_terms(
        body, "own", where, after, 1,
        [term_spec(term, stream.width, 1) for stream in streams for term in stream.terms],
        operands_of(terms),
        [whole(shape) for shape in shapes],
        [jax.ShapeDtypeStruct(shape, F32) for shape in shapes],
        length or short(2 * len(terms) * streams[0].rows * streams[0].width),
    )


def ordered_after(value, *others):
    if not others:
        return value
    return lax.optimization_barrier((value, others))[0]


AXES = ("seq", "batch")


def reduce_level(streams, bits, where, after=(), length=None):
    picks = [stream.halve(bit) for stream, bit in zip(streams, bits)]
    joined = len(set(bits)) == 1
    sends = sums_to_send(picks, streams, len(streams) if joined else 1, where, after, length)
    recvs = []
    for (axis, bit), send in zip(bits, sends):
        recvs.append(
            lax.ppermute(send, AXES[axis], partners(lax.axis_size(AXES[axis]), 1 << bit))
        )
    for j, stream in enumerate(streams):
        column = j * stream.width if joined else 0
        resident = stream.resident or stream.count <= 4
        stream.terms.append((recvs[0 if joined else j], resident, column, 0, ()))
    return sends, recvs


def exchange(streams, bits, where, after=()):
    axis = AXES[bits[0][0]]
    picks, recvs = [], []
    for mask in range(1, 1 << len(bits)):
        for stream in streams:
            count, terms = stream.count, stream.terms
            for j, bit in enumerate(bits):
                count //= 2
                sign, shift = (-1, count) if (mask >> j) & 1 else (1, 0)
                terms = [
                    (a, r, c, at + shift, adds + ((bit, sign * count),))
                    for a, r, c, at, adds in terms
                ]
            picks.append(terms)
    for stream in streams:
        for bit in bits:
            stream.halve(bit)
    sends = sums_to_send(picks, streams, len(streams), where, after, None)
    for mask, send in enumerate(sends, 1):
        partner = sum(((mask >> j) & 1) << bit[1] for j, bit in enumerate(bits))
        recv = lax.ppermute(send, axis, partners(lax.axis_size(axis), partner))
        column = 0
        for stream in streams:
            stream.terms.append((recv, stream.resident, column, 0, ()))
            column += stream.width
    return sends


def on_device(
    tokens, segment_ids, attn_gain, attn_shift, mlp_gain, mlp_shift, w_query, b_query,
    w_keyvalue, w_out, b_out, w_up, b_up, w_down, b_down, out_grad,
):
    row_count, length, width = tokens.shape
    head_size = w_keyvalue.shape[1] // 2
    heads = width // head_size
    hidden = w_up.shape[1]
    token_count = row_count * length
    seq_devices = lax.axis_size("seq")
    batch_devices = lax.axis_size("batch")
    devices = seq_devices * batch_devices
    seq_index = lax.axis_index("seq").astype(jnp.int32)
    batch_index = lax.axis_index("batch").astype(jnp.int32)
    side = (seq_index & 1).reshape(1)
    where = jnp.stack([seq_index, batch_index])
    rows = width // devices
    permuted = rows % 8 == 0
    seq_bits = list(range(seq_devices.bit_length() - 1))

    def reversed_bits(value, count):
        return sum(((value >> j) & 1) << (count - 1 - j) for j in range(count))

    batch_order = [
        reversed_bits(z, batch_devices.bit_length() - 1) for z in range(batch_devices)
    ]

    def device_order(bits):
        order = []
        for k in range(seq_devices):
            at = 0
            for j, bit in enumerate(bits):
                at |= ((k >> (len(bits) - 1 - j)) & 1) << bit
            order += [z * seq_devices + at for z in batch_order]
        return order

    order_a = device_order(seq_bits)
    order_b = device_order(seq_bits[:1] + seq_bits[:0:-1])

    def ordered(values, order):
        if permuted:
            return values
        shaped = values.reshape(values.shape[:-2] + (devices, rows, values.shape[-1]))
        return jnp.take(shaped, jnp.array(order), axis=-3).reshape(values.shape)

    positions = (seq_index * length + jnp.arange(length)).astype(F32)
    inverse = 10000.0 ** (-(jnp.arange(HALF_ROT).astype(F32) * (2.0 / ROT_DIMS)))
    angles = inverse[:, None] * positions[None, :]
    cosine, sine = jnp.cos(angles), jnp.sin(angles)
    segments_spec = whole((row_count, length))
    turn_spec = whole((HALF_ROT, length))
    width_spec = whole((width,))

    def row_block(shape, first=0):
        return pl.BlockSpec((1,) + shape, lambda r, *_: (first + r, 0, 0))

    token_block = pl.BlockSpec((length, width), lambda r, *_: (r, 0))
    whole_lanes = length % LANES == 0

    def column_block(first=0):
        if whole_lanes:
            return pl.BlockSpec((width, length), lambda r, *_: (0, first + r))
        return pl.BlockSpec((None, width, length), lambda r, *_: (first + r, 0, 0))

    columns = jax.ShapeDtypeStruct(
        (width, token_count) if whole_lanes else (row_count, width, length), BF
    )

    def joined(values):
        if whole_lanes:
            return values
        return jnp.transpose(values, (1, 0, 2)).reshape(width, token_count)

    lanes = heads * length
    mlp_in, bg, mlp_t, bg_t, attn_t, q_t, g_t, keyvalue, payload = pl.pallas_call(
        functools.partial(entry_kernel, head_size, order_a, order_b, rows, permuted),
        grid=(row_count,),
        in_specs=[
            row_block((length, width)), row_block((length, width)), segments_spec,
            width_spec, width_spec, width_spec, width_spec, width_spec,
            whole((width, width)), whole((width, 2 * head_size)), whole((width, width)),
            turn_spec, turn_spec,
        ],
        out_specs=[
            token_block, token_block, column_block(), column_block(), column_block(),
            row_block((head_size, lanes)), row_block((head_size, lanes)),
            row_block((length, 2 * head_size)), row_block((length + COUNT_ROWS, 2 * head_size)),
        ],
        out_shape=[
            jax.ShapeDtypeStruct((token_count, width), BF),
            jax.ShapeDtypeStruct((token_count, width), BF),
            columns,
            columns,
            columns,
            jax.ShapeDtypeStruct((row_count, head_size, lanes), BF),
            jax.ShapeDtypeStruct((row_count, head_size, lanes), BF),
            jax.ShapeDtypeStruct((row_count, length, 2 * head_size), BF),
            jax.ShapeDtypeStruct((row_count, length + COUNT_ROWS, 2 * head_size), BF),
        ],
        compiler_params=params(60),
        cost_estimate=LONG,
        name="entry",
    )(
        tokens, out_grad, segment_ids, attn_gain, attn_shift, mlp_gain, mlp_shift, b_query,
        w_query, w_keyvalue, w_out, cosine, sine,
    )
    mlp_t, attn_t = ordered(mlp_t, order_a), ordered(attn_t, order_a)
    bg_t = ordered(bg_t, order_b)

    gathered = [payload]
    for mask in range(2, seq_devices, 2):
        gathered.append(lax.ppermute(payload, "seq", partners(seq_devices, mask)))

    tile = math.gcd(512, hidden)
    half = width // 2
    pair_cols = pl.BlockSpec((2, half, tile), lambda f, *_: (0, 0, f))
    pair_shape = jax.ShapeDtypeStruct((2, half, hidden), BF)
    keep, send, mlp_out, mlp_din, b_up_part = pl.pallas_call(
        functools.partial(mlp_kernel, token_count),
        grid_spec=pltpu.PrefetchScalarGridSpec(
            num_scalar_prefetch=1,
            grid=(hidden // tile,),
            in_specs=[
                whole((token_count, width)), whole((token_count, width)),
                whole((width, token_count)), whole((width, token_count)),
                pl.BlockSpec((width, tile), lambda f, *_: (0, f)),
                whole((hidden,)),
                pl.BlockSpec((tile, width), lambda f, *_: (f, 0)),
            ],
            out_specs=[
                pair_cols, pair_cols, whole((token_count, width)), whole((token_count, width)),
                pl.BlockSpec((1, tile), lambda f, *_: (0, f)),
            ],
            scratch_shapes=[
                pltpu.VMEM((token_count, tile), BF), pltpu.VMEM((token_count, tile), BF),
            ],
        ),
        out_shape=[
            pair_shape, pair_shape,
            jax.ShapeDtypeStruct((token_count, width), F32),
            jax.ShapeDtypeStruct((token_count, width), F32),
            jax.ShapeDtypeStruct((1, hidden), F32),
        ],
        compiler_params=params(60),
        cost_estimate=LONG,
        name="mlp",
    )(side, mlp_in, bg, joined(mlp_t), joined(bg_t), w_up, b_up, w_down)

    gathered = ordered_after(tuple(gathered), b_up_part)

    def stack_body(*refs):
        for j, ref in enumerate(refs[:-1]):
            refs[-1][j] = ref[...]

    even = pl.pallas_call(
        stack_body,
        in_specs=[pl.BlockSpec(memory_space=pltpu.VMEM)] * len(gathered),
        out_specs=pl.BlockSpec(memory_space=pltpu.VMEM),
        out_shape=jax.ShapeDtypeStruct((len(gathered),) + payload.shape, BF),
        compiler_params=pltpu.CompilerParams(vmem_limit_bytes=24 * 1024 * 1024),
        cost_estimate=LONGEST,
        name="stack",
    )(*gathered)
    odd = lax.ppermute(even, "seq", partners(seq_devices, 1))

    bits = [(0, bit) for bit in range(1, seq_devices.bit_length() - 1)]
    batch_bits = [(1, bit) for bit in range(batch_devices.bit_length() - 1)]
    blocks = devices // 2

    def pair_streams(keep, send, resident):
        shape = (2 * blocks, rows, keep.shape[2])
        keep = keep.reshape(shape)
        recv = lax.ppermute(send.reshape(shape), "seq", partners(seq_devices, 1))
        return [
            Stream([(keep, at), (recv, at)], blocks, resident, keep.shape[2])
            for at in (0, blocks)
        ]

    mlp_streams = pair_streams(keep, send, False)

    half_seq = seq_devices // 2
    key_blocks = length * seq_devices // KEY_BLOCK
    stat_rows = -(-heads // 8) * 8

    def attention(first, count, after, before):
        kv_rows = pl.BlockSpec(
            (half_seq, 1, length + COUNT_ROWS, 2 * head_size), lambda r, *_: (0, first + r, 0, 0)
        )
        dkv_rows = pl.BlockSpec(
            (half_seq, 1, length, 2 * head_size), lambda r, *_: (0, first + r, 0, 0)
        )
        dkv_shape = jax.ShapeDtypeStruct((half_seq, row_count, length, 2 * head_size), BF)
        return pl.pallas_call(
            functools.partial(attention_kernel, heads, head_size, seq_devices, first),
            grid_spec=pltpu.PrefetchScalarGridSpec(
                num_scalar_prefetch=1,
                grid=(count,),
                in_specs=[
                    segments_spec, row_block((head_size, lanes), first),
                    row_block((head_size, lanes), first), kv_rows, kv_rows, turn_spec, turn_spec,
                ]
                + [pl.BlockSpec(memory_space=pl.ANY)] * len(before),
                out_specs=[column_block(first), column_block(first), dkv_rows, dkv_rows],
                scratch_shapes=[
                    pltpu.VMEM((key_blocks * KEY_BLOCK, 2 * head_size), BF),
                    pltpu.VMEM((key_blocks, 2 * head_size, KEY_BLOCK), BF),
                    pltpu.VMEM((KEY_BLOCK, length), F32),
                    pltpu.VMEM((key_blocks, KEY_BLOCK, lanes), BF),
                    pltpu.VMEM((KEY_BLOCK, lanes), BF),
                    pltpu.VMEM((head_size, lanes), BF),
                    pltpu.VMEM((head_size, lanes), F32),
                    pltpu.VMEM((head_size, lanes), F32),
                    pltpu.VMEM((key_blocks * KEY_BLOCK, 2 * head_size), BF),
                    pltpu.VMEM((stat_rows, length), F32),
                    pltpu.VMEM((stat_rows, length), F32),
                    pltpu.VMEM((stat_rows, length), F32),
                    pltpu.VMEM((key_blocks, stat_rows, length), F32),
                ],
            ),
            out_shape=[columns, columns, dkv_shape, dkv_shape],
            input_output_aliases={8 + j: j for j in range(len(before))},
            compiler_params=params(60),
            cost_estimate=LONG,
        name="attention",
        )(
            ordered_after(where, *after), segment_ids, q_t, g_t, in_hbm(even), in_hbm(odd), cosine,
            sine, *before,
        )

    pair_levels = [(bits[i], bits[-1 - i]) for i in range(len(bits))]
    batch_levels = [(bit, bit) for bit in batch_bits]
    mlp_levels = iter(pair_levels + batch_levels)
    results, first_row = [b_up_part], 0
    last_share = max(row_count // 4, 1)
    for share in (row_count - last_share, last_share):
        after = results[:1] if first_row else [even]
        after, _ = reduce_level(mlp_streams, next(mlp_levels), where, after, LONG)
        results = attention(first_row, share, after, results if first_row else [])
        first_row += share
    mix_t, qpg_t, dkv_keep, dkv_send = results
    dkv_recv = lax.ppermute(dkv_send, "seq", partners(seq_devices, 1))
    after, mlp_recv = reduce_level(mlp_streams, next(mlp_levels), where, [mix_t], LONG)

    def share_body(where_ref, keep_ref, recv_ref, *out_refs):
        for j, out_ref in enumerate(out_refs):
            out_ref[...] = (keep_ref[j].astype(F32) + recv_ref[j].astype(F32)).astype(BF)

    shares = call_on_terms(
        share_body, "share", where, after, 1,
        [pl.BlockSpec(memory_space=pltpu.VMEM)] * 2, [dkv_keep, dkv_recv],
        [pl.BlockSpec(memory_space=pltpu.VMEM)] * half_seq,
        [jax.ShapeDtypeStruct(dkv_keep.shape[1:], BF)] * half_seq,
        short(6 * dkv_keep.size),
    )
    dkv_parts = [shares[0]]
    for j in range(1, half_seq):
        dkv_parts.append(lax.ppermute(shares[j], "seq", partners(seq_devices, 2 * j)))

    pair_spec = pl.BlockSpec(memory_space=pltpu.VMEM)
    pair_width = jax.ShapeDtypeStruct((2, half, width), BF)
    output, keep, send = pl.pallas_call(
        mix_kernel,
        grid_spec=pltpu.PrefetchScalarGridSpec(
            num_scalar_prefetch=1,
            grid=(row_count,),
            in_specs=[
                row_block((length, width)), segments_spec, column_block(), column_block(),
                column_block(), column_block(), token_block, whole((width, width)),
                width_spec, width_spec,
            ],
            out_specs=[row_block((length, width)), pair_spec, pair_spec],
            scratch_shapes=[pltpu.VMEM((width, width), F32), pltpu.VMEM((width, width), F32)],
        ),
        out_shape=[
            jax.ShapeDtypeStruct((row_count, length, width), BF), pair_width, pair_width,
        ],
        compiler_params=params(56),
        cost_estimate=LONG,
        name="mix",
    )(
        ordered_after(side, dkv_parts[0]), tokens, segment_ids, mix_t, qpg_t, attn_t, bg_t,
        mlp_out, w_out, b_out, b_down,
    )
    mix_streams = pair_streams(keep, send, True)
    after = [keep, *mlp_recv, *dkv_parts[1:]]
    after, _ = reduce_level(mlp_streams, next(mlp_levels), where, after, LONG)
    after, _ = reduce_level(mix_streams, pair_levels[0], where, after)

    dkv_count = len(dkv_parts)

    def exit_body(*refs):
        fixed, rest = refs[:15], refs[15:]
        exit_kernel(order_a, rows, permuted, *fixed, rest[:dkv_count], *rest[dkv_count:])

    if permuted:
        shuffle = cosine
    else:
        places = (jnp.array(order_a)[:, None] * rows + jnp.arange(rows)[None, :]).reshape(width, 1)
        shuffle = (places == jnp.arange(width)[None, :]).astype(F32)
    b_up_rows = jnp.transpose(
        b_up_part.reshape(devices, hidden // width, rows), (1, 0, 2)
    ).reshape(hidden // width, width)
    extra_spec = pl.BlockSpec(memory_space=pltpu.VMEM)
    extra_shape = jax.ShapeDtypeStruct((half, 2 * LANES), BF)
    tokens_grad, keep, send = pl.pallas_call(
        exit_body,
        grid_spec=pltpu.PrefetchScalarGridSpec(
            num_scalar_prefetch=1,
            grid=(row_count,),
            in_specs=[
                row_block((length, width)), row_block((length, width)), segments_spec,
                column_block(), column_block(), token_block, whole((width, width)),
                whole((width, 2 * head_size)), width_spec, width_spec, turn_spec, turn_spec,
                whole((hidden // width, width)), whole(shuffle.shape),
            ]
            + [row_block((length, 2 * head_size))] * dkv_count,
            out_specs=[row_block((length, width)), extra_spec, extra_spec],
            scratch_shapes=[
                pltpu.VMEM((width, 2 * head_size), F32), pltpu.VMEM((LANES, width), F32),
            ],
        ),
        out_shape=[
            jax.ShapeDtypeStruct((row_count, length, width), BF), extra_shape, extra_shape,
        ],
        compiler_params=params(56),
        cost_estimate=LONG,
        name="exit",
    )(
        ordered_after(side, *after), tokens, out_grad, segment_ids, qpg_t, attn_t, mlp_din, w_query, w_keyvalue,
        attn_gain, mlp_gain, cosine, sine, b_up_rows, shuffle,
        *dkv_parts,
    )

    shape = (blocks, rows, 2 * LANES)
    keep = keep.reshape(shape)
    recv = lax.ppermute(send.reshape(shape), "seq", partners(seq_devices, 1))
    extra_streams = [Stream([(keep, 0), (recv, 0)], blocks, True, 2 * LANES)]
    after = [keep]
    for level in pair_levels[1:]:
        after, _ = reduce_level(mix_streams, level, where, after)
    after = exchange(extra_streams, bits, where, after)[:1]
    for level in mlp_levels:
        after, _ = reduce_level(mlp_streams, level, where, after)
    sums = own_sums(mlp_streams, where, after, LONG)
    small_streams = mix_streams + extra_streams
    exchange(small_streams, batch_bits, where, sums[:1])
    several = tuple(range(8, 8 + hidden // width))
    sums += own_sums(small_streams, where, vectors=[(0,), (1,), (2,), (3,), (4,), (5,), (5,), several])
    w_up_grad, w_down_grad_t, w_query_grad, w_out_grad_t, w_keyvalue_grad, *vectors = sums
    return (
        output,
        keyvalue,
        tokens_grad,
        vectors[0],
        vectors[1],
        vectors[2],
        vectors[3],
        w_query_grad,
        vectors[4],
        w_keyvalue_grad,
        w_out_grad_t.T,
        vectors[5],
        w_up_grad,
        vectors[7],
        w_down_grad_t.T,
        vectors[6],
    )


def solution(mesh):
    row_spec = P("batch", "seq", None)
    split = P(("batch", "seq"))
    first = P(("batch", "seq"), None)
    last = P(None, ("batch", "seq"))
    return jax.shard_map(
        on_device,
        mesh=mesh,
        in_specs=(row_spec, P("batch", "seq")) + (P(),) * 13 + (row_spec,),
        out_specs=(
            row_spec, row_spec, row_spec, split, split, split, split, first, split, first, last,
            split, first, split, last, split,
        ),
        check_vma=False,
    )
```
